32 devices in a mesh: ctx: 8 (over z, x), fsdp: 4 (over y, core).
Axes of the slice: x: 2, y: 2, z: 4, core: 2. Of those that a mesh axis runs over, the one named last changes fastest.
Arguments:
- hidden: bfloat16 [8, 1024, 1024], P('fsdp', 'ctx'), may hold values from -6 to 6
- segment_ids: int32 [8, 1024], P('fsdp', 'ctx'), may hold values from 0 to 3, never falling along the last dimension, each value on 1 to 512 neighbouring positions
- cotangent: bfloat16 [8, 1024, 1024], P('fsdp', 'ctx'), may hold values from -6 to 6
- w_qkv: bfloat16 [1024, 3072], P('fsdp'), may hold values from -0.1875 to 0.1875
- w_attn_out: bfloat16 [1024, 1024], P('fsdp'), may hold values from -3 to 3
- w_in: bfloat16 [1024, 5248], P('fsdp'), may hold values from -0.1875 to 0.1875
- w_mlp_out: bfloat16 [2624, 1024], P('fsdp'), may hold values from -0.15625 to 0.15625
- gain_attn: bfloat16 [1024], P('fsdp'), may hold values from 0.099609375 to 1.8984375
- gain_mlp: bfloat16 [1024], P('fsdp'), may hold values from 0.099609375 to 1.8984375
Outputs:
- output: bfloat16 [8, 1024, 1024], P('fsdp', 'ctx')
- input_grad: float32 [8, 1024, 1024], P('fsdp', 'ctx')
- grad_w_qkv: float32 [1024, 3072], P('fsdp')
- grad_w_attn_out: float32 [1024, 1024], P('fsdp')
- grad_w_in: float32 [1024, 5248], P('fsdp')
- grad_w_mlp_out: float32 [2624, 1024], P('fsdp')
- grad_gain_attn: float32 [1024], P('fsdp')
- grad_gain_mlp: float32 [1024], P('fsdp')
The draws below stay inside these ranges and needn't reach their ends.
Inputs may be any that keep to these rules, and one draw needn't show every extreme that they name: `segment_ids`: along each sequence the document numbers never fall; every document spans at most half of 1024 positions, and one in each sequence spans exactly that many.
All inputs are finite; a program needn't handle non-finite values.
Results may differ from the reference program's by a relative error of at most 0.024.
Values may be sent and summed in bfloat16 or wider, within the bound.
No kernel may reach another device: no remote copies, remote signals or barrier semaphores. Data moves between devices by JAX's collectives and lax.ppermute only.
A program may use at most 192 MiB of HBM per device.

```python
import math
from functools import partial
import jax
import jax.numpy as jnp
import numpy as np
from jax import lax

D = 1024
HEADS = 16
HEAD = 64
FF = 2624
DOCS = 4
SEQ = 1024
SEQS = 8


def level_of(stream_key, shape, shards, low, largest):
    loudness, own = 1.0, jax.random.fold_in(stream_key, 6)
    for position, blocks in shards:
        steps = jnp.exp(jax.random.uniform(jax.random.fold_in(own, position), (blocks,), jnp.float32, low / len(shards), largest / len(shards)))
        loudness = loudness * jnp.repeat(steps, shape[position] // blocks).reshape([-1 if axis == position else 1 for axis in range(len(shape))])
    return loudness


def length_profile(amount, total, most, lean):
    portions = [(1 << 20) // math.isqrt(rank ** lean) + 1 for rank in range(2, amount + 1)]
    spare, counts = total - most - (amount - 1), [1] * (amount - 1)
    while spare > 0:
        free = [i for i in range(amount - 1) if counts[i] < most]
        mass, budget = sum([portions[i] for i in free]), spare
        for i in free:
            addition = min(most - counts[i], max(1, budget * portions[i] // mass), spare)
            counts[i] = counts[i] + addition
            spare = spare - addition
    return np.array([most] + counts)


def uneven(key, count, total, bound, skew):
    if count == 2:
        one = jax.random.randint(key, (), max(1, total - bound), min(bound, total - 1) + 1)
        return jnp.stack([one, total - one])
    sizes = jnp.asarray(length_profile(count, total, bound, skew), jnp.int32)
    twos = (count - 1) // 2
    giver, taker = sizes[1:1 + 2 * twos:2], sizes[2:2 + 2 * twos:2]
    room = jnp.minimum(giver - 1, bound - taker)
    moved = jax.random.randint(jax.random.fold_in(key, 1), (twos,), 0, 1 << 20) % (room + 1)
    sizes = sizes.at[1:1 + 2 * twos:2].set(giver - moved).at[2:2 + 2 * twos:2].set(taker + moved)
    return sizes[jax.random.permutation(jax.random.fold_in(key, 2), count)]


def normal_values(rng, extent, scale, bound, cuts=(), kind=jnp.bfloat16):
    loudness = level_of(rng, extent, cuts, -0.22, 0.18) if cuts else 1.0
    drawn = jax.random.normal(rng, extent, jnp.float32) * scale * loudness
    return jnp.minimum(jnp.maximum(drawn, -bound), bound).astype(kind)


def setup_inputs(seed: int = 0) -> dict:
    key_of = jax.random.split(jax.random.key(seed), 10)
    hidden = normal_values(key_of[0], (SEQS, SEQ, D), 1.0, 6.0, ((0, 4), (1, 8)))
    segment_ids = jax.vmap(lambda own: jnp.searchsorted(jnp.cumsum(uneven(own, DOCS, SEQ, SEQ // 2, 1)), jnp.arange(SEQ), side="right"))(jax.random.split(key_of[1], SEQS)).reshape((SEQS, SEQ)).astype(jnp.int32)
    cotangent = normal_values(key_of[2], (SEQS, SEQ, D), 1.0, 6.0, ((0, 4), (1, 8)))
    w_qkv = normal_values(key_of[3], (D, 3 * D), D ** -0.5, 0.1875, ((0, 4),))
    w_attn_out = normal_values(key_of[4], (D, D), (max(D // 256, 4)) ** -0.5, 3.0, ((0, 4),))
    w_in = normal_values(key_of[5], (D, 2 * FF), D ** -0.5, 0.1875, ((0, 4),))
    w_mlp_out = normal_values(key_of[6], (FF, D), (FF // 2) ** -0.5, 0.15625, ((0, 4),))
    gain_attn = jnp.clip(1.0 + 0.18 * jax.random.normal(key_of[7], (D,), jnp.float32), 0.099609375, 1.8984375).astype(jnp.bfloat16)
    gain_mlp = jnp.clip(1.0 + 0.18 * jax.random.normal(key_of[8], (D,), jnp.float32), 0.099609375, 1.8984375).astype(jnp.bfloat16)
    return {"hidden": hidden, "segment_ids": segment_ids, "cotangent": cotangent, "w_qkv": w_qkv, "w_attn_out": w_attn_out, "w_in": w_in, "w_mlp_out": w_mlp_out, "gain_attn": gain_attn, "gain_mlp": gain_mlp}


highest = lax.Precision.HIGHEST
rope_base = 160000.0
norm_eps = 1e-05
masked_score = -1e+30

@jax.custom_vjp
def low(v):
    return lax.optimization_barrier(v.astype(jnp.bfloat16)).astype(jnp.float32)

@jax.custom_vjp
def low_back(v):
    return v

def low_keep(v):
    return (low(v), None)

def low_pass(kept, grad):
    return (grad,)

def back_keep(v):
    return (v, None)

def back_low(kept, grad):
    return (low(grad),)
low.defvjp(low_keep, low_pass)
low_back.defvjp(back_keep, back_low)

def norm_scale(values, gain):
    center = values - lax.optimization_barrier(jnp.mean(values, axis=-1, keepdims=True))
    spread = lax.optimization_barrier(jnp.mean(center * center, axis=-1, keepdims=True))
    return center * lax.rsqrt(spread + norm_eps) * gain

def rope_tables(positions, head_size):
    half = head_size // 2
    inverse = rope_base ** (-(jnp.arange(half, dtype=jnp.float32) * 2.0 / head_size))
    angles = positions.astype(jnp.float32)[:, None] * inverse[None, :]
    return (jnp.cos(angles), jnp.sin(angles))

def rotate_heads(values, cosine, sine, heads):
    shape = values.shape
    split = values.reshape(shape[:-1] + (heads, shape[-1] // heads))
    half = split.shape[-1] // 2
    first = split[..., :half]
    second = split[..., half:]
    cos_heads = cosine[:, None, :]
    sin_heads = sine[:, None, :]
    turned = jnp.concatenate([first * cos_heads - second * sin_heads, second * cos_heads + first * sin_heads], axis=-1)
    return turned.reshape(shape)

def attend_rows(query_block, query_segments, key_rows, value_rows, key_segments):
    raw = jnp.einsum('qhd,khd->hqk', query_block, key_rows, precision=highest)
    scores = low_back(raw)
    allowed = query_segments[:, None] == key_segments[None, :]
    probs = low(jax.nn.softmax(jnp.where(allowed[None], scores, masked_score), axis=-1))
    return jnp.einsum('hqk,khd->qhd', probs, value_rows, precision=highest)

def layer_forward(segments, rows, w_qkv, w_attn_out, w_in, w_mlp_out, gain_attn, gain_mlp):
    positions = jnp.arange(SEQ, dtype=jnp.int32)
    cosine, sine = rope_tables(positions, HEAD)
    scale = HEAD ** (-0.5)
    normed = low(norm_scale(rows, gain_attn))
    mixed = low_back(jnp.dot(normed, w_qkv, precision=highest, preferred_element_type=jnp.float32))
    queries = low(rotate_heads(mixed[:, :D], cosine, sine, HEADS) * scale)
    key_rows = low(rotate_heads(mixed[:, D:2 * D], cosine, sine, HEADS))
    value_rows = low(mixed[:, 2 * D:])
    block = min(512, SEQ)
    count = SEQ // block
    key_heads = key_rows.reshape(SEQ, HEADS, HEAD)
    value_heads = value_rows.reshape(SEQ, HEADS, HEAD)

    def one_block(pieces):
        return attend_rows(pieces[0], pieces[1], key_heads, value_heads, segments)
    attended = lax.map(jax.checkpoint(one_block), (queries.reshape(count, block, HEADS, HEAD), segments.reshape(count, block)))
    attended = low(low_back(attended.reshape(SEQ, D)))
    residual = rows + low_back(jnp.dot(attended, w_attn_out, precision=highest, preferred_element_type=jnp.float32))
    normed_mlp = low(norm_scale(residual, gain_mlp))
    inner = low_back(jnp.dot(normed_mlp, w_in, precision=highest, preferred_element_type=jnp.float32))
    activated = low(jax.nn.gelu(inner[:, :FF], approximate=False) * inner[:, FF:])
    return residual + low_back(jnp.dot(activated, w_mlp_out, precision=highest, preferred_element_type=jnp.float32))

def reference(hidden, segment_ids, cotangent, w_qkv, w_attn_out, w_in, w_mlp_out, gain_attn, gain_mlp):
    weights = tuple((piece.astype(jnp.float32) for piece in (w_qkv, w_attn_out, w_in, w_mlp_out, gain_attn, gain_mlp)))

    def one_sequence(totals, inputs):
        seq_rows, seq_segments, seq_cotangent = inputs
        result, pullback = jax.vjp(partial(layer_forward, seq_segments), seq_rows.astype(jnp.float32), *weights)
        gradients = pullback(seq_cotangent.astype(jnp.float32))
        totals = tuple((before + extra for before, extra in zip(totals, gradients[1:])))
        return (totals, (result.astype(jnp.bfloat16), gradients[0]))
    zeros = tuple((jnp.zeros(piece.shape, jnp.float32) for piece in weights))
    totals, (outputs, input_grads) = lax.scan(one_sequence, zeros, (hidden, segment_ids, cotangent))
    return (outputs, input_grads, totals[0], totals[1], totals[2], totals[3], totals[4], totals[5])
```

```python
import functools

import jax
import jax.numpy as jnp
from jax import lax
from jax.experimental import pallas as pl
from jax.experimental.pallas import tpu as pltpu
from jax.sharding import PartitionSpec as P

HEADS = 16
rope_base = 160000.0
norm_eps = 1e-05
masked_score = -1e30
bf16 = jnp.bfloat16
f32 = jnp.float32
NT = (((1,), (1,)), ((), ()))
NN = (((1,), (0,)), ((), ()))
TN = (((0,), (0,)), ((), ()))


def mm(a, b, dims=NN):
    return lax.dot_general(a, b, dims, preferred_element_type=f32)


def head_mask(shape, head, size):
    return lax.broadcasted_iota(jnp.int32, shape, 1) // size == head


def attend_kernel(q_ref, k_ref, v_ref, sq_ref, sk_ref, o_ref, *, heads):
    q, k, v = q_ref[0], k_ref[0], v_ref[0]
    size = q.shape[1] // heads
    allowed = sq_ref[0] == sk_ref[0]
    total = jnp.zeros(q.shape, f32)
    for head in range(heads):
        here = head_mask(q.shape, head, size)
        scores = mm(jnp.where(here, q, jnp.zeros_like(q)), k, NT)
        scores = jnp.where(allowed, scores, masked_score)
        weights = jnp.exp(scores - jnp.max(scores, axis=1, keepdims=True))
        row = mm(weights.astype(bf16), v) / jnp.sum(weights, axis=1, keepdims=True)
        total = jnp.where(here, row, total)
    o_ref[0] = total.astype(bf16)


def attend(q, k, v, segments, heads):
    n, length, width = q.shape
    block = min(256, length)
    rows = pl.BlockSpec((1, block, width), lambda i, j: (i, j, 0))
    whole = pl.BlockSpec((1, length, width), lambda i, j: (i, 0, 0))
    return pl.pallas_call(
        functools.partial(attend_kernel, heads=heads),
        grid=(n, length // block),
        in_specs=[
            rows,
            whole,
            whole,
            pl.BlockSpec((1, block, 1), lambda i, j: (i, j, 0)),
            pl.BlockSpec((1, 1, length), lambda i, j: (i, 0, 0)),
        ],
        out_specs=rows,
        out_shape=jax.ShapeDtypeStruct(q.shape, bf16),
        compiler_params=pltpu.CompilerParams(vmem_limit_bytes=40 << 20),
        name="attend",
    )(q, k, v, segments[:, :, None], segments[:, None, :])


def attend_back_kernel(
    q_ref, g_ref, k_ref, v_ref, sq_ref, sk_ref, dq_ref, dk_ref, dv_ref, kt, dqt, *, heads
):
    step = pl.program_id(1)
    q, g, k, v = q_ref[0], g_ref[0], k_ref[0], v_ref[0]
    size = q.shape[1] // heads

    @pl.when(step == 0)
    def _():
        kt[...] = k.T
        dk_ref[...] = jnp.zeros_like(dk_ref)
        dv_ref[...] = jnp.zeros_like(dv_ref)

    allowed = sk_ref[0] == sq_ref[0]
    zero = jnp.zeros_like(q)
    for head in range(heads):
        here = head_mask(q.shape, head, size)
        own_q, own_g = jnp.where(here, q, zero), jnp.where(here, g, zero)
        scores = jnp.where(allowed, mm(k, own_q, NT), masked_score)
        weights = jnp.exp(scores - jnp.max(scores, axis=0, keepdims=True))
        probs = weights * (1.0 / jnp.sum(weights, axis=0, keepdims=True))
        grad = mm(v, own_g, NT)
        delta = jnp.sum(probs * grad, axis=0, keepdims=True)
        grad = (probs * (grad - delta)).astype(bf16)
        dv_ref[0] += mm(probs.astype(bf16), own_g)
        dk_ref[0] += mm(grad, own_q)
        dqt[pl.ds(head * size, size), :] = mm(kt[pl.ds(head * size, size), :], grad)
    dq_ref[0] = dqt[...].T


def attend_back(q, k, v, g, segments, heads):
    n, length, width = q.shape
    block = min(256, length)
    rows = pl.BlockSpec((1, block, width), lambda i, j: (i, j, 0))
    whole = pl.BlockSpec((1, length, width), lambda i, j: (i, 0, 0))
    return pl.pallas_call(
        functools.partial(attend_back_kernel, heads=heads),
        grid=(n, length // block),
        in_specs=[
            rows,
            rows,
            whole,
            whole,
            pl.BlockSpec((1, 1, block), lambda i, j: (i, 0, j)),
            pl.BlockSpec((1, length, 1), lambda i, j: (i, 0, 0)),
        ],
        out_specs=[rows, whole, whole],
        out_shape=[jax.ShapeDtypeStruct(q.shape, f32)] * 3,
        scratch_shapes=[pltpu.VMEM((width, length), bf16), pltpu.VMEM((width, block), f32)],
        compiler_params=pltpu.CompilerParams(vmem_limit_bytes=48 << 20),
        name="attend_back",
    )(q, g, k, v, segments[:, None, :], segments[:, :, None])


def swap_halves(values, heads):
    shape = values.shape
    split = values.reshape(shape[:-1] + (heads, 2, shape[-1] // heads // 2))
    return jnp.concatenate([-split[..., 1:, :], split[..., :1, :]], axis=-2).reshape(shape)


def on_device(
    hidden, segment_ids, cotangent, w_qkv, w_attn_out, w_in, w_mlp_out, gain_attn, gain_mlp
):
    fsdp, ctx = lax.axis_size("fsdp"), lax.axis_size("ctx")
    f, c = lax.axis_index("fsdp"), lax.axis_index("ctx")
    batch, span, width = hidden.shape
    pieces = ctx // fsdp
    n = batch // pieces
    own = n * pieces * span
    length = span * ctx
    heads = HEADS // fsdp
    size = width // HEADS
    cols = heads * size
    units = w_mlp_out.shape[0]
    rows = w_in.shape[0]
    both = ("ctx", "fsdp")

    def route(j):
        pairs = []
        for cc in range(ctx):
            for ff in range(fsdp):
                to_c, to_f = pieces * ff + (cc + j) % pieces, cc // pieces
                pairs.append((cc * fsdp + ff, to_c * fsdp + to_f))
        return pairs

    def deal(values):
        parts = []
        for j in range(pieces):
            part = lax.dynamic_slice_in_dim(values, (c + j) % pieces * n, n, 0)
            parts.append(lax.ppermute(part, both, route(j)))
        return jnp.stack(parts, axis=1)

    def undeal(values):
        out = jnp.zeros((batch,) + values.shape[2:], values.dtype)
        for j in range(pieces):
            part = lax.ppermute(values[:, j], both, [(b, a) for a, b in route(j)])
            out = lax.dynamic_update_slice_in_dim(out, part, (c + j) % pieces * n, 0)
        return out

    def partner(values, bit):
        return lax.ppermute(values, "fsdp", [(i, i ^ bit) for i in range(fsdp)])

    bits = []
    bit = fsdp // 2
    while bit:
        bits.append(bit)
        bit //= 2
    order = [0]
    for bit in bits:
        order = order + [o ^ bit for o in order]

    def collect(values):
        stack = values[None]
        for bit in bits:
            stack = jnp.concatenate([stack, partner(stack, bit)], axis=0)
        return stack

    def reduce(stack):
        for bit in reversed(bits):
            half = stack.shape[0] // 2
            got = partner(stack[half:], bit)
            stack = (stack[:half].astype(f32) + got.astype(f32)).astype(
                bf16 if half > 1 else f32
            )
        return stack[0]

    def to_sequences(stack):
        feat = stack.shape[-1]
        parts = stack.reshape(fsdp, n, pieces * span, feat)
        return jnp.swapaxes(parts, 0, 1).reshape(n, length, feat)

    def from_sequences(values):
        feat = values.shape[-1]
        parts = values.reshape(n, fsdp, pieces * span, feat)
        return jnp.swapaxes(parts, 0, 1).reshape(fsdp, own, feat)

    blocks = [
        (f ^ o) * pieces + (c % pieces - j) % pieces for o in order for j in range(pieces)
    ]
    positions = (jnp.stack(blocks)[:, None] * span + jnp.arange(span)[None, :]).reshape(length)
    everyone = lax.all_gather(segment_ids, both).reshape(ctx, fsdp, batch, span)
    everyone = everyone.transpose(1, 2, 0, 3).reshape(fsdp * batch, ctx, span)
    everyone = lax.dynamic_slice_in_dim(everyone, c * n, n, 0)
    segments = jnp.concatenate(
        [lax.dynamic_slice_in_dim(everyone, b, 1, 1) for b in blocks], axis=1
    ).reshape(n, length)
    half = size // 2
    inverse = rope_base ** (-(jnp.arange(half, dtype=f32) * 2.0 / size))
    angles = positions.astype(f32)[:, None] * jnp.tile(inverse, 2 * heads)[None, :]
    cosine, sine = jnp.cos(angles), jnp.sin(angles)
    scale = size**-0.5

    hidden_own = deal(hidden).reshape(own, width)
    cot_own = deal(cotangent).reshape(own, width)

    gain_a, gain_m = gain_attn.astype(f32)[:, None], gain_mlp.astype(f32)[:, None]
    qkv_rows = (w_qkv.astype(f32) * gain_a).astype(bf16).reshape(rows, 3, fsdp, cols)
    in_rows = (w_in.astype(f32) * gain_m).astype(bf16).reshape(rows, 2, fsdp, units)

    def to_columns(parts):
        feat = parts.shape[1] * parts.shape[3]
        out = jnp.zeros((fsdp * rows, feat), bf16)
        for o in range(fsdp):
            part = lax.dynamic_slice_in_dim(parts, f ^ o, 1, 2).reshape(rows, feat)
            if o:
                part = lax.ppermute(part, "fsdp", [(i, i ^ o) for i in range(fsdp)])
            out = lax.dynamic_update_slice_in_dim(out, part, (f ^ o) * rows, 0)
        return out

    def to_rows(total, groups):
        feat = total.shape[-1]
        small = total.shape[0] // (fsdp * ctx)
        parts = total.astype(bf16).reshape(fsdp, ctx, small, feat).transpose(1, 0, 2, 3)
        parts = lax.psum_scatter(parts, "ctx", scatter_dimension=0, tiled=False)
        parts = lax.all_to_all(parts, "fsdp", 0, 0, tiled=True)
        parts = parts.reshape(fsdp, small, groups, feat // groups).transpose(1, 2, 0, 3)
        parts = parts.reshape(small, fsdp * feat)
        return lax.all_gather(parts, "ctx", axis=0, tiled=True).astype(f32)

    w_qkv_cols = to_columns(qkv_rows)
    w_in_cols = to_columns(in_rows)

    def normalise(values):
        center = values - jnp.mean(values, axis=-1, keepdims=True)
        rate = lax.rsqrt(jnp.mean(center * center, axis=-1, keepdims=True) + norm_eps)
        return center * rate, rate

    def norm_back(grad, unit, rate):
        return rate * (
            grad
            - jnp.mean(grad, axis=-1, keepdims=True)
            - unit * jnp.mean(grad * unit, axis=-1, keepdims=True)
        )

    hidden_wide = hidden_own.astype(f32)
    unit1, rate1 = normalise(hidden_wide)
    unit1_all = to_sequences(collect(unit1.astype(bf16))).reshape(n * length, width)
    cot_all = collect(cot_own).reshape(fsdp * own, width)

    mixed = mm(unit1_all, w_qkv_cols).reshape(n, length, 3 * cols)
    q_wide, k_wide = mixed[..., :cols], mixed[..., cols : 2 * cols]
    q = ((q_wide * cosine + swap_halves(q_wide, heads) * sine) * scale).astype(bf16)
    k = (k_wide * cosine + swap_halves(k_wide, heads) * sine).astype(bf16)
    v = mixed[..., 2 * cols :].astype(bf16)
    attended = attend(q, k, v, segments, heads).reshape(n * length, cols)

    partial = from_sequences(mm(attended, w_attn_out).astype(bf16).reshape(n, length, width))
    residual = hidden_wide + reduce(partial)
    unit2, rate2 = normalise(residual)
    unit2_all = collect(unit2.astype(bf16)).reshape(fsdp * own, width)

    inner = mm(unit2_all, w_in_cols)
    act, gate = inner[:, :units], inner[:, units:]
    phi = 0.5 * (1.0 + lax.erf(act * (2.0**-0.5)))
    activated = (act * phi * gate).astype(bf16)
    output = residual + reduce(mm(activated, w_mlp_out).astype(bf16).reshape(fsdp, own, width))

    grad_activated = mm(cot_all, w_mlp_out, NT)
    density = jnp.exp(-0.5 * act * act) * (2.0 * jnp.pi) ** -0.5
    grad_inner = jnp.concatenate(
        [grad_activated * gate * (phi + act * density), grad_activated * act * phi], axis=1
    ).astype(bf16)
    sum_mlp_out = mm(activated, cot_all, TN)
    sum_in = mm(unit2_all, grad_inner, TN)
    u2 = reduce(mm(grad_inner, w_in_cols, NT).astype(bf16).reshape(fsdp, own, width))
    grad_residual = cot_own.astype(f32) + norm_back(u2, unit2, rate2)
    grad_low = to_sequences(collect(grad_residual.astype(bf16))).reshape(n * length, width)

    sum_attn_out = mm(attended, grad_low, TN)
    grad_attended = mm(grad_low, w_attn_out, NT).astype(bf16).reshape(n, length, cols)
    dq, dk, dv = attend_back(q, k, v, grad_attended, segments, heads)
    dq = (dq * cosine - swap_halves(dq * sine, heads)) * scale
    dk = dk * cosine - swap_halves(dk * sine, heads)
    grad_mixed = jnp.concatenate([dq, dk, dv], axis=-1).astype(bf16).reshape(n * length, 3 * cols)
    sum_qkv = mm(unit1_all, grad_mixed, TN)
    u1 = from_sequences(
        mm(grad_mixed, w_qkv_cols, NT).astype(bf16).reshape(n, length, width)
    )
    input_grad = grad_residual + norm_back(reduce(u1), unit1, rate1)

    out = undeal(output.astype(bf16).reshape(n, pieces, span, width))
    back = undeal(input_grad.astype(bf16).reshape(n, pieces, span, width)).astype(f32)

    def over_ctx(total):
        return lax.psum(total.astype(bf16), "ctx").astype(f32)

    grad_mlp_out = over_ctx(sum_mlp_out)
    grad_attn_out = over_ctx(sum_attn_out)
    sum_in_rows = to_rows(sum_in, 2)
    sum_qkv_rows = to_rows(sum_qkv, 3)
    return (
        out,
        back,
        sum_qkv_rows * gain_a,
        grad_attn_out,
        sum_in_rows * gain_m,
        grad_mlp_out,
        jnp.sum(sum_qkv_rows * w_qkv.astype(f32), axis=1),
        jnp.sum(sum_in_rows * w_in.astype(f32), axis=1),
    )


def solution(mesh):
    in_specs = (
        P("fsdp", "ctx", None),
        P("fsdp", "ctx"),
        P("fsdp", "ctx", None),
        P("fsdp", None),
        P("fsdp", None),
        P("fsdp", None),
        P("fsdp", None),
        P("fsdp"),
        P("fsdp"),
    )
    out_specs = (
        P("fsdp", "ctx", None),
        P("fsdp", "ctx", None),
        P("fsdp", None),
        P("fsdp", None),
        P("fsdp", None),
        P("fsdp", None),
        P("fsdp"),
        P("fsdp"),
    )
    return jax.shard_map(
        on_device, mesh=mesh, in_specs=in_specs, out_specs=out_specs, check_vma=False
    )
```

```python
import functools

import jax
import jax.numpy as jnp
from jax import lax
from jax.experimental import pallas as pl
from jax.experimental.pallas import tpu as pltpu
from jax.sharding import PartitionSpec as P

HEADS = 16
rope_base = 160000.0
norm_eps = 1e-05
masked_score = -1e30
bf16 = jnp.bfloat16
f32 = jnp.float32
NT = (((1,), (1,)), ((), ()))
NN = (((1,), (0,)), ((), ()))
TN = (((0,), (0,)), ((), ()))
TAG = 16


def mm(a, b, dims=NN):
    return lax.dot_general(a, b, dims, preferred_element_type=f32)


def call(kernel, name, out_shape, grid, scratch, args, flops, limit=56):
    def spec(a):
        if isinstance(a, tuple):
            return a[1]
        if a.dtype == jnp.int32:
            return pl.BlockSpec(memory_space=pltpu.SMEM)
        return pl.BlockSpec(
            a.shape, lambda s, nd=len(a.shape): (0,) * nd, pipeline_mode=pl.Buffered(1)
        )

    specs = [spec(a) for a in args]
    args = [a[0] if isinstance(a, tuple) else a for a in args]
    moved = sum(a.size * a.dtype.itemsize for a in args)
    moved += sum(a.size * a.dtype.itemsize for a in out_shape)
    return pl.pallas_call(
        kernel,
        grid=(grid,),
        in_specs=specs,
        out_specs=[spec(a) for a in out_shape],
        out_shape=out_shape,
        scratch_shapes=scratch,
        compiler_params=pltpu.CompilerParams(vmem_limit_bytes=limit << 20),
        cost_estimate=pl.CostEstimate(
            flops=int(flops), bytes_accessed=int(moved), transcendentals=0
        ),
        name=name,
    )(*args)


def shape_of(shape, dtype=bf16):
    return jax.ShapeDtypeStruct(shape, dtype)


def head_mask(shape, head, size):
    return lax.broadcasted_iota(jnp.int32, shape, 1) // size == head


def swap(values, size):
    width, half = values.shape[1], size // 2
    if width == size:
        return jnp.concatenate([values[:, half:], values[:, :half]], axis=1)
    lane = lax.broadcasted_iota(jnp.int32, values.shape, 1) % size
    return jnp.where(
        lane < half, pltpu.roll(values, width - half, 1), pltpu.roll(values, half, 1)
    )


def norm_stats(values):
    center = values - jnp.mean(values, axis=-1, keepdims=True)
    rate = lax.rsqrt(jnp.mean(center * center, axis=-1, keepdims=True) + norm_eps)
    return center * rate, rate


def norm_back(grad, unit, rate):
    return rate * (
        grad
        - jnp.mean(grad, axis=-1, keepdims=True)
        - unit * jnp.mean(grad * unit, axis=-1, keepdims=True)
    )


class Plan:
    def __init__(self, fsdp, ctx, batch, span, width, units, rows):
        self.fsdp, self.ctx, self.span, self.width = fsdp, ctx, span, width
        self.pieces = ctx // fsdp
        self.n = batch // self.pieces
        self.part = self.pieces * span
        self.own = self.n * self.part
        self.length = span * ctx
        self.heads = HEADS // fsdp
        self.size = width // HEADS
        self.cols = self.heads * self.size
        self.units, self.rows = units, rows
        self.padded = -(-units // 256) * 256
        self.small = rows // ctx
        self.groups = 2 if self.heads % 2 == 0 else 1
        self.lanes = self.cols // self.groups
        self.slab = self.lanes // ctx
        self.table = min(128, self.cols)
        bits = [1 << b for b in range(ctx.bit_length() - 1)]
        self.order = bits

    def locations(self):
        return [
            (i, j, (i * self.pieces + j) * self.span)
            for i in range(self.n)
            for j in range(self.pieces)
        ]


def storage(x, order):
    at = 0
    for bit in order:
        at = at * 2 + x // bit % 2
    return at


def cut_kernel(qkv, w_in, gain_a, gain_m, out, *, p):
    fs, cols, units, rows, small = p.fsdp, p.cols, p.units, p.rows, p.small
    if 3 * cols != units:
        out[:, rows:, units:] = jnp.zeros((fs, 2 * small, 3 * cols - units), bf16)
    for t in range(fs):
        for m in range(3):
            at = m * p.width + t * cols
            value = qkv[:, at : at + cols].astype(f32) * gain_a[...]
            out[t, :rows, m * cols : (m + 1) * cols] = value.astype(bf16)
        for m in range(2):
            at = (m * fs + t) * units
            value = w_in[:, at : at + units].astype(f32) * gain_m[...]
            out[t, rows + m * small : rows + (m + 1) * small, :units] = value.astype(bf16)


def unit_kernel(*refs, p):
    pieces, unit = refs[:-1], refs[-1]
    unit[p.own :, :] = jnp.zeros((TAG, p.width), bf16)
    for i, j, at in p.locations():
        ref = pieces[j]
        value, _ = norm_stats(ref[i, : p.span].astype(f32))
        unit[at : at + p.span] = value.astype(bf16)
        unit[p.own :, at : at + p.span] = ref[i, p.span :, : p.span]


def project_kernel(*refs, p):
    fs, gs = p.fsdp, p.part
    xs, rest = refs[:fs], refs[fs:]
    cut, cos, sin, q_ref, k_ref, v_ref, seg_ref, w, x = rest
    step = pl.program_id(0)
    scale = p.size**-0.5

    @pl.when(step == 0)
    def _():
        for ff in range(fs):
            w[ff * p.rows : (ff + 1) * p.rows] = cut[ff, : p.rows]

    for o in range(fs):

        @pl.when(step == o)
        def _(o=o):
            x[...] = xs[o][: p.own]
            for i in range(p.n):
                tag = xs[o][p.own : p.own + TAG, i * gs : (i + 1) * gs].astype(f32)
                seg_ref[i, :, o * gs : (o + 1) * gs] = tag[:8]

    mixed = mm(x[...], w[...])
    rows = pl.ds(pl.multiple_of(step * gs, gs), gs)
    reps = p.cols // p.table
    cosine = jnp.concatenate([cos[rows, :]] * reps, axis=1)
    sine = jnp.concatenate([sin[rows, :]] * reps, axis=1)
    for i in range(p.n):
        own = mixed[i * gs : (i + 1) * gs]
        query, key = own[:, : p.cols], own[:, p.cols : 2 * p.cols]
        query = (query * cosine + swap(query, p.size) * sine) * scale
        q_ref[i, rows, :] = query.astype(bf16)
        k_ref[i, rows, :] = (key * cosine + swap(key, p.size) * sine).astype(bf16)
        v_ref[i, rows, :] = own[:, 2 * p.cols :].astype(bf16)


def attend_kernel(q_ref, k_ref, v_ref, seg_ref, wo, *rest, p):
    fs, gs = p.fsdp, p.part
    parts, (att_ref, made) = rest[:fs], rest[fs:]
    step = pl.program_id(0)
    i, o = step // fs, step % fs
    rows = pl.ds(pl.multiple_of(o * gs, gs), gs)
    q, k, v = q_ref[i, rows, :], k_ref[i], v_ref[i]
    allowed = seg_ref[i, :, rows].T[:, :1] == seg_ref[i, :1, :]
    total = jnp.zeros(q.shape, f32)
    for head in range(p.heads):
        here = head_mask(q.shape, head, p.size)
        scores = mm(jnp.where(here, q, jnp.zeros_like(q)), k, NT)
        scores = jnp.where(allowed, scores, masked_score)
        weights = jnp.exp(scores - jnp.max(scores, axis=1, keepdims=True))
        row = mm(weights.astype(bf16), v) / jnp.sum(weights, axis=1, keepdims=True)
        total = jnp.where(here, row, total)
    attended = total.astype(bf16)
    att_ref[i, rows, :] = attended
    made[...] = mm(attended, wo[...]).astype(bf16)
    for oo in range(fs):

        @pl.when(o == oo)
        def _(oo=oo):
            parts[oo][pl.ds(pl.multiple_of(i * gs, gs), gs), :] = made[...]


def backward_kernel(*refs, p):
    fs, gs, cols = p.fsdp, p.part, p.lanes
    gls, xs, rest = refs[:fs], refs[fs : 2 * fs], refs[2 * fs :]
    wo, q_ref, k_ref, v_ref, att_ref, seg_ref, cos, sin, c_ref = rest[:9]
    gm, sums = rest[9:11]
    kt, dqt, dk, dv, gl, x, seg_col, sum_qkv, sum_out = rest[11:]
    step = pl.program_id(0)
    scale = p.size**-0.5
    reps = cols // p.table

    def turned(grad, rows):
        cosine = jnp.concatenate([cos[rows, :]] * reps, axis=1)
        sine = jnp.concatenate([sin[rows, :]] * reps, axis=1)
        return grad * cosine - swap(grad, p.size) * sine

    @pl.when(step == 0)
    def _():
        sum_out[...] = jnp.zeros_like(sum_out)
        sum_qkv[...] = jnp.zeros_like(sum_qkv)

    @pl.when(step < p.n * fs)
    def _():
        i, o = step // fs, step % fs
        rows = pl.ds(pl.multiple_of(o * gs, gs), gs)
        for oo in range(fs):

            @pl.when(o == oo)
            def _(oo=oo):
                gl[...] = gls[oo][pl.ds(pl.multiple_of(i * gs, gs), gs), :]

        q, k, v = q_ref[i, rows, :], k_ref[i], v_ref[i]

        @pl.when(o == 0)
        def _():
            kt[...] = k.T
            dk[...] = jnp.zeros_like(dk)
            dv[...] = jnp.zeros_like(dv)
            seg_col[...] = seg_ref[i].T[:, :1]

        low = gl[...]
        g = mm(low, wo[...], NT).astype(bf16)
        sum_out[...] += mm(att_ref[i, rows, :], low, TN)
        allowed = seg_col[...] == seg_ref[i, :1, rows]
        zero = jnp.zeros_like(q)
        for head in range(p.heads // p.groups):
            here = head_mask(q.shape, head, p.size)
            own_q, own_g = jnp.where(here, q, zero), jnp.where(here, g, zero)
            scores = jnp.where(allowed, mm(k, own_q, NT), masked_score)
            weights = jnp.exp(scores - jnp.max(scores, axis=0, keepdims=True))
            probs = weights * (1.0 / jnp.sum(weights, axis=0, keepdims=True))
            grad = mm(v, own_g, NT)
            delta = jnp.sum(probs * grad, axis=0, keepdims=True)
            grad = (probs * (grad - delta)).astype(bf16)
            dv[...] += mm(probs.astype(bf16), own_g)
            dk[...] += mm(grad, own_q)
            at = pl.ds(head * p.size, p.size)
            dqt[at, :] = mm(kt[at, :], grad)
        gm[i, rows, :cols] = (turned(dqt[...].T, rows) * scale).astype(bf16)

        @pl.when(o == fs - 1)
        def _():
            gm[i, :, cols : 2 * cols] = turned(dk[...], slice(None)).astype(bf16)
            gm[i, :, 2 * cols :] = dv[...].astype(bf16)

    @pl.when(step >= p.n * fs)
    def _():
        o = step - p.n * fs
        rows = pl.ds(pl.multiple_of(o * gs, gs), gs)
        for oo in range(fs):

            @pl.when(o == oo)
            def _(oo=oo):
                x[...] = xs[oo][: p.own]

        grad = jnp.concatenate([gm[i, rows, :] for i in range(p.n)], axis=0)
        sum_qkv[...] += mm(x[...], grad, TN)

    @pl.when(step == p.n * fs + fs - 1)
    def _():
        small, slab = p.small, p.slab
        for cc in range(p.ctx):
            away = storage(c_ref[0] ^ cc, p.order)
            for ff in range(fs):
                for m in range(3):
                    part = sum_qkv[
                        ff * p.rows + cc * small : ff * p.rows + (cc + 1) * small,
                        m * cols : (m + 1) * cols,
                    ]
                    at = (ff * 3 + m) * small
                    sums[away, at : at + small, :] = part.astype(bf16)
            for d in range(p.width // cols):
                part = sum_out[cc * slab : (cc + 1) * slab, d * cols : (d + 1) * cols]
                at = 3 * fs * small + d * slab
                sums[away, at : at + slab, :] = part.astype(bf16)


def spread_kernel(*refs, p):
    gms, w, parts, made = refs[: p.groups], refs[p.groups], refs[p.groups + 1 : -1], refs[-1]
    o, lanes = pl.program_id(0), p.lanes
    rows = pl.ds(pl.multiple_of(o * p.part, p.part), p.part)
    for i in range(p.n):
        grad = jnp.concatenate(
            [gm[i, rows, m * lanes : (m + 1) * lanes] for m in range(3) for gm in gms], axis=1
        )
        made[i * p.part : (i + 1) * p.part] = mm(grad, w[...], NT).astype(bf16)
    for oo in range(p.fsdp):

        @pl.when(o == oo)
        def _(oo=oo):
            parts[oo][...] = made[...]


def mlp_kernel(*refs, p):
    fs, units, pad = p.fsdp, p.units, p.padded
    xs, cs, rest = refs[:fs], refs[fs : 2 * fs], refs[2 * fs :]
    w_in, w_out = rest[:2]
    outs, us, rest = rest[2 : 2 + fs], rest[2 + fs : 2 + 2 * fs], rest[2 + 2 * fs :]
    act_ref, da_ref, dg_ref, wa, wg, wm, x, ct, made, made_u = rest
    step = pl.program_id(0)

    @pl.when(step == 0)
    def _():
        if pad != units:
            wa[:, units:] = jnp.zeros((p.width, pad - units), bf16)
            wg[:, units:] = jnp.zeros((p.width, pad - units), bf16)
            wm[units:, :] = jnp.zeros((pad - units, p.width), bf16)
        wm[:units, :] = w_out[...]
        for cc in range(p.ctx):
            for ff in range(fs):
                at = ff * p.rows + cc * p.small
                wa[at : at + p.small, :units] = w_in[cc, ff, : p.small]
                wg[at : at + p.small, :units] = w_in[cc, ff, p.small :]

    for o in range(fs):

        @pl.when(step == o)
        def _(o=o):
            x[...] = xs[o][...]
            ct[...] = cs[o][...]

    act, gate = mm(x[...], wa[...]), mm(x[...], wg[...])
    phi = 0.5 * (1.0 + lax.erf(act * (2.0**-0.5)))
    gelu = act * phi
    active = (gelu * gate).astype(bf16)
    made[...] = mm(active, wm[...]).astype(bf16)
    grad = mm(ct[...], wm[...], NT)
    slope = phi + act * (jnp.exp(-0.5 * act * act) * 0.3989422804014327)
    da, dg = (grad * gate * slope).astype(bf16), (grad * gelu).astype(bf16)
    made_u[...] = (mm(da, wa[...], NT) + mm(dg, wg[...], NT)).astype(bf16)
    rows = pl.ds(pl.multiple_of(step * p.own, p.own), p.own)
    act_ref[rows, :], da_ref[rows, :], dg_ref[rows, :] = active, da, dg
    for o in range(fs):

        @pl.when(step == o)
        def _(o=o):
            outs[o][...] = made[...]
            us[o][...] = made_u[...]


def mlp_sums_kernel(*refs, p):
    fs, units = p.fsdp, p.units
    xs, cs, rest = refs[:fs], refs[fs : 2 * fs], refs[2 * fs :]
    act_ref, da_ref, dg_ref, c_ref, in_out, mlp_out, sa, sg, sm, x, ct = rest
    step = pl.program_id(0)

    @pl.when(step == 0)
    def _():
        sa[...] = jnp.zeros_like(sa)
        sg[...] = jnp.zeros_like(sg)
        sm[...] = jnp.zeros_like(sm)

    for o in range(fs):

        @pl.when(step == o)
        def _(o=o):
            x[...] = xs[o][...]
            ct[...] = cs[o][...]

    rows = pl.ds(pl.multiple_of(step * p.own, p.own), p.own)
    sa[...] += mm(x[...], da_ref[rows, :], TN)
    sg[...] += mm(x[...], dg_ref[rows, :], TN)
    sm[...] += mm(act_ref[rows, :], ct[...], TN)

    @pl.when(step == fs - 1)
    def _():
        slab = p.width // p.ctx
        for cc in range(p.ctx):
            for ff in range(fs):
                at = ff * p.rows + cc * p.small
                in_out[cc, ff, 0] = sa[at : at + p.small, :units].astype(bf16)
                in_out[cc, ff, 1] = sg[at : at + p.small, :units].astype(bf16)
            away = storage(c_ref[0] ^ cc, p.order)
            mlp_out[away] = sm[:units, cc * slab : (cc + 1) * slab].astype(bf16)


def middle_kernel(*refs, p):
    g = p.pieces
    hidden, (a, b, c), (residual, unit) = refs[:g], refs[g : g + 3], refs[g + 3 :]
    for i, j, at in p.locations():
        rows = slice(at, at + p.span)
        total = a[rows].astype(f32) + b[rows].astype(f32) + c[rows].astype(f32)
        total = total + hidden[j][i, : p.span].astype(f32)
        residual[rows] = total
        unit[rows] = norm_stats(total)[0].astype(bf16)


def turn_kernel(a, b, c, residual, cot, grad, low, *, p):
    for _, _, at in p.locations():
        rows = slice(at, at + p.span)
        u = a[rows].astype(f32) + b[rows].astype(f32) + c[rows].astype(f32)
        unit, rate = norm_stats(residual[rows])
        total = cot[rows].astype(f32) + norm_back(u, unit, rate)
        grad[rows] = total
        low[rows] = total.astype(bf16)


def result_kernel(*refs, p):
    (a, b, c, residual), outs = refs[:4], refs[4:]
    for i, j, at in p.locations():
        rows = slice(at, at + p.span)
        total = a[rows].astype(f32) + b[rows].astype(f32) + c[rows].astype(f32)
        outs[j][i] = (total + residual[rows]).astype(bf16)


def last_kernel(*refs, p):
    g = p.pieces
    hidden, (a, b, c, grad), outs = refs[:g], refs[g : g + 4], refs[g + 4 :]
    for i, j, at in p.locations():
        rows = slice(at, at + p.span)
        u = a[rows].astype(f32) + b[rows].astype(f32) + c[rows].astype(f32)
        unit, rate = norm_stats(hidden[j][i, : p.span].astype(f32))
        outs[j][i] = (grad[rows] + norm_back(u, unit, rate)).astype(bf16)


def qkv_grad_kernel(*refs, p):
    stacks, rest = refs[: p.groups], refs[p.groups :]
    w, gain, c_ref, qkv, out, gain_grad = rest
    fs, small, slab, lanes = p.fsdp, p.small, p.slab, p.lanes
    for cc in range(p.ctx):
        away = storage(c_ref[0] ^ cc, p.order)
        rows = slice(cc * small, (cc + 1) * small)
        scale = gain[rows, :]
        total = jnp.zeros((small, lanes), f32)
        for g in range(p.groups):
            for ff in range(fs):
                for m in range(3):
                    at = (ff * 3 + m) * small
                    value = stacks[g][away, at : at + small, :].astype(f32)
                    there = m * p.width + ff * p.cols + g * lanes
                    qkv[rows, there : there + lanes] = value * scale
                    total = total + value * w[rows, there : there + lanes].astype(f32)
            for d in range(p.width // lanes):
                at = 3 * fs * small + d * slab
                value = stacks[g][away, at : at + slab, :].astype(f32)
                row = g * lanes + cc * slab
                out[row : row + slab, d * lanes : (d + 1) * lanes] = value
        gain_grad[rows, :] = jnp.sum(total, axis=1, keepdims=True)


def in_grad_kernel(sums, w, gain, grad, gain_grad):
    value = sums[...].astype(f32)
    grad[...] = value * gain[...]
    gain_grad[...] = jnp.sum(value * w[...].astype(f32), axis=1, keepdims=True)


def out_grad_kernel(stack, c_ref, grad, *, p):
    slab = p.width // p.ctx
    for cc in range(p.ctx):
        away = storage(c_ref[0] ^ cc, p.order)
        grad[:, cc * slab : (cc + 1) * slab] = stack[away].astype(f32)


def on_device(
    hidden, segment_ids, cotangent, w_qkv, w_attn_out, w_in, w_mlp_out, gain_attn, gain_mlp
):
    fsdp, ctx = lax.axis_size("fsdp"), lax.axis_size("ctx")
    f, c = lax.axis_index("fsdp"), lax.axis_index("ctx")
    batch, span, width = hidden.shape
    p = Plan(fsdp, ctx, batch, span, width, w_mlp_out.shape[0], w_in.shape[0])
    n, own, cols, units, rows, small = p.n, p.own, p.cols, p.units, p.rows, p.small
    length, pieces = p.length, p.pieces
    both = ("ctx", "fsdp")
    slots = range(fsdp)
    tile = shape_of((own, width))
    bits = [fsdp >> 1 + b for b in range(fsdp.bit_length() - 1)]

    def mixed_bits(index):
        out = 0
        for bit in bits:
            out = out + index // (fsdp // 2 // bit) % 2 * bit
        return out

    def route(j):
        pairs = []
        for cc in range(ctx):
            for ff in range(fsdp):
                to_c, to_f = (cc + j) % pieces * fsdp + mixed_bits(ff), cc // pieces
                pairs.append((cc * fsdp + ff, to_c * fsdp + to_f))
        return pairs

    def dealt(values):
        return [
            lax.dynamic_slice_in_dim(values, (c + j) % pieces * n, n, 0) for j in range(pieces)
        ]

    def deal(parts):
        return [lax.ppermute(part, both, route(j)) for j, part in enumerate(parts)]

    def undeal(parts):
        back = [
            lax.ppermute(part, both, [(b, a) for a, b in route(j)])
            for j, part in enumerate(parts)
        ]
        if pieces == 1:
            return back[0]
        blocks = []
        for b in range(pieces):
            block = back[0]
            for j in range(1, pieces):
                block = jnp.where((c + j) % pieces == b, back[j], block)
            blocks.append(block)
        return jnp.concatenate(blocks, axis=0)

    def partner(values, bit):
        return lax.ppermute(values, "fsdp", [(i, i ^ bit) for i in range(fsdp)])

    def collect(value):
        held = {0: value}
        for bit in bits:
            for o in list(held):
                held[o ^ bit] = partner(held[o], bit)
        return [held[o] for o in slots]

    def reduce(parts):
        held, side, last = dict(enumerate(parts)), None, None
        for bit in reversed(bits):
            for o in sorted(held, reverse=True):
                if not o & bit:
                    continue
                got, mine = partner(held.pop(o), bit), held[o ^ bit]
                if o == bits[0]:
                    last = got
                elif o == bits[1]:
                    side = got
                else:
                    held[o ^ bit] = (mine.astype(f32) + got.astype(f32)).astype(bf16)
        return held[0], side, last

    def away(values, bit):
        return lax.ppermute(values, "ctx", [(i, i ^ bit) for i in range(ctx)])

    def fold(stack, bit):
        half = stack.shape[0] // 2
        got = away(stack[half:], bit)
        return (stack[:half].astype(f32) + got.astype(f32)).astype(bf16)

    def double(value):
        stack = value[None]
        for bit in reversed(p.order):
            stack = jnp.concatenate([stack, away(stack, bit)], axis=0)
        return stack

    blocks = [
        (f ^ o) * pieces + (c // fsdp - j) % pieces for o in slots for j in range(pieces)
    ]
    positions = (jnp.stack(blocks)[:, None] * span + jnp.arange(span)[None, :]).reshape(length)
    half = p.size // 2
    inverse = rope_base ** (-(jnp.arange(half, dtype=f32) * 2.0 / p.size))
    angles = positions.astype(f32)[:, None] * inverse[None, :]
    cosine, sine = jnp.cos(angles), jnp.sin(angles)
    reps = p.table // p.size
    cosine = jnp.concatenate([cosine, cosine] * reps, axis=1)
    sine = jnp.concatenate([-sine, sine] * reps, axis=1)

    tags = jnp.pad(
        segment_ids.astype(bf16)[:, None, :], ((0, 0), (0, TAG - 1), (0, width - span))
    )
    hidden_cut, w_qkv, w_in = lax.optimization_barrier(
        (dealt(jnp.concatenate([hidden, tags], axis=1)), w_qkv, w_in)
    )
    hidden_parts = deal(hidden_cut)

    gain_a, gain_m = gain_attn.astype(f32)[:, None], gain_mlp.astype(f32)[:, None]
    here = jnp.reshape(c, (1,))
    (cut,) = call(
        functools.partial(cut_kernel, p=p),
        "cut",
        [shape_of((fsdp, rows + 2 * small, 3 * cols))],
        1,
        [],
        [
            w_qkv,
            lax.dynamic_slice_in_dim(w_in, c * small, small, 0),
            gain_a,
            lax.dynamic_slice_in_dim(gain_m, c * small, small, 0),
        ],
        1e6,
    )
    hidden_parts, cut, cotangent = lax.optimization_barrier((hidden_parts, cut, cotangent))
    cut = lax.all_to_all(cut, "fsdp", 0, 0, tiled=True)
    cot_parts = deal(dealt(cotangent))

    unit1 = call(
        functools.partial(unit_kernel, p=p),
        "unit1",
        [shape_of((own + TAG, width))],
        1,
        [],
        hidden_parts,
        1e6,
    )[0]
    unit1_slots = collect(unit1)
    unit1_slots, cut, cot_parts = lax.optimization_barrier((unit1_slots, cut, cot_parts))
    w_in_cols = lax.all_gather(cut[:, rows:, :units], "ctx", axis=0)
    cot_own = jnp.stack(cot_parts, axis=1).reshape(own, width)
    cot_slots = collect(cot_own)

    whole = shape_of((n, length, cols))
    q, k, v, segments, w_qkv_cols = call(
        functools.partial(project_kernel, p=p),
        "project",
        [whole] * 3 + [shape_of((n, 8, length), f32), shape_of((width, 3 * cols))],
        fsdp,
        [pltpu.VMEM((own, width), bf16)],
        unit1_slots + [cut, cosine, sine],
        4e9,
    )
    q, cot_slots = lax.optimization_barrier((q, cot_slots))
    made = call(
        functools.partial(attend_kernel, p=p),
        "attend",
        [tile] * fsdp + [whole],
        n * fsdp,
        [pltpu.VMEM((p.part, width), bf16)],
        [q, k, v, segments, w_attn_out],
        1.2e10,
    )
    attended_parts, attended = made[:fsdp], made[fsdp]

    residual, unit2 = call(
        functools.partial(middle_kernel, p=p),
        "middle",
        [shape_of((own, width), f32), tile],
        1,
        [],
        hidden_parts + list(reduce(attended_parts)),
        1e6,
    )
    unit2_slots = collect(unit2)

    wide = shape_of((fsdp * own, p.padded))
    made = call(
        functools.partial(mlp_kernel, p=p),
        "mlp",
        [tile] * (2 * fsdp) + [wide] * 3,
        fsdp,
        [pltpu.VMEM((width, p.padded), bf16)] * 2
        + [pltpu.VMEM((p.padded, width), bf16)]
        + [pltpu.VMEM((own, width), bf16)] * 4,
        unit2_slots + cot_slots + [w_in_cols, w_mlp_out],
        1.2e10,
    )
    out_parts, u2_parts, (active, da, dg) = made[:fsdp], made[fsdp : 2 * fsdp], made[2 * fsdp :]

    u2 = reduce(u2_parts)
    in_sums, mlp_sums = call(
        functools.partial(mlp_sums_kernel, p=p),
        "mlp_sums",
        [
            shape_of((ctx, fsdp, 2, small, units)),
            shape_of((ctx, units, width // ctx)),
        ],
        fsdp,
        [pltpu.VMEM((width, p.padded), f32)] * 2
        + [pltpu.VMEM((p.padded, width), f32)]
        + [pltpu.VMEM((own, width), bf16)] * 2,
        unit2_slots + cot_slots + [active, da, dg, here],
        6e9,
    )
    u2, in_sums, mlp_sums = lax.optimization_barrier((u2, in_sums, mlp_sums))
    grad_residual, grad_low = call(
        functools.partial(turn_kernel, p=p),
        "turn",
        [shape_of((own, width), f32), tile],
        1,
        [],
        list(u2) + [residual, cot_own],
        1e6,
    )
    low_slots = collect(grad_low)

    mlp_left = fold(mlp_sums, p.order[0])
    low_slots, mlp_left = lax.optimization_barrier((low_slots, mlp_left))
    mixed, attention_sums = [], []
    for group in range(p.groups):
        some = pl.BlockSpec(
            (n, length, p.lanes),
            lambda s, group=group: (0, 0, group),
            pipeline_mode=pl.Buffered(1),
        )
        wo_rows = pl.BlockSpec(
            (p.lanes, width), lambda s, group=group: (group, 0), pipeline_mode=pl.Buffered(1)
        )
        grad_mixed, sums = call(
            functools.partial(backward_kernel, p=p),
            "attention_back",
            [
                shape_of((n, length, 3 * p.lanes)),
                shape_of((ctx, 4 * fsdp * small, p.lanes)),
            ],
            n * fsdp + fsdp,
            [
                pltpu.VMEM((p.lanes, length), bf16),
                pltpu.VMEM((p.lanes, p.part), f32),
                pltpu.VMEM((length, p.lanes), f32),
                pltpu.VMEM((length, p.lanes), f32),
                pltpu.VMEM((p.part, width), bf16),
                pltpu.VMEM((own, width), bf16),
                pltpu.VMEM((length, 1), f32),
                pltpu.VMEM((width, 3 * p.lanes), f32),
                pltpu.VMEM((p.lanes, width), f32),
            ],
            low_slots
            + unit1_slots
            + [(w_attn_out, wo_rows), (q, some), (k, some), (v, some), (attended, some)]
            + [segments, cosine, sine, here],
            1.5e10,
        )
        if group < p.groups - 1:
            mlp_left = fold(mlp_left, p.order[1])
            low_slots, mlp_left = lax.optimization_barrier((low_slots, mlp_left))
        mixed.append(grad_mixed)
        attention_sums.append(sums)
    in_small = lax.psum_scatter(in_sums, "ctx", scatter_dimension=0, tiled=False)
    mixed, out_parts, in_small = lax.optimization_barrier((mixed, list(out_parts), in_small))
    u1_parts = call(
        functools.partial(spread_kernel, p=p),
        "spread",
        [tile] * fsdp,
        fsdp,
        [pltpu.VMEM((own, width), bf16)],
        mixed + [w_qkv_cols],
        2e9,
    )
    piece = [shape_of((n, span, width))] * pieces
    back_parts = call(
        functools.partial(last_kernel, p=p),
        "last",
        piece,
        1,
        [],
        hidden_parts + list(reduce(u1_parts)) + [grad_residual],
        1e6,
    )
    result_parts = call(
        functools.partial(result_kernel, p=p),
        "result",
        piece,
        1,
        [],
        list(reduce(out_parts)) + [residual],
        1e6,
    )
    out = undeal(result_parts)
    back = undeal(back_parts).astype(f32)

    in_small = lax.all_to_all(in_small, "fsdp", 0, 0, tiled=True)
    in_small = in_small.transpose(2, 1, 0, 3).reshape(small, 2 * fsdp * units)
    in_rows = lax.all_gather(in_small, "ctx", axis=0, tiled=True)

    while mlp_left.shape[0] > 1:
        mlp_left = fold(mlp_left, p.order[ctx.bit_length() - mlp_left.shape[0].bit_length()])
    mlp_stack = double(mlp_left[0])

    stacks = []
    for sums in attention_sums:
        for bit in p.order:
            sums = fold(sums, bit)
        mine = sums[0, : 3 * fsdp * small].reshape(fsdp, 3 * small, p.lanes)
        mine = lax.all_to_all(mine, "fsdp", 0, 0, tiled=True)
        mine = mine.reshape(3 * fsdp * small, p.lanes)
        stacks.append(double(jnp.concatenate([mine, sums[0, 3 * fsdp * small :]], axis=0)))

    grad_qkv, grad_out, grad_gain_a = call(
        functools.partial(qkv_grad_kernel, p=p),
        "qkv_grad",
        [
            shape_of((rows, 3 * width), f32),
            shape_of((cols, width), f32),
            shape_of((rows, 1), f32),
        ],
        1,
        [],
        stacks + [w_qkv, gain_a, here],
        1e6,
    )
    block = min(64, rows)
    some = pl.BlockSpec((block, 2 * fsdp * units), lambda s: (s, 0))
    thin = pl.BlockSpec((block, 1), lambda s: (s, 0))
    grad_in, grad_gain_m = pl.pallas_call(
        in_grad_kernel,
        grid=(rows // block,),
        in_specs=[some, some, thin],
        out_specs=[some, thin],
        out_shape=[shape_of(w_in.shape, f32), shape_of((rows, 1), f32)],
        compiler_params=pltpu.CompilerParams(vmem_limit_bytes=40 << 20),
        cost_estimate=pl.CostEstimate(
            flops=1000000, bytes_accessed=8 * w_in.size, transcendentals=0
        ),
        name="in_grad",
    )(in_rows, w_in, gain_m)
    (grad_mlp_out,) = call(
        functools.partial(out_grad_kernel, p=p),
        "out_grad",
        [shape_of((units, width), f32)],
        1,
        [],
        [mlp_stack, here],
        1e6,
    )
    return (
        out,
        back,
        grad_qkv,
        grad_out,
        grad_in,
        grad_mlp_out,
        grad_gain_a.reshape(rows),
        grad_gain_m.reshape(rows),
    )


def solution(mesh):
    in_specs = (
        P("fsdp", "ctx", None),
        P("fsdp", "ctx"),
        P("fsdp", "ctx", None),
        P("fsdp", None),
        P("fsdp", None),
        P("fsdp", None),
        P("fsdp", None),
        P("fsdp"),
        P("fsdp"),
    )
    out_specs = (
        P("fsdp", "ctx", None),
        P("fsdp", "ctx", None),
        P("fsdp", None),
        P("fsdp", None),
        P("fsdp", None),
        P("fsdp", None),
        P("fsdp"),
        P("fsdp"),
    )
    return jax.shard_map(
        on_device, mesh=mesh, in_specs=in_specs, out_specs=out_specs, check_vma=False
    )
```

```python
import functools

import jax
import jax.numpy as jnp
from jax import lax
from jax.experimental import pallas as pl
from jax.experimental.pallas import tpu as pltpu
from jax.sharding import PartitionSpec as P

HEADS = 16
rope_base = 160000.0
norm_eps = 1e-05
masked_score = -1e30
bf16 = jnp.bfloat16
f32 = jnp.float32
NT = (((1,), (1,)), ((), ()))
NN = (((1,), (0,)), ((), ()))
TN = (((0,), (0,)), ((), ()))
TAG = 16


def mm(a, b, dims=NN):
    return lax.dot_general(a, b, dims, preferred_element_type=f32)


class Late:
    def __init__(self, value):
        self.value = self.shape_is = value


def copies(pairs, sems):
    return [pltpu.make_async_copy(a, b, sems.at[k]) for k, (a, b) in enumerate(pairs)]


def call(kernel, name, out_shape, grid, scratch, args, flops, limit=56):
    def spec(a):
        if isinstance(a, tuple):
            return a[1]
        if isinstance(a, Late):
            return pl.BlockSpec(memory_space=pl.ANY)
        if a.dtype == jnp.int32:
            return pl.BlockSpec(memory_space=pltpu.SMEM)
        return pl.BlockSpec(
            a.shape, lambda s, nd=len(a.shape): (0,) * nd, pipeline_mode=pl.Buffered(1)
        )

    specs = [spec(a) for a in args]
    args = [a[0] if isinstance(a, tuple) else getattr(a, "value", a) for a in args]
    outs = [spec(a) for a in out_shape]
    out_shape = [a[0] if isinstance(a, tuple) else getattr(a, "shape_is", a) for a in out_shape]
    moved = sum(a.size * a.dtype.itemsize for a in args)
    moved += sum(a.size * a.dtype.itemsize for a in out_shape)
    return pl.pallas_call(
        kernel,
        grid=(grid,),
        in_specs=specs,
        out_specs=outs,
        out_shape=out_shape,
        scratch_shapes=scratch,
        compiler_params=pltpu.CompilerParams(vmem_limit_bytes=limit << 20),
        cost_estimate=pl.CostEstimate(
            flops=int(flops), bytes_accessed=int(moved), transcendentals=0
        ),
        name=name,
    )(*args)


def shape_of(shape, dtype=bf16):
    return jax.ShapeDtypeStruct(shape, dtype)


def head_mask(shape, head, size):
    return lax.broadcasted_iota(jnp.int32, shape, 1) // size == head


def swap(values, size):
    width, half = values.shape[1], size // 2
    if width == size:
        return jnp.concatenate([values[:, half:], values[:, :half]], axis=1)
    lane = lax.broadcasted_iota(jnp.int32, values.shape, 1) % size
    return jnp.where(
        lane < half, pltpu.roll(values, width - half, 1), pltpu.roll(values, half, 1)
    )


def norm_stats(values):
    center = values - jnp.mean(values, axis=-1, keepdims=True)
    rate = lax.rsqrt(jnp.mean(center * center, axis=-1, keepdims=True) + norm_eps)
    return center * rate, rate


def norm_back(grad, unit, rate):
    return rate * (
        grad
        - jnp.mean(grad, axis=-1, keepdims=True)
        - unit * jnp.mean(grad * unit, axis=-1, keepdims=True)
    )


class Plan:
    def __init__(self, fsdp, ctx, batch, span, width, units, rows):
        self.fsdp, self.ctx, self.span, self.width = fsdp, ctx, span, width
        self.pieces = ctx // fsdp
        self.n = batch // self.pieces
        self.part = self.pieces * span
        self.own = self.n * self.part
        self.length = span * ctx
        self.heads = HEADS // fsdp
        self.size = width // HEADS
        self.cols = self.heads * self.size
        self.units, self.rows = units, rows
        self.padded = -(-units // 256) * 256
        self.small = rows // ctx
        self.groups = 2 if self.heads % 2 == 0 else 1
        self.lanes = self.cols // self.groups
        self.slab = self.lanes // ctx
        self.table = min(128, self.cols)
        bits = [1 << b for b in range(ctx.bit_length() - 1)]
        self.order = bits
        self.last_order = bits[1:] + bits[:1]

    def locations(self):
        return [
            (i, j, (i * self.pieces + j) * self.span)
            for i in range(self.n)
            for j in range(self.pieces)
        ]


def storage(x, order):
    at = 0
    for bit in order:
        at = at * 2 + x // bit % 2
    return at


def cut_kernel(w, gain, at_ref, mine, other, *, p, feed):
    half, here = p.rows // 2, at_ref[0]
    side = at_ref[1] % 2
    near = pl.ds(pl.multiple_of(side * half, half), half)
    far = pl.ds(pl.multiple_of((1 - side) * half, half), half)
    size = p.units if feed else p.cols
    if feed and p.padded != size:
        mine[:, :, size:] = jnp.zeros((p.fsdp, 2 * half, p.padded - size), bf16)
        other[:, :, size:] = jnp.zeros((2, 2 * half, p.padded - size), bf16)
    for t in range(p.fsdp):
        o = t ^ here
        for m in range(2 if feed else 3):
            at = (m * p.fsdp + t) * size
            if feed:
                there = slice(m * half, (m + 1) * half), slice(0, size)
            else:
                there = slice(None), slice(m * size, (m + 1) * size)
            value = w[near, at : at + size].astype(f32) * gain[near, :]
            mine[(o,) + there] = value.astype(bf16)

            @pl.when(o < 2)
            def _(at=at, there=there, o=o):
                value = w[far, at : at + size].astype(f32) * gain[far, :]
                other[(o,) + there] = value.astype(bf16)


def unit_kernel(*refs, p):
    pieces, unit = refs[:-1], refs[-1]
    unit[p.own :, :] = jnp.zeros((TAG, p.width), bf16)
    for i, j, at in p.locations():
        ref = pieces[j]
        value, _ = norm_stats(ref[i, : p.span].astype(f32))
        unit[at : at + p.span] = value.astype(bf16)
        unit[p.own :, at : at + p.span] = ref[i, p.span :, : p.span]


def project_kernel(*refs, p):
    fs, gs = p.fsdp, p.part
    xs, rest = refs[:fs], refs[fs:]
    near, other, rest = rest[:fs], rest[fs : 2 * fs], rest[2 * fs :]
    cos, sin, at_ref, q_ref, k_ref, v_ref, seg_ref, w, x, w_sems, x_sems = rest
    step = pl.program_id(0)
    scale = p.size**-0.5
    half, side = p.rows // 2, at_ref[1] % 2
    pairs = []
    for o in range(fs):
        base = (at_ref[0] ^ o) * 2
        for part, at in ((near[o], base + side), (other[o], base + 1 - side)):
            pairs.append((part, w.at[pl.ds(pl.multiple_of(at * half, half), half), :]))
    w_copies = copies(pairs, w_sems)
    x_copies = copies([(xs[o], x.at[o]) for o in range(fs)], x_sems)

    @pl.when(step == 0)
    def _():
        for copy in x_copies[:1] + w_copies + x_copies[1:]:
            copy.start()
        for copy in w_copies:
            copy.wait()

    for o in range(fs):

        @pl.when(step == o)
        def _(o=o):
            x_copies[o].wait()
            for i in range(p.n):
                tag = x[o, p.own : p.own + TAG, i * gs : (i + 1) * gs].astype(f32)
                seg_ref[i, :, o * gs : (o + 1) * gs] = tag[:8]

    mixed = mm(x[step, : p.own], w[...])
    rows = pl.ds(pl.multiple_of(step * gs, gs), gs)
    reps = p.cols // p.table
    cosine = jnp.concatenate([cos[rows, :]] * reps, axis=1)
    sine = jnp.concatenate([sin[rows, :]] * reps, axis=1)
    for i in range(p.n):
        own = mixed[i * gs : (i + 1) * gs]
        query, key = own[:, : p.cols], own[:, p.cols : 2 * p.cols]
        query = (query * cosine + swap(query, p.size) * sine) * scale
        q_ref[i, rows, :] = query.astype(bf16)
        k_ref[i, rows, :] = (key * cosine + swap(key, p.size) * sine).astype(bf16)
        v_ref[i, rows, :] = own[:, 2 * p.cols :].astype(bf16)


def attend_kernel(q_ref, k_ref, v_ref, seg_ref, wo, *rest, p):
    fs, gs = p.fsdp, p.part
    parts, (att_ref, norm_ref, made) = rest[:fs], rest[fs:]
    step = pl.program_id(0)
    i, o = step // fs, step % fs
    rows = pl.ds(pl.multiple_of(o * gs, gs), gs)
    q, k, v = q_ref[i, rows, :], k_ref[i], v_ref[i]
    allowed = seg_ref[i, :, rows].T[:, :1] == seg_ref[i, :1, :]
    attended = jnp.zeros(q.shape, f32)
    norms = jnp.zeros((gs, 128), f32)
    lane = lax.broadcasted_iota(jnp.int32, norms.shape, 1)
    for head in range(p.heads):
        here = head_mask(q.shape, head, p.size)
        scores = mm(jnp.where(here, q, jnp.zeros_like(q)), k, NT)
        scores = jnp.where(allowed, scores, masked_score)
        peak = jnp.max(scores, axis=1, keepdims=True)
        weights = jnp.exp(scores - peak)
        total = jnp.sum(weights, axis=1, keepdims=True)
        attended = jnp.where(here, mm(weights.astype(bf16), v) / total, attended)
        norms = jnp.where(lane == head, peak + jnp.log(total), norms)
    norm_ref[i, :, rows] = norms.T[:8]
    attended = attended.astype(bf16)
    att_ref[i, rows, :] = attended
    made[...] = mm(attended, wo[...]).astype(bf16)
    for oo in range(fs):

        @pl.when(o == oo)
        def _(oo=oo):
            parts[oo][pl.ds(pl.multiple_of(i * gs, gs), gs), :] = made[...]


def flip_kernel(*refs, p):
    xs, out = refs[:-1], refs[-1]
    gs = p.part
    for o in range(p.fsdp):

        @pl.when(pl.program_id(0) == o)
        def _(o=o):
            for i in range(p.n):
                out[i, :, o * gs : (o + 1) * gs] = xs[o][i * gs : (i + 1) * gs, :].T


def shares(span_ref, i, a, b, fs):
    one, two = (i * fs + a) * 2, (i * fs + b) * 2
    return jnp.logical_and(
        span_ref[one] <= span_ref[two + 1], span_ref[two] <= span_ref[one + 1]
    )


def backward_kernel(*refs, p, group):
    fs, gs, cols = p.fsdp, p.part, p.lanes
    gls, rest = refs[:fs], refs[fs:]
    xt, wo, rest = rest[0], rest[1], rest[2:]
    q_ref, k_ref, v_ref, att_ref, seg_ref, norm_ref, cos, sin, c_ref, span_ref = rest[:10]
    gm, sums, kt, dqt, dk, dv, gl, seg_col, sum_qkv, sum_out, flat, sems, flat_sem = rest[10:]
    step = pl.program_id(0)
    scale = p.size**-0.5
    reps = cols // p.table

    def turned(grad, rows):
        cosine = jnp.concatenate([cos[rows, :]] * reps, axis=1)
        sine = jnp.concatenate([sin[rows, :]] * reps, axis=1)
        return grad * cosine - swap(grad, p.size) * sine

    pairs = [
        (gls[o].at[i * gs : (i + 1) * gs], gl.at[i, o * gs : (o + 1) * gs])
        for i in range(p.n)
        for o in range(fs)
    ]
    low_copies = copies(pairs, sems)
    flat_copy = pltpu.make_async_copy(xt, flat, flat_sem.at[0])

    @pl.when(step == 0)
    def _():
        for copy in low_copies:
            copy.start()
        flat_copy.start()

    @pl.when(step < p.n * fs)
    def _():
        i, o = step // fs, step % fs
        rows = pl.ds(pl.multiple_of(o * gs, gs), gs)
        for k in range(p.n * fs):

            @pl.when(step == k)
            def _(k=k):
                low_copies[k].wait()

        q = q_ref[i, rows, :]

        @pl.when(o == 0)
        def _():
            kt[...] = k_ref[i].T
            dk[...] = jnp.zeros_like(dk)
            dv[...] = jnp.zeros_like(dv)
            seg_col[...] = seg_ref[i].T[:, :1]

        attended = att_ref[i, rows, :]
        g = mm(gl[i, rows, :], wo[...], NT).astype(bf16)
        count = p.heads // p.groups
        picks = lax.broadcasted_iota(jnp.int32, (8, cols), 0)
        picks = (lax.broadcasted_iota(jnp.int32, (8, cols), 1) // p.size == picks).astype(f32)
        deltas = lax.dot_general(
            picks,
            g.astype(f32) * attended.astype(f32),
            NT,
            precision=lax.Precision.HIGHEST,
            preferred_element_type=f32,
        )
        zero = jnp.zeros_like(q)
        masks = [head_mask(q.shape, h, p.size) for h in range(count)]
        own_q = [jnp.where(mask, q, zero) for mask in masks]
        own_g = [jnp.where(mask, g, zero) for mask in masks]
        mine = seg_ref[i, :1, rows]
        dqt[...] = jnp.zeros_like(dqt)
        for kk in range(fs):
            keys = slice(kk * gs, (kk + 1) * gs)

            @pl.when(shares(span_ref, i, o, kk, fs))
            def _(keys=keys):
                k, v = k_ref[i, keys, :], v_ref[i, keys, :]
                allowed = seg_col[keys, :] == mine
                for h in range(count):
                    first = group * count + h
                    scores = jnp.where(allowed, mm(k, own_q[h], NT), masked_score)
                    probs = jnp.exp(scores - norm_ref[i, first : first + 1, rows])
                    grad = mm(v, own_g[h], NT)
                    grad = (probs * (grad - deltas[h : h + 1, :])).astype(bf16)
                    dv[keys, :] += mm(probs.astype(bf16), own_g[h])
                    dk[keys, :] += mm(grad, own_q[h])
                    at = slice(h * p.size, (h + 1) * p.size)
                    dqt[at, :] += mm(kt[at, keys], grad)

        gm[i, rows, :cols] = (turned(dqt[...].T, rows) * scale).astype(bf16)

        @pl.when(o == fs - 1)
        def _():
            gm[i, :, cols : 2 * cols] = turned(dk[...], slice(None)).astype(bf16)
            gm[i, :, 2 * cols :] = dv[...].astype(bf16)

    @pl.when(step == p.n * fs)
    def _():
        flat_copy.wait()
        total = [mm(flat[i], gm[i]) for i in range(p.n)]
        sum_qkv[...] = sum(total[1:], total[0])
        total = [mm(att_ref[i].T, gl[i]) for i in range(p.n)]
        sum_out[...] = sum(total[1:], total[0])
        small, slab = p.small, p.slab
        for cc in range(p.ctx):
            away = storage(c_ref[0] ^ cc, p.order)
            for ff in range(fs):
                for m in range(3):
                    part = sum_qkv[
                        ff * p.rows + cc * small : ff * p.rows + (cc + 1) * small,
                        m * cols : (m + 1) * cols,
                    ]
                    at = (ff * 3 + m) * small
                    sums[away, at : at + small, :] = part.astype(bf16)
            for d in range(p.width // cols):
                part = sum_out[cc * slab : (cc + 1) * slab, d * cols : (d + 1) * cols]
                at = 3 * fs * small + d * slab
                sums[away, at : at + slab, :] = part.astype(bf16)


def spread_kernel(*refs, p):
    gms, w, parts, made = refs[: p.groups], refs[p.groups], refs[p.groups + 1 : -1], refs[-1]
    o, lanes = pl.program_id(0), p.lanes
    rows = pl.ds(pl.multiple_of(o * p.part, p.part), p.part)
    for i in range(p.n):
        grad = jnp.concatenate(
            [gm[i, rows, m * lanes : (m + 1) * lanes] for m in range(3) for gm in gms], axis=1
        )
        made[i * p.part : (i + 1) * p.part] = mm(grad, w[...], NT).astype(bf16)
    for oo in range(p.fsdp):

        @pl.when(o == oo)
        def _(oo=oo):
            parts[oo][...] = made[...]


def mlp_kernel(*refs, p):
    fs, units, pad = p.fsdp, p.units, p.padded
    xs, cs, rest = refs[:fs], refs[fs : 2 * fs], refs[2 * fs :]
    near, other, rest = rest[:fs], rest[fs : 2 * fs], rest[2 * fs :]
    w_out, at_ref, rest = rest[0], rest[1], rest[2:]
    outs, us, rest = rest[:fs], rest[fs : 2 * fs], rest[2 * fs :]
    act_ref, da_ref, dg_ref, wa, wg, wm, x, ct, made, made_u, w_sems, sems, out_sems = rest
    step = pl.program_id(0)
    half, side = p.rows // 2, at_ref[1] % 2
    pairs = []
    for o in range(fs):
        base = (at_ref[0] ^ o) * 2
        for part, at in ((near[o], base + side), (other[o], base + 1 - side)):
            at = pl.ds(pl.multiple_of(at * half, half), half)
            pairs.append((part.at[:half], wa.at[at, :]))
            pairs.append((part.at[half:], wg.at[at, :]))
    w_copies = copies(pairs, w_sems)
    pairs = []
    for o in range(fs):
        pairs += [(xs[o], x.at[o]), (cs[o], ct.at[o])]
    x_copies = copies(pairs, sems)
    pairs = []
    for o in range(fs):
        pairs += [(made.at[o], outs[o]), (made_u.at[o], us[o])]
    out_copies = copies(pairs, out_sems)

    @pl.when(step == 0)
    def _():
        for copy in x_copies[:1] + w_copies + x_copies[1:]:
            copy.start()
        if pad != units:
            wm[units:, :] = jnp.zeros((pad - units, p.width), bf16)
        wm[:units, :] = w_out[...]
        for copy in w_copies:
            copy.wait()

    for o in range(fs):

        @pl.when(step == o)
        def _(o=o):
            x_copies[2 * o].wait()
            x_copies[2 * o + 1].wait()

    act, gate = mm(x[step], wa[...]), mm(x[step], wg[...])
    phi = 0.5 * (1.0 + lax.erf(act * (2.0**-0.5)))
    gelu = act * phi
    active = (gelu * gate).astype(bf16)
    made[step] = mm(active, wm[...]).astype(bf16)
    grad = mm(ct[step], wm[...], NT)
    slope = phi + act * (jnp.exp(-0.5 * act * act) * 0.3989422804014327)
    da, dg = (grad * gate * slope).astype(bf16), (grad * gelu).astype(bf16)
    made_u[step] = (mm(da, wa[...], NT) + mm(dg, wg[...], NT)).astype(bf16)
    act_ref[...], da_ref[...], dg_ref[...] = active, da, dg
    for o in range(fs):

        @pl.when(step == o)
        def _(o=o):
            out_copies[2 * o].start()
            out_copies[2 * o + 1].start()

    @pl.when(step == fs - 1)
    def _():
        for copy in out_copies:
            copy.wait()


def mlp_sums_kernel(*refs, p):
    fs, units = p.fsdp, p.units
    xs, cs, rest = refs[:fs], refs[fs : 2 * fs], refs[2 * fs :]
    act_ref, da_ref, dg_ref, c_ref, one, two, sa, sg, sm, x, ct = rest
    step = pl.program_id(0)

    @pl.when(step == 0)
    def _():
        sa[...] = jnp.zeros_like(sa)
        sg[...] = jnp.zeros_like(sg)
        sm[...] = jnp.zeros_like(sm)

    for o in range(fs):

        @pl.when(step == o)
        def _(o=o):
            x[...] = xs[o][...]
            ct[...] = cs[o][...]

    rows = pl.ds(pl.multiple_of(step * p.own, p.own), p.own)
    sa[...] += mm(x[...], da_ref[rows, :], TN)
    sg[...] += mm(x[...], dg_ref[rows, :], TN)
    sm[...] += mm(ct[...], act_ref[rows, :], TN)

    @pl.when(step == fs - 1)
    def _():
        for cc in range(p.ctx):
            away = storage(c_ref[0] ^ cc, p.order)
            late = storage(c_ref[0] ^ cc, p.last_order)
            for ff in range(fs):
                at = slice(ff * p.rows + cc * p.small, ff * p.rows + (cc + 1) * p.small)
                one[away, ff, 0] = sa[at, :units].astype(bf16)
                one[away, ff, 1] = sm[at, :units].astype(bf16)
                two[late, ff] = sg[at, :units].astype(bf16)


def middle_kernel(*refs, p):
    g = p.pieces
    hidden, (a, b, c), (residual, unit) = refs[:g], refs[g : g + 3], refs[g + 3 :]
    for i, j, at in p.locations():
        rows = slice(at, at + p.span)
        total = a[rows].astype(f32) + b[rows].astype(f32) + c[rows].astype(f32)
        total = total + hidden[j][i, : p.span].astype(f32)
        residual[rows] = total
        unit[rows] = norm_stats(total)[0].astype(bf16)


def turn_kernel(a, b, c, residual, cot, grad, low, *, p):
    for _, _, at in p.locations():
        rows = slice(at, at + p.span)
        u = a[rows].astype(f32) + b[rows].astype(f32) + c[rows].astype(f32)
        unit, rate = norm_stats(residual[rows])
        total = cot[rows].astype(f32) + norm_back(u, unit, rate)
        grad[rows] = total
        low[rows] = total.astype(bf16)


def result_kernel(*refs, p):
    (a, b, residual), outs = refs[:3], refs[3:]
    for i, j, at in p.locations():
        rows = slice(at, at + p.span)
        total = a[rows].astype(f32) + b[rows].astype(f32)
        outs[j][i] = (total + residual[rows]).astype(bf16)


def last_kernel(*refs, p):
    g = p.pieces
    hidden, (a, b, c, grad), outs = refs[:g], refs[g : g + 4], refs[g + 4 :]
    for i, j, at in p.locations():
        rows = slice(at, at + p.span)
        u = a[rows].astype(f32) + b[rows].astype(f32) + c[rows].astype(f32)
        unit, rate = norm_stats(hidden[j][i, : p.span].astype(f32))
        outs[j][i] = (grad[rows] + norm_back(u, unit, rate)).astype(bf16)


def qkv_grad_kernel(*refs, p):
    stack, w, gain, c_ref, qkv, out, gain_grad = refs
    fs, small, slab, lanes = p.fsdp, p.small, p.slab, p.lanes
    for cc in range(p.ctx):
        away = storage(c_ref[0] ^ cc, p.last_order)
        rows = slice(cc * small, (cc + 1) * small)
        scale = gain[rows, :]
        total = jnp.zeros((small, lanes), f32)
        for g in range(p.groups):
            for ff in range(fs):
                for m in range(3):
                    at = (ff * 3 + m) * small
                    value = stack[away, g, at : at + small, :].astype(f32)
                    there = m * p.width + ff * p.cols + g * lanes
                    qkv[rows, there : there + lanes] = value * scale
                    total = total + value * w[rows, there : there + lanes].astype(f32)
            for d in range(p.width // lanes):
                at = 3 * fs * small + d * slab
                value = stack[away, g, at : at + slab, :].astype(f32)
                row = g * lanes + cc * slab
                out[row : row + slab, d * lanes : (d + 1) * lanes] = value
        gain_grad[rows, :] = jnp.sum(total, axis=1, keepdims=True)


def in_grad_kernel(table, low, high, w, gain, grad, gain_grad, *, top):
    def write(value):
        grad[...] = value * gain[...]
        gain_grad[...] = jnp.sum(value * w[...].astype(f32), axis=1, keepdims=True)

    step = pl.program_id(0)

    @pl.when(table[step] < top)
    def _():
        write(low[0].astype(f32))

    @pl.when(table[step] >= top)
    def _():
        write(high[0].astype(f32))


def out_grad_kernel(stack, c_ref, grad, *, p):
    for cc in range(p.ctx):
        away = storage(c_ref[0] ^ cc, p.order)
        for ff in range(p.fsdp):
            at = ff * p.rows + cc * p.small
            grad[:, at : at + p.small] = stack[away, ff].astype(f32).T


def on_device(
    hidden, segment_ids, cotangent, w_qkv, w_attn_out, w_in, w_mlp_out, gain_attn, gain_mlp
):
    fsdp, ctx = lax.axis_size("fsdp"), lax.axis_size("ctx")
    f, c = lax.axis_index("fsdp"), lax.axis_index("ctx")
    batch, span, width = hidden.shape
    p = Plan(fsdp, ctx, batch, span, width, w_mlp_out.shape[0], w_in.shape[0])
    n, own, cols, units, rows, small = p.n, p.own, p.cols, p.units, p.rows, p.small
    length, pieces = p.length, p.pieces
    both = ("ctx", "fsdp")
    slots = range(fsdp)
    tile = shape_of((own, width))
    bits = [fsdp >> 1 + b for b in range(fsdp.bit_length() - 1)]

    def mixed_bits(index):
        out = 0
        for bit in bits:
            out = out + index // (fsdp // 2 // bit) % 2 * bit
        return out

    def route(j):
        pairs = []
        for cc in range(ctx):
            for ff in range(fsdp):
                to_c = (cc + j) % pieces * fsdp + mixed_bits(ff)
                to_f = cc // pieces ^ ff % 2 * (fsdp // 2)
                pairs.append((cc * fsdp + ff, to_c * fsdp + to_f))
        return pairs

    def dealt(values):
        return [
            lax.dynamic_slice_in_dim(values, (c + j) % pieces * n, n, 0) for j in range(pieces)
        ]

    def deal(parts):
        return [lax.ppermute(part, both, route(j)) for j, part in enumerate(parts)]

    def undeal(parts):
        back = [
            lax.ppermute(part, both, [(b, a) for a, b in route(j)])
            for j, part in enumerate(parts)
        ]
        return back

    def assemble(back):
        if pieces == 1:
            return back[0]
        blocks = []
        for b in range(pieces):
            block = back[0]
            for j in range(1, pieces):
                block = jnp.where((c + j) % pieces == b, back[j], block)
            blocks.append(block)
        return jnp.concatenate(blocks, axis=0)

    def partner(values, bit):
        return lax.ppermute(values, "fsdp", [(i, i ^ bit) for i in range(fsdp)])

    def meet(*values):
        return lax.optimization_barrier(values)

    def first_hop(value):
        return [value, partner(value, bits[0])]

    def later_hops(held):
        held = {0: held[0], bits[0]: held[1]}
        for bit in bits[1:]:
            for o in list(held):
                held[o ^ bit] = partner(held[o], bit)
        return [held[o] for o in slots]

    def reduce(parts):
        held, side, last = dict(enumerate(parts)), None, None
        for bit in reversed(bits):
            for o in sorted(held, reverse=True):
                if not o & bit:
                    continue
                got, mine = partner(held.pop(o), bit), held[o ^ bit]
                if o == bits[0]:
                    last = got
                elif o == bits[1]:
                    side = got
                else:
                    held[o ^ bit] = (mine.astype(f32) + got.astype(f32)).astype(bf16)
        return held[0], side, last

    def away(values, bit):
        return lax.ppermute(values, "ctx", [(i, i ^ bit) for i in range(ctx)])

    def send(stack, bit):
        half = stack.shape[0] // 2
        return stack[:half], away(stack[half:], bit)

    def add(pair):
        return (pair[0].astype(f32) + pair[1].astype(f32)).astype(bf16)

    def grow(stack, bit):
        return stack, away(stack, bit)

    def join(pair):
        return jnp.concatenate(pair, axis=0)

    flip = c % fsdp // (fsdp // 2) * (fsdp // 2)
    blocks = [
        (f ^ o ^ flip) * pieces + (c // fsdp - j) % pieces for o in slots for j in range(pieces)
    ]
    positions = (jnp.stack(blocks)[:, None] * span + jnp.arange(span)[None, :]).reshape(length)
    turns = p.size // 2
    inverse = rope_base ** (-(jnp.arange(turns, dtype=f32) * 2.0 / p.size))
    angles = positions.astype(f32)[:, None] * inverse[None, :]
    cosine, sine = jnp.cos(angles), jnp.sin(angles)
    reps = p.table // p.size
    cosine = jnp.concatenate([cosine, cosine] * reps, axis=1)
    sine = jnp.concatenate([-sine, sine] * reps, axis=1)

    tags = jnp.pad(
        segment_ids.astype(bf16)[:, None, :], ((0, 0), (0, TAG - 1), (0, width - span))
    )
    hidden_cut, w_qkv, w_in = lax.optimization_barrier(
        (dealt(jnp.concatenate([hidden, tags], axis=1)), w_qkv, w_in)
    )
    hidden_parts = deal(hidden_cut)

    gain_a, gain_m = gain_attn.astype(f32)[:, None], gain_mlp.astype(f32)[:, None]
    here, place = jnp.reshape(c, (1,)), jnp.stack([f, c])
    half = rows // 2
    mine, other = call(
        functools.partial(cut_kernel, p=p, feed=False),
        "cut",
        [shape_of((fsdp, half, 3 * cols)), shape_of((2, half, 3 * cols))],
        1,
        [],
        [w_qkv, gain_a, place],
        1e6,
    )

    def spread_out(mine, other):
        near = [mine[0]] + [
            lax.ppermute(mine[o], "fsdp", [(i, i ^ o) for i in range(fsdp)]) for o in slots[1:]
        ]
        return near, [other[0], partner(other[1], 1)]

    near, other = spread_out(mine, other)
    hidden_parts, near, other, cosine, sine, cotangent, w_in = meet(
        hidden_parts, near, other, cosine, sine, cotangent, w_in
    )
    far = [away(part, 1) for part in near[2:]]
    cot_parts = deal(dealt(cotangent))
    unit1 = call(
        functools.partial(unit_kernel, p=p),
        "unit1",
        [shape_of((own + TAG, width))],
        1,
        [],
        hidden_parts,
        1e6,
    )[0]
    unit1, w_in_late = meet(unit1, w_in)
    mine_in, kept_in = call(
        functools.partial(cut_kernel, p=p, feed=True),
        "cut_in",
        [shape_of((fsdp, rows, p.padded)), shape_of((2, rows, p.padded))],
        1,
        [],
        [w_in_late, gain_m, place],
        1e6,
    )
    held, far, cot_parts, mine_in, kept_in = meet(
        first_hop(unit1), far, cot_parts, mine_in, kept_in
    )
    unit1_slots = later_hops(held)
    cot_own = jnp.stack(cot_parts, axis=1).reshape(own, width)
    unit1_slots, cot_own, mine_in, kept_in = meet(unit1_slots, cot_own, mine_in, kept_in)
    cot_held = first_hop(cot_own)
    near_in, other_in = spread_out(mine_in, kept_in)

    whole = shape_of((n, length, cols))
    q, k, v, segments, w_qkv_cols = call(
        functools.partial(project_kernel, p=p),
        "project",
        [whole] * 3 + [shape_of((n, 8, length), f32), shape_of((width, 3 * cols))],
        fsdp,
        [
            pltpu.VMEM((fsdp, own + TAG, width), bf16),
            pltpu.SemaphoreType.DMA((2 * fsdp,)),
            pltpu.SemaphoreType.DMA((fsdp,)),
        ],
        [Late(a) for a in unit1_slots + near + other + far] + [cosine, sine, place],
        4e9,
    )
    ranges = segments[:, 0].reshape(n, fsdp, p.part)
    spans = jnp.stack([jnp.min(ranges, axis=2), jnp.max(ranges, axis=2)], axis=2)
    spans = spans.astype(jnp.int32).reshape(2 * n * fsdp)
    made = call(
        functools.partial(attend_kernel, p=p),
        "attend",
        [tile] * fsdp + [whole, shape_of((n, 8, length), f32)],
        n * fsdp,
        [pltpu.VMEM((p.part, width), bf16)],
        [q, k, v, segments, w_attn_out],
        1.2e10,
    )
    made, cot_held, near_in, other_in = meet(made, cot_held, near_in, other_in)
    far_in = [away(part, 1) for part in near_in[2:]]
    cot_slots = later_hops(cot_held)
    attended_parts, attended, norms = made[:fsdp], made[fsdp], made[fsdp + 1]

    attended_parts = list(attended_parts)
    attended_parts[0], unit1_late = meet(attended_parts[0], unit1_slots)
    (flipped,) = call(
        functools.partial(flip_kernel, p=p),
        "flip",
        [shape_of((n, width, length))],
        fsdp,
        [],
        list(unit1_late),
        1e6,
    )
    addends = reduce(attended_parts)
    addends, flipped = meet(addends, flipped)
    residual, unit2 = call(
        functools.partial(middle_kernel, p=p),
        "middle",
        [shape_of((own, width), f32), tile],
        1,
        [],
        hidden_parts + list(addends),
        1e6,
    )
    unit2, far_in, cot_slots = meet(unit2, far_in, cot_slots)
    unit2_slots = later_hops(first_hop(unit2))

    wide = shape_of((fsdp * own, p.padded))
    made = call(
        functools.partial(mlp_kernel, p=p),
        "mlp",
        [Late(tile)] * (2 * fsdp)
        + [(wide, pl.BlockSpec((own, p.padded), lambda s: (s, 0)))] * 3,
        fsdp,
        [pltpu.VMEM((width, p.padded), bf16)] * 2
        + [pltpu.VMEM((p.padded, width), bf16)]
        + [pltpu.VMEM((fsdp, own, width), bf16)] * 4
        + [
            pltpu.SemaphoreType.DMA((4 * fsdp,)),
            pltpu.SemaphoreType.DMA((2 * fsdp,)),
            pltpu.SemaphoreType.DMA((2 * fsdp,)),
        ],
        [Late(a) for a in unit2_slots + cot_slots + near_in + other_in + far_in]
        + [w_mlp_out, place],
        1.2e10,
    )
    out_parts, u2_parts, (active, da, dg) = made[:fsdp], made[fsdp : 2 * fsdp], made[2 * fsdp :]

    u2 = reduce(u2_parts)
    mlp_sums, gate_sums = call(
        functools.partial(mlp_sums_kernel, p=p),
        "mlp_sums",
        [
            shape_of((ctx, fsdp, 2, small, units)),
            shape_of((ctx, fsdp, small, units)),
        ],
        fsdp,
        [pltpu.VMEM((width, p.padded), f32)] * 3 + [pltpu.VMEM((own, width), bf16)] * 2,
        unit2_slots + cot_slots + [active, da, dg, here],
        6e9,
    )
    u2, mlp_sums, gate_sums = lax.optimization_barrier((u2, mlp_sums, gate_sums))
    grad_residual, grad_low = call(
        functools.partial(turn_kernel, p=p),
        "turn",
        [shape_of((own, width), f32), tile],
        1,
        [],
        list(u2) + [residual, cot_own],
        1e6,
    )
    order = p.order
    gate_order = p.last_order
    piece = [shape_of((n, span, width))] * pieces
    grad_low, out_parts, mlp_sums, gate_sums = meet(
        grad_low, list(out_parts), mlp_sums, gate_sums
    )
    low_held = first_hop(grad_low)
    mlp_pair, gate_pair = send(mlp_sums, order[0]), send(gate_sums, gate_order[0])
    held = dict(enumerate(out_parts))
    for bit in reversed(bits[1:]):
        for o in sorted(held, reverse=True):
            if o & bit:
                held[o ^ bit] = add((held[o ^ bit], partner(held.pop(o), bit)))
    low_held, out_near, out_far, mlp_pair, gate_pair = meet(
        low_held, held[0], held[bits[0]], mlp_pair, gate_pair
    )
    mlp_sums, gate_sums = add(mlp_pair), add(gate_pair)
    low_slots = later_hops(low_held)
    low_slots, out_far, mlp_sums, gate_sums = meet(low_slots, out_far, mlp_sums, gate_sums)
    mlp_pair, gate_pair = send(mlp_sums, order[1]), send(gate_sums, gate_order[1])
    out_got = partner(out_far, bits[0])
    mixed, attention_sums = [], []
    for group in range(p.groups):
        some = pl.BlockSpec(
            (n, length, p.lanes),
            lambda s, group=group: (0, 0, group),
            pipeline_mode=pl.Buffered(1),
        )
        wo_rows = pl.BlockSpec(
            (p.lanes, width), lambda s, group=group: (group, 0), pipeline_mode=pl.Buffered(1)
        )
        grad_mixed, sums = call(
            functools.partial(backward_kernel, p=p, group=group),
            "attention_back",
            [
                shape_of((n, length, 3 * p.lanes)),
                shape_of((ctx, 4 * fsdp * small, p.lanes)),
            ],
            n * fsdp + 1,
            [
                pltpu.VMEM((p.lanes, length), bf16),
                pltpu.VMEM((p.lanes, p.part), f32),
                pltpu.VMEM((length, p.lanes), f32),
                pltpu.VMEM((length, p.lanes), f32),
                pltpu.VMEM((n, length, width), bf16),
                pltpu.VMEM((length, 1), f32),
                pltpu.VMEM((width, 3 * p.lanes), f32),
                pltpu.VMEM((p.lanes, width), f32),
                pltpu.VMEM((n, width, length), bf16),
                pltpu.SemaphoreType.DMA((n * fsdp,)),
                pltpu.SemaphoreType.DMA((1,)),
            ],
            [Late(a) for a in low_slots]
            + [Late(flipped), (w_attn_out, wo_rows), (q, some), (k, some), (v, some), (attended, some)]
            + [segments, norms, cosine, sine, here, spans],
            1.5e10,
        )
        mixed.append(grad_mixed)
        if group == 0:
            sums, low_slots, mlp_pair, gate_pair, out_got = meet(
                sums, low_slots, mlp_pair, gate_pair, out_got
            )
            pairs = [send(sums, order[0])]
            mlp_sums, gate_sums = add(mlp_pair), add(gate_pair)
            for bit, gate_bit in zip(order[2:-1], gate_order[2:-1]):
                mlp_sums, gate_sums = add(send(mlp_sums, bit)), add(send(gate_sums, gate_bit))
            mlp_pair, gate_pair = send(mlp_sums, order[-1]), send(gate_sums, gate_order[-1])
            result_parts = call(
                functools.partial(result_kernel, p=p),
                "result",
                piece,
                1,
                [],
                [out_near, out_got, residual],
                1e6,
            )
            low_slots, result_parts = meet(low_slots, result_parts)
            out_back = undeal(result_parts)
        else:
            sums, pairs, mlp_pair, gate_pair = meet(sums, pairs, mlp_pair, gate_pair)
            pairs = pairs + [send(sums, order[0])]

    def step_of(sums):
        return order[ctx.bit_length() - sums.shape[0].bit_length()]

    back_order = order[::-1]
    mlp_sums, gate_sums = add(mlp_pair)[0], add(gate_pair)[0]
    mlp_stack = grow(mlp_sums[None, :, 1], back_order[0])
    in_small = jnp.stack([mlp_sums[:, 0], gate_sums], axis=1)
    early, late = pairs[:-1], pairs[-1]
    if early:
        sums = add(early[0])
        early = [send(sums, step_of(sums))]
    u1_parts = call(
        functools.partial(spread_kernel, p=p),
        "spread",
        [tile] * fsdp,
        fsdp,
        [pltpu.VMEM((own, width), bf16)],
        mixed + [w_qkv_cols],
        2e9,
    )
    in_small = lax.all_to_all(in_small, "fsdp", 0, 0, tiled=True)
    in_small = in_small.transpose(2, 1, 0, 3).reshape(1, small, 2 * fsdp * units)
    u1_parts, early, late, mlp_stack, in_small = meet(
        list(u1_parts), early, late, mlp_stack, in_small
    )
    in_pair = grow(in_small, back_order[0])
    u1 = reduce(u1_parts)
    if early:
        sums = add(early[0])
        early = [send(sums, step_of(sums))]
    sums = add(late)
    late = send(sums, step_of(sums))
    mlp_stack = grow(join(mlp_stack), back_order[1])
    u1, early, late, mlp_stack, out_back = meet(u1, early, late, mlp_stack, out_back)
    back_parts = call(
        functools.partial(last_kernel, p=p),
        "last",
        piece,
        1,
        [],
        hidden_parts + list(u1) + [grad_residual],
        1e6,
    )
    sums = add(late)
    late = send(sums, step_of(sums))
    mlp_stack = grow(join(mlp_stack), back_order[2])
    back_parts, late, in_pair = meet(back_parts, late, in_pair)
    back = undeal(back_parts)
    in_pair = grow(join(in_pair), back_order[1])

    def finished(pair):
        sums = add(pair)
        while sums.shape[0] > 1:
            sums = add(send(sums, step_of(sums)))
        return sums

    sums = jnp.concatenate([finished(pair) for pair in early + [late]], axis=0)
    mine = sums[:, : 3 * fsdp * small].reshape(p.groups, fsdp, 3 * small, p.lanes)
    mine = lax.all_to_all(mine, "fsdp", 1, 1, tiled=True)
    mine = mine.reshape(p.groups, 3 * fsdp * small, p.lanes)
    stack = jnp.concatenate([mine, sums[:, 3 * fsdp * small :]], axis=1)[None]
    last_back = p.last_order[::-1]
    stack = grow(stack, last_back[0])
    for bit in back_order[3:]:
        mlp_stack = grow(join(mlp_stack), bit)
    stack, in_pair, mlp_stack = meet(stack, in_pair, mlp_stack)
    mlp_stack = join(mlp_stack)
    stack = grow(join(stack), last_back[1])
    for bit in back_order[2:]:
        in_pair = grow(join(in_pair), bit)
    stack, back, mlp_stack = meet(stack, back, mlp_stack)
    for bit in last_back[2:]:
        stack = grow(join(stack), bit)
    stack = join(stack)
    out, back = assemble(out_back), assemble(back).astype(f32)

    grad_qkv, grad_out, grad_gain_a = call(
        functools.partial(qkv_grad_kernel, p=p),
        "qkv_grad",
        [
            shape_of((rows, 3 * width), f32),
            shape_of((cols, width), f32),
            shape_of((rows, 1), f32),
        ],
        1,
        [],
        [stack, w_qkv, gain_a, here],
        1e6,
    )
    table = storage(c ^ jnp.arange(ctx, dtype=jnp.int32), order)
    low_part, high_part, block = in_pair[0], in_pair[1], small
    if small % 8:
        low_part = join(in_pair)
        parts = [
            lax.dynamic_slice_in_dim(low_part, storage(c ^ cc, order), 1, 0) for cc in range(ctx)
        ]
        low_part = jnp.concatenate(parts, axis=1)
        high_part, block, table = low_part, rows, jnp.zeros((1,), jnp.int32)
    top = low_part.shape[0]
    some = pl.BlockSpec((block, 2 * fsdp * units), lambda s, t: (s, 0))
    thin = pl.BlockSpec((block, 1), lambda s, t: (s, 0))
    one = (1, block, 2 * fsdp * units)
    grad_in, grad_gain_m = pl.pallas_call(
        functools.partial(in_grad_kernel, top=top),
        grid_spec=pltpu.PrefetchScalarGridSpec(
            num_scalar_prefetch=1,
            grid=(rows // block,),
            in_specs=[
                pl.BlockSpec(one, lambda s, t: (jnp.minimum(t[s], top - 1), 0, 0)),
                pl.BlockSpec(one, lambda s, t: (jnp.maximum(t[s] - top, 0), 0, 0)),
                some,
                thin,
            ],
            out_specs=[some, thin],
        ),
        out_shape=[shape_of(w_in.shape, f32), shape_of((rows, 1), f32)],
        compiler_params=pltpu.CompilerParams(vmem_limit_bytes=40 << 20),
        cost_estimate=pl.CostEstimate(
            flops=1000000, bytes_accessed=8 * w_in.size, transcendentals=0
        ),
        name="in_grad",
    )(table, low_part, high_part, w_in, gain_m)
    (grad_mlp_out,) = call(
        functools.partial(out_grad_kernel, p=p),
        "out_grad",
        [shape_of((units, width), f32)],
        1,
        [],
        [mlp_stack, here],
        1e6,
    )
    return (
        out,
        back,
        grad_qkv,
        grad_out,
        grad_in,
        grad_mlp_out,
        grad_gain_a.reshape(rows),
        grad_gain_m.reshape(rows),
    )


def solution(mesh):
    in_specs = (
        P("fsdp", "ctx", None),
        P("fsdp", "ctx"),
        P("fsdp", "ctx", None),
        P("fsdp", None),
        P("fsdp", None),
        P("fsdp", None),
        P("fsdp", None),
        P("fsdp"),
        P("fsdp"),
    )
    out_specs = (
        P("fsdp", "ctx", None),
        P("fsdp", "ctx", None),
        P("fsdp", None),
        P("fsdp", None),
        P("fsdp", None),
        P("fsdp", None),
        P("fsdp"),
        P("fsdp"),
    )
    return jax.shard_map(
        on_device, mesh=mesh, in_specs=in_specs, out_specs=out_specs, check_vma=False
    )
```

```python
import functools

import jax
import jax.numpy as jnp
from jax import lax
from jax.experimental import pallas as pl
from jax.experimental.pallas import tpu as pltpu
from jax.sharding import PartitionSpec as P

HEADS = 16
rope_base = 160000.0
norm_eps = 1e-05
masked_score = -1e30
bf16 = jnp.bfloat16
f32 = jnp.float32
NT = (((1,), (1,)), ((), ()))
NN = (((1,), (0,)), ((), ()))
TN = (((0,), (0,)), ((), ()))
TAG = 16


def mm(a, b, dims=NN):
    return lax.dot_general(a, b, dims, preferred_element_type=f32)


class Late:
    def __init__(self, value):
        self.value = self.shape_is = value


def copies(pairs, sems):
    return [pltpu.make_async_copy(a, b, sems.at[k]) for k, (a, b) in enumerate(pairs)]


def call(kernel, name, out_shape, grid, scratch, args, flops, limit=56):
    def spec(a):
        if isinstance(a, tuple):
            return a[1]
        if isinstance(a, Late):
            return pl.BlockSpec(memory_space=pl.ANY)
        if a.dtype == jnp.int32:
            return pl.BlockSpec(memory_space=pltpu.SMEM)
        return pl.BlockSpec(
            a.shape, lambda s, nd=len(a.shape): (0,) * nd, pipeline_mode=pl.Buffered(1)
        )

    specs = [spec(a) for a in args]
    args = [a[0] if isinstance(a, tuple) else getattr(a, "value", a) for a in args]
    outs = [spec(a) for a in out_shape]
    out_shape = [a[0] if isinstance(a, tuple) else getattr(a, "shape_is", a) for a in out_shape]
    moved = sum(a.size * a.dtype.itemsize for a in args)
    moved += sum(a.size * a.dtype.itemsize for a in out_shape)
    return pl.pallas_call(
        kernel,
        grid=(grid,),
        in_specs=specs,
        out_specs=outs,
        out_shape=out_shape,
        scratch_shapes=scratch,
        compiler_params=pltpu.CompilerParams(vmem_limit_bytes=limit << 20),
        cost_estimate=pl.CostEstimate(
            flops=int(flops), bytes_accessed=int(moved), transcendentals=0
        ),
        name=name,
    )(*args)


def shape_of(shape, dtype=bf16):
    return jax.ShapeDtypeStruct(shape, dtype)


def head_mask(shape, head, size):
    return lax.broadcasted_iota(jnp.int32, shape, 1) // size == head


def swap(values, size):
    width, half = values.shape[1], size // 2
    if width == size:
        return jnp.concatenate([values[:, half:], values[:, :half]], axis=1)
    lane = lax.broadcasted_iota(jnp.int32, values.shape, 1) % size
    return jnp.where(
        lane < half, pltpu.roll(values, width - half, 1), pltpu.roll(values, half, 1)
    )


def norm_stats(values):
    center = values - jnp.mean(values, axis=-1, keepdims=True)
    rate = lax.rsqrt(jnp.mean(center * center, axis=-1, keepdims=True) + norm_eps)
    return center * rate, rate


def norm_back(grad, unit, rate):
    return rate * (
        grad
        - jnp.mean(grad, axis=-1, keepdims=True)
        - unit * jnp.mean(grad * unit, axis=-1, keepdims=True)
    )


class Plan:
    def __init__(self, fsdp, ctx, batch, span, width, units, rows):
        self.fsdp, self.ctx, self.span, self.width = fsdp, ctx, span, width
        self.pieces = ctx // fsdp
        self.n = batch // self.pieces
        self.part = self.pieces * span
        self.own = self.n * self.part
        self.length = span * ctx
        self.heads = HEADS // fsdp
        self.size = width // HEADS
        self.cols = self.heads * self.size
        self.units, self.rows = units, rows
        self.padded = -(-units // 256) * 256
        self.small = rows // ctx
        self.groups = 2 if self.heads % 2 == 0 else 1
        self.lanes = self.cols // self.groups
        self.slab = self.lanes // ctx
        self.table = min(128, self.cols)
        bits = [1 << b for b in range(ctx.bit_length() - 1)]
        self.order = bits
        self.last_order = bits[1:] + bits[:1]

    def locations(self):
        return [
            (i, j, (i * self.pieces + j) * self.span)
            for i in range(self.n)
            for j in range(self.pieces)
        ]


def storage(x, order):
    at = 0
    for bit in order:
        at = at * 2 + x // bit % 2
    return at


def cut_kernel(w, gain, at_ref, mine, other, *, p, feed):
    half, here = p.rows // 2, at_ref[0]
    side = at_ref[1] % 2
    near = pl.ds(pl.multiple_of(side * half, half), half)
    far = pl.ds(pl.multiple_of((1 - side) * half, half), half)
    size = p.units if feed else p.cols
    if feed and p.padded != size:
        mine[:, :, size:] = jnp.zeros((p.fsdp, 2 * half, p.padded - size), bf16)
        other[:, :, size:] = jnp.zeros((2, 2 * half, p.padded - size), bf16)
    for t in range(p.fsdp):
        o = t ^ here
        for m in range(2 if feed else 3):
            at = (m * p.fsdp + t) * size
            if feed:
                there = slice(m * half, (m + 1) * half), slice(0, size)
            else:
                there = slice(None), slice(m * size, (m + 1) * size)
            value = w[near, at : at + size].astype(f32) * gain[near, :]
            mine[(o,) + there] = value.astype(bf16)

            @pl.when(o < 2)
            def _(at=at, there=there, o=o):
                value = w[far, at : at + size].astype(f32) * gain[far, :]
                other[(o,) + there] = value.astype(bf16)


def unit_kernel(*refs, p):
    pieces, unit = refs[:-1], refs[-1]
    unit[p.own :, :] = jnp.zeros((TAG, p.width), bf16)
    for i, j, at in p.locations():
        ref = pieces[j]
        value, _ = norm_stats(ref[i, : p.span].astype(f32))
        unit[at : at + p.span] = value.astype(bf16)
        unit[p.own :, at : at + p.span] = ref[i, p.span :, : p.span]


def project_kernel(*refs, p):
    fs, gs = p.fsdp, p.part
    xs, rest = refs[:fs], refs[fs:]
    near, other, rest = rest[:fs], rest[fs : 2 * fs], rest[2 * fs :]
    cos, sin, at_ref, q_ref, k_ref, v_ref, seg_ref, w, x, w_sems, x_sems = rest
    step = pl.program_id(0)
    scale = p.size**-0.5
    half, side = p.rows // 2, at_ref[1] % 2
    pairs = []
    for o in range(fs):
        base = (at_ref[0] ^ o) * 2
        for part, at in ((near[o], base + side), (other[o], base + 1 - side)):
            pairs.append((part, w.at[pl.ds(pl.multiple_of(at * half, half), half), :]))
    w_copies = copies(pairs, w_sems)
    x_copies = copies([(xs[o], x.at[o]) for o in range(fs)], x_sems)

    @pl.when(step == 0)
    def _():
        for copy in x_copies[:1] + w_copies + x_copies[1:]:
            copy.start()
        for copy in w_copies:
            copy.wait()

    for o in range(fs):

        @pl.when(step == o)
        def _(o=o):
            x_copies[o].wait()
            for i in range(p.n):
                tag = x[o, p.own : p.own + TAG, i * gs : (i + 1) * gs].astype(f32)
                seg_ref[i, :, o * gs : (o + 1) * gs] = tag[:8]

    mixed = mm(x[step, : p.own], w[...])
    rows = pl.ds(pl.multiple_of(step * gs, gs), gs)
    reps = p.cols // p.table
    cosine = jnp.concatenate([cos[rows, :]] * reps, axis=1)
    sine = jnp.concatenate([sin[rows, :]] * reps, axis=1)
    for i in range(p.n):
        own = mixed[i * gs : (i + 1) * gs]
        query, key = own[:, : p.cols], own[:, p.cols : 2 * p.cols]
        query = (query * cosine + swap(query, p.size) * sine) * scale
        q_ref[i, rows, :] = query.astype(bf16)
        k_ref[i, rows, :] = (key * cosine + swap(key, p.size) * sine).astype(bf16)
        v_ref[i, rows, :] = own[:, 2 * p.cols :].astype(bf16)


def attend_kernel(q_ref, k_ref, v_ref, seg_ref, wo, *rest, p):
    fs, gs = p.fsdp, p.part
    parts, (att_ref, norm_ref, made) = rest[:fs], rest[fs:]
    step = pl.program_id(0)
    i, o = step // fs, step % fs
    rows = pl.ds(pl.multiple_of(o * gs, gs), gs)
    q, k, v = q_ref[i, rows, :], k_ref[i], v_ref[i]
    allowed = seg_ref[i, :, rows].T[:, :1] == seg_ref[i, :1, :]
    attended = jnp.zeros(q.shape, f32)
    norms = jnp.zeros((gs, 128), f32)
    lane = lax.broadcasted_iota(jnp.int32, norms.shape, 1)
    for head in range(p.heads):
        here = head_mask(q.shape, head, p.size)
        scores = mm(jnp.where(here, q, jnp.zeros_like(q)), k, NT)
        scores = jnp.where(allowed, scores, masked_score)
        peak = jnp.max(scores, axis=1, keepdims=True)
        weights = jnp.exp(scores - peak)
        total = jnp.sum(weights, axis=1, keepdims=True)
        attended = jnp.where(here, mm(weights.astype(bf16), v) / total, attended)
        norms = jnp.where(lane == head, peak + jnp.log(total), norms)
    norm_ref[i, :, rows] = norms.T[:8]
    attended = attended.astype(bf16)
    att_ref[i, rows, :] = attended
    made[...] = mm(attended, wo[...]).astype(bf16)
    for oo in range(fs):

        @pl.when(o == oo)
        def _(oo=oo):
            parts[oo][pl.ds(pl.multiple_of(i * gs, gs), gs), :] = made[...]


def flip_kernel(*refs, p):
    xs, out = refs[:-1], refs[-1]
    gs = p.part
    for o in range(p.fsdp):

        @pl.when(pl.program_id(0) == o)
        def _(o=o):
            for i in range(p.n):
                out[i, :, o * gs : (o + 1) * gs] = xs[o][i * gs : (i + 1) * gs, :].T


def shares(span_ref, i, a, b, fs):
    one, two = (i * fs + a) * 2, (i * fs + b) * 2
    return jnp.logical_and(
        span_ref[one] <= span_ref[two + 1], span_ref[two] <= span_ref[one + 1]
    )


def backward_kernel(*refs, p, group):
    fs, gs, cols = p.fsdp, p.part, p.lanes
    gls, rest = refs[:fs], refs[fs:]
    xt, wo, rest = rest[0], rest[1], rest[2:]
    q_ref, k_ref, v_ref, att_ref, seg_ref, norm_ref, cos, sin, c_ref, span_ref = rest[:10]
    gm, sums, kt, dqt, dk, dv, gl, seg_col, sum_qkv, sum_out, flat, sems, flat_sem = rest[10:]
    step = pl.program_id(0)
    scale = p.size**-0.5
    reps = cols // p.table

    def turned(grad, rows):
        cosine = jnp.concatenate([cos[rows, :]] * reps, axis=1)
        sine = jnp.concatenate([sin[rows, :]] * reps, axis=1)
        return grad * cosine - swap(grad, p.size) * sine

    pairs = [
        (gls[o].at[i * gs : (i + 1) * gs], gl.at[i, o * gs : (o + 1) * gs])
        for i in range(p.n)
        for o in range(fs)
    ]
    low_copies = copies(pairs, sems)
    flat_copy = pltpu.make_async_copy(xt, flat, flat_sem.at[0])

    @pl.when(step == 0)
    def _():
        for copy in low_copies:
            copy.start()
        flat_copy.start()

    @pl.when(step < p.n * fs)
    def _():
        i, o = step // fs, step % fs
        rows = pl.ds(pl.multiple_of(o * gs, gs), gs)
        for k in range(p.n * fs):

            @pl.when(step == k)
            def _(k=k):
                low_copies[k].wait()

        q = q_ref[i, rows, :]

        @pl.when(o == 0)
        def _():
            kt[...] = k_ref[i].T
            dk[...] = jnp.zeros_like(dk)
            dv[...] = jnp.zeros_like(dv)
            seg_col[...] = seg_ref[i].T[:, :1]

        attended = att_ref[i, rows, :]
        g = mm(gl[i, rows, :], wo[...], NT).astype(bf16)
        count = p.heads // p.groups
        picks = lax.broadcasted_iota(jnp.int32, (8, cols), 0)
        picks = (lax.broadcasted_iota(jnp.int32, (8, cols), 1) // p.size == picks).astype(f32)
        deltas = lax.dot_general(
            picks,
            g.astype(f32) * attended.astype(f32),
            NT,
            precision=lax.Precision.HIGHEST,
            preferred_element_type=f32,
        )
        zero = jnp.zeros_like(q)
        masks = [head_mask(q.shape, h, p.size) for h in range(count)]
        own_q = [jnp.where(mask, q, zero) for mask in masks]
        own_g = [jnp.where(mask, g, zero) for mask in masks]
        mine = seg_ref[i, :1, rows]
        dqt[...] = jnp.zeros_like(dqt)
        for kk in range(fs):
            keys = slice(kk * gs, (kk + 1) * gs)

            @pl.when(shares(span_ref, i, o, kk, fs))
            def _(keys=keys):
                k, v = k_ref[i, keys, :], v_ref[i, keys, :]
                allowed = seg_col[keys, :] == mine
                for h in range(count):
                    first = group * count + h
                    scores = jnp.where(allowed, mm(k, own_q[h], NT), masked_score)
                    probs = jnp.exp(scores - norm_ref[i, first : first + 1, rows])
                    grad = mm(v, own_g[h], NT)
                    grad = (probs * (grad - deltas[h : h + 1, :])).astype(bf16)
                    dv[keys, :] += mm(probs.astype(bf16), own_g[h])
                    dk[keys, :] += mm(grad, own_q[h])
                    at = slice(h * p.size, (h + 1) * p.size)
                    dqt[at, :] += mm(kt[at, keys], grad)

        gm[i, rows, :cols] = (turned(dqt[...].T, rows) * scale).astype(bf16)

        @pl.when(o == fs - 1)
        def _():
            gm[i, :, cols : 2 * cols] = turned(dk[...], slice(None)).astype(bf16)
            gm[i, :, 2 * cols :] = dv[...].astype(bf16)

    @pl.when(step == p.n * fs)
    def _():
        flat_copy.wait()
        total = [mm(flat[i], gm[i]) for i in range(p.n)]
        sum_qkv[...] = sum(total[1:], total[0])
        total = [mm(att_ref[i].T, gl[i]) for i in range(p.n)]
        sum_out[...] = sum(total[1:], total[0])
        small, slab = p.small, p.slab
        for cc in range(p.ctx):
            away = storage(c_ref[0] ^ cc, p.order)
            for ff in range(fs):
                for m in range(3):
                    part = sum_qkv[
                        ff * p.rows + cc * small : ff * p.rows + (cc + 1) * small,
                        m * cols : (m + 1) * cols,
                    ]
                    at = (ff * 3 + m) * small
                    sums[away, at : at + small, :] = part.astype(bf16)
            for d in range(p.width // cols):
                part = sum_out[cc * slab : (cc + 1) * slab, d * cols : (d + 1) * cols]
                at = 3 * fs * small + d * slab
                sums[away, at : at + slab, :] = part.astype(bf16)


def spread_kernel(*refs, p):
    gms, w, parts, made = refs[: p.groups], refs[p.groups], refs[p.groups + 1 : -1], refs[-1]
    o, lanes = pl.program_id(0), p.lanes
    rows = pl.ds(pl.multiple_of(o * p.part, p.part), p.part)
    for i in range(p.n):
        grad = jnp.concatenate(
            [gm[i, rows, m * lanes : (m + 1) * lanes] for m in range(3) for gm in gms], axis=1
        )
        made[i * p.part : (i + 1) * p.part] = mm(grad, w[...], NT).astype(bf16)
    for oo in range(p.fsdp):

        @pl.when(o == oo)
        def _(oo=oo):
            parts[oo][...] = made[...]


def mlp_kernel(*refs, p):
    fs, units, pad = p.fsdp, p.units, p.padded
    xs, cs, rest = refs[:fs], refs[fs : 2 * fs], refs[2 * fs :]
    near, other, rest = rest[:fs], rest[fs : 2 * fs], rest[2 * fs :]
    w_out, at_ref, rest = rest[0], rest[1], rest[2:]
    outs, us, rest = rest[:fs], rest[fs : 2 * fs], rest[2 * fs :]
    act_ref, da_ref, dg_ref, wa, wg, wm, x, ct, made, made_u, w_sems, sems, out_sems = rest
    step = pl.program_id(0)
    half, side = p.rows // 2, at_ref[1] % 2
    pairs = []
    for o in range(fs):
        base = (at_ref[0] ^ o) * 2
        for part, at in ((near[o], base + side), (other[o], base + 1 - side)):
            at = pl.ds(pl.multiple_of(at * half, half), half)
            pairs.append((part.at[:half], wa.at[at, :]))
            pairs.append((part.at[half:], wg.at[at, :]))
    w_copies = copies(pairs, w_sems)
    pairs = []
    for o in range(fs):
        pairs += [(xs[o], x.at[o]), (cs[o], ct.at[o])]
    x_copies = copies(pairs, sems)
    pairs = []
    for o in range(fs):
        pairs += [(made.at[o], outs[o]), (made_u.at[o], us[o])]
    out_copies = copies(pairs, out_sems)

    @pl.when(step == 0)
    def _():
        for copy in x_copies[:1] + w_copies + x_copies[1:]:
            copy.start()
        if pad != units:
            wm[units:, :] = jnp.zeros((pad - units, p.width), bf16)
        wm[:units, :] = w_out[...]
        for copy in w_copies:
            copy.wait()

    for o in range(fs):

        @pl.when(step == o)
        def _(o=o):
            x_copies[2 * o].wait()
            x_copies[2 * o + 1].wait()

    act, gate = mm(x[step], wa[...]), mm(x[step], wg[...])
    phi = 0.5 * (1.0 + lax.erf(act * (2.0**-0.5)))
    gelu = act * phi
    active = (gelu * gate).astype(bf16)
    made[step] = mm(active, wm[...]).astype(bf16)
    grad = mm(ct[step], wm[...], NT)
    slope = phi + act * (jnp.exp(-0.5 * act * act) * 0.3989422804014327)
    da, dg = (grad * gate * slope).astype(bf16), (grad * gelu).astype(bf16)
    made_u[step] = (mm(da, wa[...], NT) + mm(dg, wg[...], NT)).astype(bf16)
    act_ref[...], da_ref[...], dg_ref[...] = active, da, dg
    for o in range(fs):

        @pl.when(step == o)
        def _(o=o):
            out_copies[2 * o].start()
            out_copies[2 * o + 1].start()

    @pl.when(step == fs - 1)
    def _():
        for copy in out_copies:
            copy.wait()


def mlp_sums_kernel(*refs, p):
    fs, units = p.fsdp, p.units
    xs, cs, rest = refs[:fs], refs[fs : 2 * fs], refs[2 * fs :]
    act_ref, da_ref, dg_ref, c_ref, one, two, three, sa, sg, sm, x, ct = rest
    step = pl.program_id(0)

    @pl.when(step == 0)
    def _():
        sa[...] = jnp.zeros_like(sa)
        sg[...] = jnp.zeros_like(sg)
        sm[...] = jnp.zeros_like(sm)

    for o in range(fs):

        @pl.when(step == o)
        def _(o=o):
            x[...] = xs[o][...]
            ct[...] = cs[o][...]

    rows = pl.ds(pl.multiple_of(step * p.own, p.own), p.own)
    sa[...] += mm(x[...], da_ref[rows, :], TN)
    sg[...] += mm(x[...], dg_ref[rows, :], TN)
    sm[...] += mm(ct[...], act_ref[rows, :], TN)

    @pl.when(step == fs - 1)
    def _():
        for cc in range(p.ctx):
            away = storage(c_ref[0] ^ cc, p.order)
            late = storage(c_ref[0] ^ cc, p.last_order)
            for ff in range(fs):
                at = slice(ff * p.rows + cc * p.small, ff * p.rows + (cc + 1) * p.small)
                one[away, ff] = sa[at, :units].astype(bf16)
                two[late, ff] = sg[at, :units].astype(bf16)
                three[away, ff] = sm[at, :units].astype(bf16)


def middle_kernel(*refs, p):
    g = p.pieces
    hidden, (a, b, c), (residual, unit) = refs[:g], refs[g : g + 3], refs[g + 3 :]
    for i, j, at in p.locations():
        rows = slice(at, at + p.span)
        total = a[rows].astype(f32) + b[rows].astype(f32) + c[rows].astype(f32)
        total = total + hidden[j][i, : p.span].astype(f32)
        residual[rows] = total
        unit[rows] = norm_stats(total)[0].astype(bf16)


def turn_kernel(a, b, c, residual, cot, grad, low, *, p):
    for _, _, at in p.locations():
        rows = slice(at, at + p.span)
        u = a[rows].astype(f32) + b[rows].astype(f32) + c[rows].astype(f32)
        unit, rate = norm_stats(residual[rows])
        total = cot[rows].astype(f32) + norm_back(u, unit, rate)
        grad[rows] = total
        low[rows] = total.astype(bf16)


def result_kernel(*refs, p):
    (a, b, residual), outs = refs[:3], refs[3:]
    for i, j, at in p.locations():
        rows = slice(at, at + p.span)
        total = a[rows].astype(f32) + b[rows].astype(f32)
        outs[j][i] = (total + residual[rows]).astype(bf16)


def last_kernel(*refs, p):
    g = p.pieces
    hidden, (a, b, c, grad), outs = refs[:g], refs[g : g + 4], refs[g + 4 :]
    for i, j, at in p.locations():
        rows = slice(at, at + p.span)
        u = a[rows].astype(f32) + b[rows].astype(f32) + c[rows].astype(f32)
        unit, rate = norm_stats(hidden[j][i, : p.span].astype(f32))
        outs[j][i] = (grad[rows] + norm_back(u, unit, rate)).astype(bf16)


def row_sums(values):
    ones = jnp.ones((8, values.shape[1]), f32)
    total = lax.dot_general(
        ones, values, NT, precision=lax.Precision.HIGHEST, preferred_element_type=f32
    )
    return total[:1]


def qkv_grad_kernel(low, high, w, gain, c_ref, qkv, out, gain_grad, stack, sems, *, p):
    fs, small, slab, lanes = p.fsdp, p.small, p.slab, p.lanes
    top = low.shape[0]
    loads = copies([(low, stack.at[:top]), (high, stack.at[top:])], sems)
    for load in loads:
        load.start()
    for load in loads:
        load.wait()
    for cc in range(p.ctx):
        away = storage(c_ref[0] ^ cc, p.last_order)
        rows = slice(cc * small, (cc + 1) * small)
        scale = gain[rows, :]
        total = jnp.zeros((small, lanes), f32)
        for g in range(p.groups):
            for ff in range(fs):
                for m in range(3):
                    at = (ff * 3 + m) * small
                    value = stack[away, g, at : at + small, :].astype(f32)
                    there = m * p.width + ff * p.cols + g * lanes
                    qkv[rows, there : there + lanes] = value * scale
                    total = total + value * w[rows, there : there + lanes].astype(f32)
            for d in range(p.width // lanes):
                at = 3 * fs * small + d * slab
                value = stack[away, g, at : at + slab, :].astype(f32)
                row = g * lanes + cc * slab
                out[row : row + slab, d * lanes : (d + 1) * lanes] = value
        gain_grad[:, rows] = row_sums(total)


def in_grad_kernel(table, sums, w, gain, *rest):
    grad, gain_grad = rest[-2:]
    value = sums[0].astype(f32)
    grad[...] = value * gain[...]
    total = jnp.zeros((value.shape[0], 128), f32)
    for at in range(0, value.shape[1], 128):
        total = total + value[:, at : at + 128] * w[:, at : at + 128].astype(f32)
    gain_grad[0] = row_sums(total)


def out_grad_kernel(stack, c_ref, grad, *, p):
    for cc in range(p.ctx):
        away = storage(c_ref[0] ^ cc, p.order)
        for ff in range(p.fsdp):
            at = ff * p.rows + cc * p.small
            grad[:, at : at + p.small] = stack[away, ff].astype(f32).T


def on_device(
    hidden, segment_ids, cotangent, w_qkv, w_attn_out, w_in, w_mlp_out, gain_attn, gain_mlp
):
    fsdp, ctx = lax.axis_size("fsdp"), lax.axis_size("ctx")
    f, c = lax.axis_index("fsdp"), lax.axis_index("ctx")
    batch, span, width = hidden.shape
    p = Plan(fsdp, ctx, batch, span, width, w_mlp_out.shape[0], w_in.shape[0])
    n, own, cols, units, rows, small = p.n, p.own, p.cols, p.units, p.rows, p.small
    length, pieces = p.length, p.pieces
    both = ("ctx", "fsdp")
    slots = range(fsdp)
    tile = shape_of((own, width))
    bits = [fsdp >> 1 + b for b in range(fsdp.bit_length() - 1)]

    def mixed_bits(index):
        out = 0
        for bit in bits:
            out = out + index // (fsdp // 2 // bit) % 2 * bit
        return out

    def route(j):
        pairs = []
        for cc in range(ctx):
            for ff in range(fsdp):
                to_c = (cc + j) % pieces * fsdp + mixed_bits(ff)
                to_f = cc // pieces ^ ff % 2 * (fsdp // 2)
                pairs.append((cc * fsdp + ff, to_c * fsdp + to_f))
        return pairs

    def dealt(values):
        return [
            lax.dynamic_slice_in_dim(values, (c + j) % pieces * n, n, 0) for j in range(pieces)
        ]

    def deal(parts):
        return [lax.ppermute(part, both, route(j)) for j, part in enumerate(parts)]

    def undeal(parts):
        back = [
            lax.ppermute(part, both, [(b, a) for a, b in route(j)])
            for j, part in enumerate(parts)
        ]
        return back

    def assemble(back):
        if pieces == 1:
            return back[0]
        blocks = []
        for b in range(pieces):
            block = back[0]
            for j in range(1, pieces):
                block = jnp.where((c + j) % pieces == b, back[j], block)
            blocks.append(block)
        return jnp.concatenate(blocks, axis=0)

    def partner(values, bit):
        return lax.ppermute(values, "fsdp", [(i, i ^ bit) for i in range(fsdp)])

    def meet(*values):
        return lax.optimization_barrier(values)

    def first_hop(value):
        return [value, partner(value, bits[0])]

    def later_hops(held):
        held = {0: held[0], bits[0]: held[1]}
        for bit in bits[1:]:
            for o in list(held):
                held[o ^ bit] = partner(held[o], bit)
        return [held[o] for o in slots]

    def reduce(parts):
        held, side, last = dict(enumerate(parts)), None, None
        for bit in reversed(bits):
            for o in sorted(held, reverse=True):
                if not o & bit:
                    continue
                got, mine = partner(held.pop(o), bit), held[o ^ bit]
                if o == bits[0]:
                    last = got
                elif o == bits[1]:
                    side = got
                else:
                    held[o ^ bit] = (mine.astype(f32) + got.astype(f32)).astype(bf16)
        return held[0], side, last

    def away(values, bit):
        return lax.ppermute(values, "ctx", [(i, i ^ bit) for i in range(ctx)])

    def send(stack, bit):
        half = stack.shape[0] // 2
        return stack[:half], away(stack[half:], bit)

    def add(pair):
        return (pair[0].astype(f32) + pair[1].astype(f32)).astype(bf16)

    def grow(stack, bit):
        return stack, away(stack, bit)

    def join(pair):
        return jnp.concatenate(pair, axis=0)

    flip = c % fsdp // (fsdp // 2) * (fsdp // 2)
    blocks = [
        (f ^ o ^ flip) * pieces + (c // fsdp - j) % pieces for o in slots for j in range(pieces)
    ]
    positions = (jnp.stack(blocks)[:, None] * span + jnp.arange(span)[None, :]).reshape(length)
    turns = p.size // 2
    inverse = rope_base ** (-(jnp.arange(turns, dtype=f32) * 2.0 / p.size))
    angles = positions.astype(f32)[:, None] * inverse[None, :]
    cosine, sine = jnp.cos(angles), jnp.sin(angles)
    reps = p.table // p.size
    cosine = jnp.concatenate([cosine, cosine] * reps, axis=1)
    sine = jnp.concatenate([-sine, sine] * reps, axis=1)

    tags = jnp.pad(
        segment_ids.astype(bf16)[:, None, :], ((0, 0), (0, TAG - 1), (0, width - span))
    )
    hidden_cut, w_qkv, w_in = lax.optimization_barrier(
        (dealt(jnp.concatenate([hidden, tags], axis=1)), w_qkv, w_in)
    )
    hidden_parts = deal(hidden_cut)

    gain_a, gain_m = gain_attn.astype(f32)[:, None], gain_mlp.astype(f32)[:, None]
    here, place = jnp.reshape(c, (1,)), jnp.stack([f, c])
    half = rows // 2
    mine, other = call(
        functools.partial(cut_kernel, p=p, feed=False),
        "cut",
        [shape_of((fsdp, half, 3 * cols)), shape_of((2, half, 3 * cols))],
        1,
        [],
        [w_qkv, gain_a, place],
        1e6,
    )

    def spread_out(mine, other):
        near = [mine[0]] + [
            lax.ppermute(mine[o], "fsdp", [(i, i ^ o) for i in range(fsdp)]) for o in slots[1:]
        ]
        return near, [other[0], partner(other[1], 1)]

    near, other = spread_out(mine, other)
    hidden_parts, near, other, cosine, sine, cotangent, w_in = meet(
        hidden_parts, near, other, cosine, sine, cotangent, w_in
    )
    far = [away(part, 1) for part in near[2:]]
    cot_parts = deal(dealt(cotangent))
    unit1 = call(
        functools.partial(unit_kernel, p=p),
        "unit1",
        [shape_of((own + TAG, width))],
        1,
        [],
        hidden_parts,
        1e6,
    )[0]
    unit1, w_in_late = meet(unit1, w_in)
    mine_in, kept_in = call(
        functools.partial(cut_kernel, p=p, feed=True),
        "cut_in",
        [shape_of((fsdp, rows, p.padded)), shape_of((2, rows, p.padded))],
        1,
        [],
        [w_in_late, gain_m, place],
        1e6,
    )
    held, far, cot_parts, mine_in, kept_in = meet(
        first_hop(unit1), far, cot_parts, mine_in, kept_in
    )
    unit1_slots = later_hops(held)
    cot_own = jnp.stack(cot_parts, axis=1).reshape(own, width)
    unit1_slots, cot_own, mine_in, kept_in = meet(unit1_slots, cot_own, mine_in, kept_in)
    cot_held = first_hop(cot_own)
    near_in, other_in = spread_out(mine_in, kept_in)

    whole = shape_of((n, length, cols))
    q, k, v, segments, w_qkv_cols = call(
        functools.partial(project_kernel, p=p),
        "project",
        [whole] * 3 + [shape_of((n, 8, length), f32), shape_of((width, 3 * cols))],
        fsdp,
        [
            pltpu.VMEM((fsdp, own + TAG, width), bf16),
            pltpu.SemaphoreType.DMA((2 * fsdp,)),
            pltpu.SemaphoreType.DMA((fsdp,)),
        ],
        [Late(a) for a in unit1_slots + near + other + far] + [cosine, sine, place],
        4e9,
    )
    ranges = segments[:, 0].reshape(n, fsdp, p.part)
    spans = jnp.stack([jnp.min(ranges, axis=2), jnp.max(ranges, axis=2)], axis=2)
    spans = spans.astype(jnp.int32).reshape(2 * n * fsdp)
    made = call(
        functools.partial(attend_kernel, p=p),
        "attend",
        [tile] * fsdp + [whole, shape_of((n, 8, length), f32)],
        n * fsdp,
        [pltpu.VMEM((p.part, width), bf16)],
        [q, k, v, segments, w_attn_out],
        1.2e10,
    )
    made, cot_held, near_in, other_in = meet(made, cot_held, near_in, other_in)
    far_in = [away(part, 1) for part in near_in[2:]]
    cot_slots = later_hops(cot_held)
    attended_parts, attended, norms = made[:fsdp], made[fsdp], made[fsdp + 1]

    attended_parts = list(attended_parts)
    attended_parts[0], unit1_late = meet(attended_parts[0], unit1_slots)
    (flipped,) = call(
        functools.partial(flip_kernel, p=p),
        "flip",
        [shape_of((n, width, length))],
        fsdp,
        [],
        list(unit1_late),
        1e6,
    )
    addends = reduce(attended_parts)
    addends, flipped = meet(addends, flipped)
    residual, unit2 = call(
        functools.partial(middle_kernel, p=p),
        "middle",
        [shape_of((own, width), f32), tile],
        1,
        [],
        hidden_parts + list(addends),
        1e6,
    )
    unit2, far_in, cot_slots = meet(unit2, far_in, cot_slots)
    unit2_slots = later_hops(first_hop(unit2))

    wide = shape_of((fsdp * own, p.padded))
    made = call(
        functools.partial(mlp_kernel, p=p),
        "mlp",
        [Late(tile)] * (2 * fsdp)
        + [(wide, pl.BlockSpec((own, p.padded), lambda s: (s, 0)))] * 3,
        fsdp,
        [pltpu.VMEM((width, p.padded), bf16)] * 2
        + [pltpu.VMEM((p.padded, width), bf16)]
        + [pltpu.VMEM((fsdp, own, width), bf16)] * 4
        + [
            pltpu.SemaphoreType.DMA((4 * fsdp,)),
            pltpu.SemaphoreType.DMA((2 * fsdp,)),
            pltpu.SemaphoreType.DMA((2 * fsdp,)),
        ],
        [Late(a) for a in unit2_slots + cot_slots + near_in + other_in + far_in]
        + [w_mlp_out, place],
        1.2e10,
    )
    out_parts, u2_parts, (active, da, dg) = made[:fsdp], made[fsdp : 2 * fsdp], made[2 * fsdp :]

    u2 = reduce(u2_parts)
    act_sums, gate_sums, down_sums = call(
        functools.partial(mlp_sums_kernel, p=p),
        "mlp_sums",
        [shape_of((ctx, fsdp, small, units))] * 3,
        fsdp,
        [pltpu.VMEM((width, p.padded), f32)] * 3 + [pltpu.VMEM((own, width), bf16)] * 2,
        unit2_slots + cot_slots + [active, da, dg, here],
        6e9,
    )
    u2, act_sums, gate_sums, down_sums = meet(u2, act_sums, gate_sums, down_sums)
    grad_residual, grad_low = call(
        functools.partial(turn_kernel, p=p),
        "turn",
        [shape_of((own, width), f32), tile],
        1,
        [],
        list(u2) + [residual, cot_own],
        1e6,
    )
    order = p.order
    gate_order = p.last_order
    piece = [shape_of((n, span, width))] * pieces
    grad_low, out_parts, act_sums, gate_sums = meet(
        grad_low, list(out_parts), act_sums, gate_sums
    )
    low_held = first_hop(grad_low)
    act_pair, gate_pair = send(act_sums, order[0]), send(gate_sums, gate_order[0])
    held = dict(enumerate(out_parts))
    for bit in reversed(bits[1:]):
        for o in sorted(held, reverse=True):
            if o & bit:
                held[o ^ bit] = add((held[o ^ bit], partner(held.pop(o), bit)))
    low_held, out_near, out_far, act_pair, gate_pair = meet(
        low_held, held[0], held[bits[0]], act_pair, gate_pair
    )
    act_sums, gate_sums = add(act_pair), add(gate_pair)
    low_slots = later_hops(low_held)
    low_slots, out_far, act_sums, gate_sums, down_sums = meet(
        low_slots, out_far, act_sums, gate_sums, down_sums
    )
    act_pair, gate_pair = send(act_sums, order[1]), send(gate_sums, gate_order[1])
    down_pair = send(down_sums, order[0])
    out_got = partner(out_far, bits[0])
    mixed, attention_sums = [], []
    for group in range(p.groups):
        some = pl.BlockSpec(
            (n, length, p.lanes),
            lambda s, group=group: (0, 0, group),
            pipeline_mode=pl.Buffered(1),
        )
        wo_rows = pl.BlockSpec(
            (p.lanes, width), lambda s, group=group: (group, 0), pipeline_mode=pl.Buffered(1)
        )
        grad_mixed, sums = call(
            functools.partial(backward_kernel, p=p, group=group),
            "attention_back",
            [
                shape_of((n, length, 3 * p.lanes)),
                shape_of((ctx, 4 * fsdp * small, p.lanes)),
            ],
            n * fsdp + 1,
            [
                pltpu.VMEM((p.lanes, length), bf16),
                pltpu.VMEM((p.lanes, p.part), f32),
                pltpu.VMEM((length, p.lanes), f32),
                pltpu.VMEM((length, p.lanes), f32),
                pltpu.VMEM((n, length, width), bf16),
                pltpu.VMEM((length, 1), f32),
                pltpu.VMEM((width, 3 * p.lanes), f32),
                pltpu.VMEM((p.lanes, width), f32),
                pltpu.VMEM((n, width, length), bf16),
                pltpu.SemaphoreType.DMA((n * fsdp,)),
                pltpu.SemaphoreType.DMA((1,)),
            ],
            [Late(a) for a in low_slots]
            + [Late(flipped), (w_attn_out, wo_rows), (q, some), (k, some), (v, some), (attended, some)]
            + [segments, norms, cosine, sine, here, spans],
            1.5e10,
        )
        mixed.append(grad_mixed)
        if group == 0:
            sums, low_slots, act_pair, gate_pair, down_pair, out_got = meet(
                sums, low_slots, act_pair, gate_pair, down_pair, out_got
            )
            pairs = [send(sums, order[0])]
            act_sums, gate_sums, down_sums = add(act_pair), add(gate_pair), add(down_pair)
            for bit, gate_bit in zip(order[2:-1], gate_order[2:-1]):
                act_sums, gate_sums = add(send(act_sums, bit)), add(send(gate_sums, gate_bit))
            act_pair, gate_pair = send(act_sums, order[-1]), send(gate_sums, gate_order[-1])
            down_pair = send(down_sums, order[1])
            result_parts = call(
                functools.partial(result_kernel, p=p),
                "result",
                piece,
                1,
                [],
                [out_near, out_got, residual],
                1e6,
            )
            low_slots, result_parts = meet(low_slots, result_parts)
            out_back = undeal(result_parts)
        else:
            sums, pairs, act_pair, gate_pair, down_pair, out_back = meet(
                sums, pairs, act_pair, gate_pair, down_pair, out_back
            )
            pairs = pairs + [send(sums, order[0])]

    back_order = order[::-1]

    def step_of(sums):
        return order[ctx.bit_length() - sums.shape[0].bit_length()]

    in_small = jnp.stack([add(act_pair)[0], add(gate_pair)[0]], axis=1)
    down_sums = add(down_pair)
    for bit in order[2:-1]:
        down_sums = add(send(down_sums, bit))
    down_pair = send(down_sums, order[-1])
    early, late = pairs[:-1], pairs[-1]
    if early:
        sums = add(early[0])
        early = [send(sums, step_of(sums))]
    u1_parts = call(
        functools.partial(spread_kernel, p=p),
        "spread",
        [tile] * fsdp,
        fsdp,
        [pltpu.VMEM((own, width), bf16)],
        mixed + [w_qkv_cols],
        2e9,
    )
    in_small = lax.all_to_all(in_small, "fsdp", 0, 0, tiled=True)
    in_small = in_small.transpose(2, 1, 0, 3).reshape(1, small, 2 * fsdp * units)
    u1_parts, early, late, in_small = meet(list(u1_parts), early, late, in_small)
    u1 = reduce(u1_parts)
    if early:
        sums = add(early[0])
        early = [send(sums, step_of(sums))]
    sums = add(late)
    late = send(sums, step_of(sums))
    u1, early, late, down_pair = meet(u1, early, late, down_pair)
    back_parts = call(
        functools.partial(last_kernel, p=p),
        "last",
        piece,
        1,
        [],
        hidden_parts + list(u1) + [grad_residual],
        1e6,
    )
    sums = add(late)
    late = send(sums, step_of(sums))
    down = grow(add(down_pair), back_order[0])
    late, down, in_small = meet(late, down, in_small)

    def finished(pair):
        sums = add(pair)
        while sums.shape[0] > 1:
            sums = add(send(sums, step_of(sums)))
        return sums

    sums = jnp.concatenate([finished(pair) for pair in early + [late]], axis=0)
    in_pair = grow(in_small, back_order[0])
    back = undeal(back_parts)
    down = grow(join(down), back_order[1])
    mine = sums[:, : 3 * fsdp * small].reshape(p.groups, fsdp, 3 * small, p.lanes)
    mine = lax.all_to_all(mine, "fsdp", 1, 1, tiled=True)
    mine = mine.reshape(p.groups, 3 * fsdp * small, p.lanes)
    stack = jnp.concatenate([mine, sums[:, 3 * fsdp * small :]], axis=1)[None]
    last_back = p.last_order[::-1]
    stack = grow(stack, last_back[0])
    stack, in_pair, down, back = meet(stack, in_pair, down, back)
    stack = grow(join(stack), last_back[1])
    in_pair = grow(join(in_pair), back_order[1])
    down = grow(join(down), back_order[2])
    for bit in back_order[3:]:
        down = grow(join(down), bit)
    stack, in_pair, down = meet(stack, in_pair, down)
    mlp_stack = join(down)
    for bit in back_order[2:]:
        in_pair = grow(join(in_pair), bit)
    for bit in last_back[2:]:
        stack = grow(join(stack), bit)
    out, back = assemble(out_back), assemble(back).astype(f32)

    grad_qkv, grad_out, grad_gain_a = call(
        functools.partial(qkv_grad_kernel, p=p),
        "qkv_grad",
        [
            shape_of((rows, 3 * width), f32),
            shape_of((cols, width), f32),
            shape_of((1, rows), f32),
        ],
        1,
        [
            pltpu.VMEM((ctx, p.groups, 4 * fsdp * small, p.lanes), bf16),
            pltpu.SemaphoreType.DMA((2,)),
        ],
        [Late(stack[0]), Late(stack[1]), w_qkv, gain_a, here],
        1e6,
    )

    wide_in = 2 * fsdp * units

    def in_grads(table, sums, block, before):
        some = pl.BlockSpec((block, wide_in), lambda s, t: (t[s], 0))
        any_spec = pl.BlockSpec(memory_space=pl.ANY)
        small_out = pl.BlockSpec((1, 1, block), lambda s, t: (t[s], 0, 0))
        return pl.pallas_call(
            in_grad_kernel,
            grid_spec=pltpu.PrefetchScalarGridSpec(
                num_scalar_prefetch=1,
                grid=(sums.shape[0],),
                in_specs=[
                    pl.BlockSpec((1, block, wide_in), lambda s, t: (s, 0, 0)),
                    some,
                    pl.BlockSpec((block, 1), lambda s, t: (t[s], 0)),
                ]
                + [any_spec] * len(before),
                out_specs=[some, small_out],
            ),
            out_shape=[
                shape_of(w_in.shape, f32),
                shape_of((rows // block, 1, block), f32),
            ],
            input_output_aliases={4 + k: k for k in range(len(before))},
            compiler_params=pltpu.CompilerParams(vmem_limit_bytes=40 << 20),
            cost_estimate=pl.CostEstimate(
                flops=1000000, bytes_accessed=8 * w_in.size, transcendentals=0
            ),
            name="in_grad",
        )(table, sums, w_in, gain_m, *before)

    if small % 8:
        parts = join(in_pair)
        parts = [
            lax.dynamic_slice_in_dim(parts, storage(c ^ cc, order), 1, 0) for cc in range(ctx)
        ]
        parts = jnp.concatenate(parts, axis=1)
        grad_in, grad_gain_m = in_grads(jnp.zeros((1,), jnp.int32), parts, rows, [])
    else:
        place_of = {storage(x, order): x for x in range(ctx)}
        table = jnp.stack([c ^ place_of[at] for at in range(ctx)])
        top = ctx // 2
        before = in_grads(table[:top], in_pair[0], small, [])
        grad_in, grad_gain_m = in_grads(table[top:], in_pair[1], small, list(before))
    (grad_mlp_out,) = call(
        functools.partial(out_grad_kernel, p=p),
        "out_grad",
        [shape_of((units, width), f32)],
        1,
        [],
        [mlp_stack, here],
        1e6,
    )
    return (
        out,
        back,
        grad_qkv,
        grad_out,
        grad_in,
        grad_mlp_out,
        grad_gain_a.reshape(rows),
        grad_gain_m.reshape(rows),
    )


def solution(mesh):
    in_specs = (
        P("fsdp", "ctx", None),
        P("fsdp", "ctx"),
        P("fsdp", "ctx", None),
        P("fsdp", None),
        P("fsdp", None),
        P("fsdp", None),
        P("fsdp", None),
        P("fsdp"),
        P("fsdp"),
    )
    out_specs = (
        P("fsdp", "ctx", None),
        P("fsdp", "ctx", None),
        P("fsdp", None),
        P("fsdp", None),
        P("fsdp", None),
        P("fsdp", None),
        P("fsdp"),
        P("fsdp"),
    )
    return jax.shard_map(
        on_device, mesh=mesh, in_specs=in_specs, out_specs=out_specs, check_vma=False
    )
```

```python
import functools

import jax
import jax.numpy as jnp
from jax import lax
from jax.experimental import pallas as pl
from jax.experimental.pallas import tpu as pltpu
from jax.sharding import PartitionSpec as P

HEADS = 16
rope_base = 160000.0
norm_eps = 1e-05
masked_score = -1e30
bf16 = jnp.bfloat16
f32 = jnp.float32
NT = (((1,), (1,)), ((), ()))
NN = (((1,), (0,)), ((), ()))
TN = (((0,), (0,)), ((), ()))
TAG = 16


def mm(a, b, dims=NN):
    return lax.dot_general(a, b, dims, preferred_element_type=f32)


class Late:
    def __init__(self, value):
        self.value = self.shape_is = value


def copies(pairs, sems):
    return [pltpu.make_async_copy(a, b, sems.at[k]) for k, (a, b) in enumerate(pairs)]


def call(kernel, name, out_shape, grid, scratch, args, flops, limit=56):
    def spec(a):
        if isinstance(a, tuple):
            return a[1]
        if isinstance(a, Late):
            return pl.BlockSpec(memory_space=pl.ANY)
        if a.dtype == jnp.int32:
            return pl.BlockSpec(memory_space=pltpu.SMEM)
        return pl.BlockSpec(
            a.shape, lambda s, nd=len(a.shape): (0,) * nd, pipeline_mode=pl.Buffered(1)
        )

    specs = [spec(a) for a in args]
    args = [a[0] if isinstance(a, tuple) else getattr(a, "value", a) for a in args]
    outs = [spec(a) for a in out_shape]
    out_shape = [a[0] if isinstance(a, tuple) else getattr(a, "shape_is", a) for a in out_shape]
    moved = sum(a.size * a.dtype.itemsize for a in args)
    moved += sum(a.size * a.dtype.itemsize for a in out_shape)
    return pl.pallas_call(
        kernel,
        grid=(grid,),
        in_specs=specs,
        out_specs=outs,
        out_shape=out_shape,
        scratch_shapes=scratch,
        compiler_params=pltpu.CompilerParams(vmem_limit_bytes=limit << 20),
        cost_estimate=pl.CostEstimate(
            flops=int(flops), bytes_accessed=int(moved), transcendentals=0
        ),
        name=name,
    )(*args)


def shape_of(shape, dtype=bf16):
    return jax.ShapeDtypeStruct(shape, dtype)


def head_mask(shape, head, size):
    return lax.broadcasted_iota(jnp.int32, shape, 1) // size == head


def swap(values, size):
    width, half = values.shape[1], size // 2
    if width == size:
        return jnp.concatenate([values[:, half:], values[:, :half]], axis=1)
    lane = lax.broadcasted_iota(jnp.int32, values.shape, 1) % size
    return jnp.where(
        lane < half, pltpu.roll(values, width - half, 1), pltpu.roll(values, half, 1)
    )


def norm_stats(values):
    center = values - jnp.mean(values, axis=-1, keepdims=True)
    rate = lax.rsqrt(jnp.mean(center * center, axis=-1, keepdims=True) + norm_eps)
    return center * rate, rate


def norm_back(grad, unit, rate):
    return rate * (
        grad
        - jnp.mean(grad, axis=-1, keepdims=True)
        - unit * jnp.mean(grad * unit, axis=-1, keepdims=True)
    )


class Plan:
    def __init__(self, fsdp, ctx, batch, span, width, units, rows):
        self.fsdp, self.ctx, self.span, self.width = fsdp, ctx, span, width
        self.pieces = ctx // fsdp
        self.n = batch // self.pieces
        self.part = self.pieces * span
        self.own = self.n * self.part
        self.length = span * ctx
        self.heads = HEADS // fsdp
        self.size = width // HEADS
        self.cols = self.heads * self.size
        self.units, self.rows = units, rows
        self.padded = -(-units // 256) * 256
        self.small = rows // ctx
        self.groups = 2 if self.heads % 2 == 0 else 1
        self.lanes = self.cols // self.groups
        self.slab = self.lanes // ctx
        self.table = min(128, self.cols)
        bits = [1 << b for b in range(ctx.bit_length() - 1)]
        self.order = bits
        self.last_order = bits[1:] + bits[:1]

    def locations(self):
        return [
            (i, j, (i * self.pieces + j) * self.span)
            for i in range(self.n)
            for j in range(self.pieces)
        ]


def storage(x, order):
    at = 0
    for bit in order:
        at = at * 2 + x // bit % 2
    return at


def cut_kernel(w, gain, at_ref, mine, other, *, p, feed):
    half, here = p.rows // 2, at_ref[0]
    side = at_ref[1] % 2
    near = pl.ds(pl.multiple_of(side * half, half), half)
    far = pl.ds(pl.multiple_of((1 - side) * half, half), half)
    size = p.units if feed else p.cols
    if feed and p.padded != size:
        mine[:, :, size:] = jnp.zeros((p.fsdp, 2 * half, p.padded - size), bf16)
        other[:, :, size:] = jnp.zeros((2, 2 * half, p.padded - size), bf16)
    for t in range(p.fsdp):
        o = t ^ here
        for m in range(2 if feed else 3):
            at = (m * p.fsdp + t) * size
            if feed:
                there = slice(m * half, (m + 1) * half), slice(0, size)
            else:
                there = slice(None), slice(m * size, (m + 1) * size)
            value = w[near, at : at + size].astype(f32) * gain[near, :]
            mine[(o,) + there] = value.astype(bf16)

            @pl.when(o < 2)
            def _(at=at, there=there, o=o):
                value = w[far, at : at + size].astype(f32) * gain[far, :]
                other[(o,) + there] = value.astype(bf16)


def unit_kernel(*refs, p):
    pieces, unit = refs[:-1], refs[-1]
    unit[p.own :, :] = jnp.zeros((TAG, p.width), bf16)
    for i, j, at in p.locations():
        ref = pieces[j]
        value, _ = norm_stats(ref[i, : p.span].astype(f32))
        unit[at : at + p.span] = value.astype(bf16)
        unit[p.own :, at : at + p.span] = ref[i, p.span :, : p.span]


def project_kernel(*refs, p):
    fs, gs = p.fsdp, p.part
    xs, rest = refs[:fs], refs[fs:]
    near, other, rest = rest[:fs], rest[fs : 2 * fs], rest[2 * fs :]
    cos, sin, at_ref, q_ref, k_ref, v_ref, seg_ref, w, x, w_sems, x_sems = rest
    step = pl.program_id(0)
    scale = p.size**-0.5
    half, side = p.rows // 2, at_ref[1] % 2
    pairs = []
    for o in range(fs):
        base = (at_ref[0] ^ o) * 2
        for part, at in ((near[o], base + side), (other[o], base + 1 - side)):
            pairs.append((part, w.at[pl.ds(pl.multiple_of(at * half, half), half), :]))
    w_copies = copies(pairs, w_sems)
    x_copies = copies([(xs[o], x.at[o]) for o in range(fs)], x_sems)

    @pl.when(step == 0)
    def _():
        for copy in x_copies[:1] + w_copies + x_copies[1:]:
            copy.start()
        for copy in w_copies:
            copy.wait()

    for o in range(fs):

        @pl.when(step == o)
        def _(o=o):
            x_copies[o].wait()
            for i in range(p.n):
                tag = x[o, p.own : p.own + TAG, i * gs : (i + 1) * gs].astype(f32)
                seg_ref[i, :, o * gs : (o + 1) * gs] = tag[:8]

    mixed = mm(x[step, : p.own], w[...])
    rows = pl.ds(pl.multiple_of(step * gs, gs), gs)
    reps = p.cols // p.table
    cosine = jnp.concatenate([cos[rows, :]] * reps, axis=1)
    sine = jnp.concatenate([sin[rows, :]] * reps, axis=1)
    for i in range(p.n):
        own = mixed[i * gs : (i + 1) * gs]
        query, key = own[:, : p.cols], own[:, p.cols : 2 * p.cols]
        query = (query * cosine + swap(query, p.size) * sine) * scale
        q_ref[i, rows, :] = query.astype(bf16)
        k_ref[i, rows, :] = (key * cosine + swap(key, p.size) * sine).astype(bf16)
        v_ref[i, rows, :] = own[:, 2 * p.cols :].astype(bf16)


def attend_kernel(q_ref, k_ref, v_ref, seg_ref, wo, *rest, p):
    fs, gs = p.fsdp, p.part
    parts, (att_ref, norm_ref, made) = rest[:fs], rest[fs:]
    step = pl.program_id(0)
    i, o = step // fs, step % fs
    rows = pl.ds(pl.multiple_of(o * gs, gs), gs)
    q, k, v = q_ref[i, rows, :], k_ref[i], v_ref[i]
    allowed = seg_ref[i, :, rows].T[:, :1] == seg_ref[i, :1, :]
    attended = jnp.zeros(q.shape, f32)
    norms = jnp.zeros((gs, 128), f32)
    lane = lax.broadcasted_iota(jnp.int32, norms.shape, 1)
    for head in range(p.heads):
        here = head_mask(q.shape, head, p.size)
        scores = mm(jnp.where(here, q, jnp.zeros_like(q)), k, NT)
        scores = jnp.where(allowed, scores, masked_score)
        peak = jnp.max(scores, axis=1, keepdims=True)
        weights = jnp.exp(scores - peak)
        total = jnp.sum(weights, axis=1, keepdims=True)
        attended = jnp.where(here, mm(weights.astype(bf16), v) / total, attended)
        norms = jnp.where(lane == head, peak + jnp.log(total), norms)
    norm_ref[i, :, rows] = norms.T[:8]
    attended = attended.astype(bf16)
    att_ref[i, rows, :] = attended
    made[...] = mm(attended, wo[...]).astype(bf16)
    for oo in range(fs):

        @pl.when(o == oo)
        def _(oo=oo):
            parts[oo][pl.ds(pl.multiple_of(i * gs, gs), gs), :] = made[...]


def flip_kernel(*refs, p):
    xs, out = refs[:-1], refs[-1]
    gs = p.part
    for o in range(p.fsdp):

        @pl.when(pl.program_id(0) == o)
        def _(o=o):
            for i in range(p.n):
                out[i, :, o * gs : (o + 1) * gs] = xs[o][i * gs : (i + 1) * gs, :].T


def shares(span_ref, i, a, b, fs):
    one, two = (i * fs + a) * 2, (i * fs + b) * 2
    return jnp.logical_and(
        span_ref[one] <= span_ref[two + 1], span_ref[two] <= span_ref[one + 1]
    )


def backward_kernel(*refs, p, group):
    fs, gs, cols = p.fsdp, p.part, p.lanes
    gls, rest = refs[:fs], refs[fs:]
    xt, wo, rest = rest[0], rest[1], rest[2:]
    q_ref, k_ref, v_ref, att_ref, seg_ref, norm_ref, cos, sin, c_ref, span_ref = rest[:10]
    gm, sums, kt, dqt, dk, dv, gl, seg_col, sum_qkv, sum_out, flat, sems, flat_sem = rest[10:]
    step = pl.program_id(0)
    scale = p.size**-0.5
    reps = cols // p.table

    def turned(grad, rows):
        cosine = jnp.concatenate([cos[rows, :]] * reps, axis=1)
        sine = jnp.concatenate([sin[rows, :]] * reps, axis=1)
        return grad * cosine - swap(grad, p.size) * sine

    pairs = [
        (gls[o].at[i * gs : (i + 1) * gs], gl.at[i, o * gs : (o + 1) * gs])
        for i in range(p.n)
        for o in range(fs)
    ]
    low_copies = copies(pairs, sems)
    flat_copy = pltpu.make_async_copy(xt, flat, flat_sem.at[0])

    @pl.when(step == 0)
    def _():
        for copy in low_copies:
            copy.start()
        flat_copy.start()

    @pl.when(step < p.n * fs)
    def _():
        i, o = step // fs, step % fs
        rows = pl.ds(pl.multiple_of(o * gs, gs), gs)
        for k in range(p.n * fs):

            @pl.when(step == k)
            def _(k=k):
                low_copies[k].wait()

        q = q_ref[i, rows, :]

        @pl.when(o == 0)
        def _():
            kt[...] = k_ref[i].T
            dk[...] = jnp.zeros_like(dk)
            dv[...] = jnp.zeros_like(dv)
            seg_col[...] = seg_ref[i].T[:, :1]

        attended = att_ref[i, rows, :]
        g = mm(gl[i, rows, :], wo[...], NT).astype(bf16)
        count = p.heads // p.groups
        picks = lax.broadcasted_iota(jnp.int32, (8, cols), 0)
        picks = (lax.broadcasted_iota(jnp.int32, (8, cols), 1) // p.size == picks).astype(f32)
        deltas = lax.dot_general(
            picks,
            g.astype(f32) * attended.astype(f32),
            NT,
            precision=lax.Precision.HIGHEST,
            preferred_element_type=f32,
        )
        zero = jnp.zeros_like(q)
        masks = [head_mask(q.shape, h, p.size) for h in range(count)]
        own_q = [jnp.where(mask, q, zero) for mask in masks]
        own_g = [jnp.where(mask, g, zero) for mask in masks]
        mine = seg_ref[i, :1, rows]
        dqt[...] = jnp.zeros_like(dqt)
        for kk in range(fs):
            keys = slice(kk * gs, (kk + 1) * gs)

            @pl.when(shares(span_ref, i, o, kk, fs))
            def _(keys=keys):
                k, v = k_ref[i, keys, :], v_ref[i, keys, :]
                allowed = seg_col[keys, :] == mine
                for h in range(count):
                    first = group * count + h
                    scores = jnp.where(allowed, mm(k, own_q[h], NT), masked_score)
                    probs = jnp.exp(scores - norm_ref[i, first : first + 1, rows])
                    grad = mm(v, own_g[h], NT)
                    grad = (probs * (grad - deltas[h : h + 1, :])).astype(bf16)
                    dv[keys, :] += mm(probs.astype(bf16), own_g[h])
                    dk[keys, :] += mm(grad, own_q[h])
                    at = slice(h * p.size, (h + 1) * p.size)
                    dqt[at, :] += mm(kt[at, keys], grad)

        gm[i, rows, :cols] = (turned(dqt[...].T, rows) * scale).astype(bf16)

        @pl.when(o == fs - 1)
        def _():
            gm[i, :, cols : 2 * cols] = turned(dk[...], slice(None)).astype(bf16)
            gm[i, :, 2 * cols :] = dv[...].astype(bf16)

    @pl.when(step == p.n * fs)
    def _():
        flat_copy.wait()
        total = [mm(flat[i], gm[i]) for i in range(p.n)]
        sum_qkv[...] = sum(total[1:], total[0])
        total = [mm(att_ref[i].T, gl[i]) for i in range(p.n)]
        sum_out[...] = sum(total[1:], total[0])
        small, slab = p.small, p.slab
        for cc in range(p.ctx):
            away = storage(c_ref[0] ^ cc, p.order)
            for ff in range(fs):
                for m in range(3):
                    part = sum_qkv[
                        ff * p.rows + cc * small : ff * p.rows + (cc + 1) * small,
                        m * cols : (m + 1) * cols,
                    ]
                    at = (ff * 3 + m) * small
                    sums[away, at : at + small, :] = part.astype(bf16)
            for d in range(p.width // cols):
                part = sum_out[cc * slab : (cc + 1) * slab, d * cols : (d + 1) * cols]
                at = 3 * fs * small + d * slab
                sums[away, at : at + slab, :] = part.astype(bf16)


def spread_kernel(*refs, p):
    gms, w, parts, made = refs[: p.groups], refs[p.groups], refs[p.groups + 1 : -1], refs[-1]
    o, lanes = pl.program_id(0), p.lanes
    rows = pl.ds(pl.multiple_of(o * p.part, p.part), p.part)
    for i in range(p.n):
        grad = jnp.concatenate(
            [gm[i, rows, m * lanes : (m + 1) * lanes] for m in range(3) for gm in gms], axis=1
        )
        made[i * p.part : (i + 1) * p.part] = mm(grad, w[...], NT).astype(bf16)
    for oo in range(p.fsdp):

        @pl.when(o == oo)
        def _(oo=oo):
            parts[oo][...] = made[...]


def mlp_kernel(*refs, p):
    fs, units, pad = p.fsdp, p.units, p.padded
    xs, cs, rest = refs[:fs], refs[fs : 2 * fs], refs[2 * fs :]
    near, other, rest = rest[:fs], rest[fs : 2 * fs], rest[2 * fs :]
    w_out, at_ref, rest = rest[0], rest[1], rest[2:]
    outs, us, rest = rest[:fs], rest[fs : 2 * fs], rest[2 * fs :]
    act_ref, da_ref, dg_ref, wa, wg, wm, x, ct, made, made_u, w_sems, sems, out_sems = rest
    step = pl.program_id(0)
    half, side = p.rows // 2, at_ref[1] % 2
    pairs = []
    for o in range(fs):
        base = (at_ref[0] ^ o) * 2
        for part, at in ((near[o], base + side), (other[o], base + 1 - side)):
            at = pl.ds(pl.multiple_of(at * half, half), half)
            pairs.append((part.at[:half], wa.at[at, :]))
            pairs.append((part.at[half:], wg.at[at, :]))
    w_copies = copies(pairs, w_sems)
    pairs = []
    for o in range(fs):
        pairs += [(xs[o], x.at[o]), (cs[o], ct.at[o])]
    x_copies = copies(pairs, sems)
    pairs = []
    for o in range(fs):
        pairs += [(made.at[o], outs[o]), (made_u.at[o], us[o])]
    out_copies = copies(pairs, out_sems)

    @pl.when(step == 0)
    def _():
        for copy in x_copies[:1] + w_copies + x_copies[1:]:
            copy.start()
        if pad != units:
            wm[units:, :] = jnp.zeros((pad - units, p.width), bf16)
        wm[:units, :] = w_out[...]
        for copy in w_copies:
            copy.wait()

    for o in range(fs):

        @pl.when(step == o)
        def _(o=o):
            x_copies[2 * o].wait()
            x_copies[2 * o + 1].wait()

    act, gate = mm(x[step], wa[...]), mm(x[step], wg[...])
    phi = 0.5 * (1.0 + lax.erf(act * (2.0**-0.5)))
    gelu = act * phi
    active = (gelu * gate).astype(bf16)
    made[step] = mm(active, wm[...]).astype(bf16)
    grad = mm(ct[step], wm[...], NT)
    slope = phi + act * (jnp.exp(-0.5 * act * act) * 0.3989422804014327)
    da, dg = (grad * gate * slope).astype(bf16), (grad * gelu).astype(bf16)
    made_u[step] = (mm(da, wa[...], NT) + mm(dg, wg[...], NT)).astype(bf16)
    act_ref[...], da_ref[...], dg_ref[...] = active, da, dg
    for o in range(fs):

        @pl.when(step == o)
        def _(o=o):
            out_copies[2 * o].start()
            out_copies[2 * o + 1].start()

    @pl.when(step == fs - 1)
    def _():
        for copy in out_copies:
            copy.wait()


def mlp_sums_kernel(*refs, p):
    fs, units = p.fsdp, p.units
    xs, cs, rest = refs[:fs], refs[fs : 2 * fs], refs[2 * fs :]
    act_ref, da_ref, dg_ref, c_ref, one, two, three, sa, sg, sm, x, ct = rest
    step = pl.program_id(0)

    @pl.when(step == 0)
    def _():
        sa[...] = jnp.zeros_like(sa)
        sg[...] = jnp.zeros_like(sg)
        sm[...] = jnp.zeros_like(sm)

    for o in range(fs):

        @pl.when(step == o)
        def _(o=o):
            x[...] = xs[o][...]
            ct[...] = cs[o][...]

    rows = pl.ds(pl.multiple_of(step * p.own, p.own), p.own)
    sa[...] += mm(x[...], da_ref[rows, :], TN)
    sg[...] += mm(x[...], dg_ref[rows, :], TN)
    sm[...] += mm(ct[...], act_ref[rows, :], TN)

    @pl.when(step == fs - 1)
    def _():
        for cc in range(p.ctx):
            away = storage(c_ref[0] ^ cc, p.order)
            late = storage(c_ref[0] ^ cc, p.last_order)
            for ff in range(fs):
                at = slice(ff * p.rows + cc * p.small, ff * p.rows + (cc + 1) * p.small)
                one[away, ff] = sa[at, :units].astype(bf16)
                two[late, ff] = sg[at, :units].astype(bf16)
                three[away, ff] = sm[at, :units].astype(bf16)


def middle_kernel(*refs, p):
    g = p.pieces
    hidden, (a, b, c), (residual, unit) = refs[:g], refs[g : g + 3], refs[g + 3 :]
    for i, j, at in p.locations():
        rows = slice(at, at + p.span)
        total = a[rows].astype(f32) + b[rows].astype(f32) + c[rows].astype(f32)
        total = total + hidden[j][i, : p.span].astype(f32)
        residual[rows] = total
        unit[rows] = norm_stats(total)[0].astype(bf16)


def turn_kernel(a, b, c, residual, cot, grad, low, *, p):
    for _, _, at in p.locations():
        rows = slice(at, at + p.span)
        u = a[rows].astype(f32) + b[rows].astype(f32) + c[rows].astype(f32)
        unit, rate = norm_stats(residual[rows])
        total = cot[rows].astype(f32) + norm_back(u, unit, rate)
        grad[rows] = total
        low[rows] = total.astype(bf16)


def result_kernel(*refs, p):
    (a, b, residual), outs = refs[:3], refs[3:]
    for i, j, at in p.locations():
        rows = slice(at, at + p.span)
        total = a[rows].astype(f32) + b[rows].astype(f32)
        outs[j][i] = (total + residual[rows]).astype(bf16)


def last_kernel(*refs, p):
    g = p.pieces
    hidden, (a, b, c, grad), outs = refs[:g], refs[g : g + 4], refs[g + 4 :]
    for i, j, at in p.locations():
        rows = slice(at, at + p.span)
        u = a[rows].astype(f32) + b[rows].astype(f32) + c[rows].astype(f32)
        unit, rate = norm_stats(hidden[j][i, : p.span].astype(f32))
        outs[j][i] = (grad[rows] + norm_back(u, unit, rate)).astype(bf16)


def row_sums(values):
    ones = jnp.ones((8, values.shape[1]), f32)
    total = lax.dot_general(
        ones, values, NT, precision=lax.Precision.HIGHEST, preferred_element_type=f32
    )
    return total[:1]


def qkv_grad_kernel(low, high, w, gain, c_ref, qkv, out, gain_grad, stack, sems, *, p):
    fs, small, slab, lanes = p.fsdp, p.small, p.slab, p.lanes
    top = low.shape[0]
    loads = copies([(low, stack.at[:top]), (high, stack.at[top:])], sems)
    for load in loads:
        load.start()
    for load in loads:
        load.wait()
    for cc in range(p.ctx):
        away = storage(c_ref[0] ^ cc, p.last_order)
        rows = slice(cc * small, (cc + 1) * small)
        scale = gain[rows, :]
        total = jnp.zeros((small, lanes), f32)
        for g in range(p.groups):
            for ff in range(fs):
                for m in range(3):
                    at = (ff * 3 + m) * small
                    value = stack[away, g, at : at + small, :].astype(f32)
                    there = m * p.width + ff * p.cols + g * lanes
                    qkv[rows, there : there + lanes] = value * scale
                    total = total + value * w[rows, there : there + lanes].astype(f32)
            for d in range(p.width // lanes):
                at = 3 * fs * small + d * slab
                value = stack[away, g, at : at + slab, :].astype(f32)
                row = g * lanes + cc * slab
                out[row : row + slab, d * lanes : (d + 1) * lanes] = value
        gain_grad[:, rows] = row_sums(total)


def in_grad_kernel(table, sums, w, gain, *rest):
    grad, gain_grad = rest[-2:]
    value = sums[0].astype(f32)
    grad[...] = value * gain[...]
    total = jnp.zeros((value.shape[0], 128), f32)
    for at in range(0, value.shape[1], 128):
        total = total + value[:, at : at + 128] * w[:, at : at + 128].astype(f32)
    gain_grad[0] = row_sums(total)


def out_grad_kernel(stack, c_ref, grad, *, p):
    for cc in range(p.ctx):
        away = storage(c_ref[0] ^ cc, p.order)
        for ff in range(p.fsdp):
            at = ff * p.rows + cc * p.small
            grad[:, at : at + p.small] = stack[away, ff].astype(f32).T


def on_device(
    hidden, segment_ids, cotangent, w_qkv, w_attn_out, w_in, w_mlp_out, gain_attn, gain_mlp
):
    fsdp, ctx = lax.axis_size("fsdp"), lax.axis_size("ctx")
    f, c = lax.axis_index("fsdp"), lax.axis_index("ctx")
    batch, span, width = hidden.shape
    p = Plan(fsdp, ctx, batch, span, width, w_mlp_out.shape[0], w_in.shape[0])
    n, own, cols, units, rows, small = p.n, p.own, p.cols, p.units, p.rows, p.small
    length, pieces = p.length, p.pieces
    both = ("ctx", "fsdp")
    slots = range(fsdp)
    tile = shape_of((own, width))
    bits = [fsdp >> 1 + b for b in range(fsdp.bit_length() - 1)]

    def mixed_bits(index):
        out = 0
        for bit in bits:
            out = out + index // (fsdp // 2 // bit) % 2 * bit
        return out

    def route(j):
        pairs = []
        for cc in range(ctx):
            for ff in range(fsdp):
                to_c = (cc + j) % pieces * fsdp + mixed_bits(ff)
                to_f = cc // pieces ^ ff % 2 * (fsdp // 2)
                pairs.append((cc * fsdp + ff, to_c * fsdp + to_f))
        return pairs

    def dealt(values):
        return [
            lax.dynamic_slice_in_dim(values, (c + j) % pieces * n, n, 0) for j in range(pieces)
        ]

    def deal(parts):
        return [lax.ppermute(part, both, route(j)) for j, part in enumerate(parts)]

    def undeal(parts):
        back = [
            lax.ppermute(part, both, [(b, a) for a, b in route(j)])
            for j, part in enumerate(parts)
        ]
        return back

    def assemble(back):
        if pieces == 1:
            return back[0]
        blocks = []
        for b in range(pieces):
            block = back[0]
            for j in range(1, pieces):
                block = jnp.where((c + j) % pieces == b, back[j], block)
            blocks.append(block)
        return jnp.concatenate(blocks, axis=0)

    def partner(values, bit):
        return lax.ppermute(values, "fsdp", [(i, i ^ bit) for i in range(fsdp)])

    def meet(*values):
        return lax.optimization_barrier(values)

    def first_hop(value):
        return [value, partner(value, bits[0])]

    def later_hops(held):
        held = {0: held[0], bits[0]: held[1]}
        for bit in bits[1:]:
            for o in list(held):
                held[o ^ bit] = partner(held[o], bit)
        return [held[o] for o in slots]

    def reduce(parts):
        held, side, last = dict(enumerate(parts)), None, None
        for bit in reversed(bits):
            for o in sorted(held, reverse=True):
                if not o & bit:
                    continue
                got, mine = partner(held.pop(o), bit), held[o ^ bit]
                if o == bits[0]:
                    last = got
                elif o == bits[1]:
                    side = got
                else:
                    held[o ^ bit] = (mine.astype(f32) + got.astype(f32)).astype(bf16)
        return held[0], side, last

    def away(values, bit):
        return lax.ppermute(values, "ctx", [(i, i ^ bit) for i in range(ctx)])

    def send(stack, bit):
        half = stack.shape[0] // 2
        return stack[:half], away(stack[half:], bit)

    def add(pair):
        return (pair[0].astype(f32) + pair[1].astype(f32)).astype(bf16)

    def grow(stack, bit):
        return stack, away(stack, bit)

    def join(pair):
        return jnp.concatenate(pair, axis=0)

    flip = c % fsdp // (fsdp // 2) * (fsdp // 2)
    blocks = [
        (f ^ o ^ flip) * pieces + (c // fsdp - j) % pieces for o in slots for j in range(pieces)
    ]
    positions = (jnp.stack(blocks)[:, None] * span + jnp.arange(span)[None, :]).reshape(length)
    turns = p.size // 2
    inverse = rope_base ** (-(jnp.arange(turns, dtype=f32) * 2.0 / p.size))
    angles = positions.astype(f32)[:, None] * inverse[None, :]
    cosine, sine = jnp.cos(angles), jnp.sin(angles)
    reps = p.table // p.size
    cosine = jnp.concatenate([cosine, cosine] * reps, axis=1)
    sine = jnp.concatenate([-sine, sine] * reps, axis=1)

    tags = jnp.pad(
        segment_ids.astype(bf16)[:, None, :], ((0, 0), (0, TAG - 1), (0, width - span))
    )
    hidden_cut, w_qkv, w_in = lax.optimization_barrier(
        (dealt(jnp.concatenate([hidden, tags], axis=1)), w_qkv, w_in)
    )
    hidden_parts = deal(hidden_cut)

    gain_a, gain_m = gain_attn.astype(f32)[:, None], gain_mlp.astype(f32)[:, None]
    here, place = jnp.reshape(c, (1,)), jnp.stack([f, c])
    half = rows // 2
    mine, other = call(
        functools.partial(cut_kernel, p=p, feed=False),
        "cut",
        [shape_of((fsdp, half, 3 * cols)), shape_of((2, half, 3 * cols))],
        1,
        [],
        [w_qkv, gain_a, place],
        1e6,
    )

    def spread_out(mine, other):
        near = [mine[0]] + [
            lax.ppermute(mine[o], "fsdp", [(i, i ^ o) for i in range(fsdp)]) for o in slots[1:]
        ]
        return near, [other[0], partner(other[1], 1)]

    near, other = spread_out(mine, other)
    hidden_parts, near, other, cosine, sine, cotangent, w_in = meet(
        hidden_parts, near, other, cosine, sine, cotangent, w_in
    )
    far = [away(part, 1) for part in near[2:]]
    cot_parts = deal(dealt(cotangent))
    unit1 = call(
        functools.partial(unit_kernel, p=p),
        "unit1",
        [shape_of((own + TAG, width))],
        1,
        [],
        hidden_parts,
        1e6,
    )[0]
    unit1, w_in_late = meet(unit1, w_in)
    mine_in, kept_in = call(
        functools.partial(cut_kernel, p=p, feed=True),
        "cut_in",
        [shape_of((fsdp, rows, p.padded)), shape_of((2, rows, p.padded))],
        1,
        [],
        [w_in_late, gain_m, place],
        1e6,
    )
    held, far, cot_parts, mine_in, kept_in = meet(
        first_hop(unit1), far, cot_parts, mine_in, kept_in
    )
    unit1_slots = later_hops(held)
    cot_own = jnp.stack(cot_parts, axis=1).reshape(own, width)
    unit1_slots, cot_own, mine_in, kept_in = meet(unit1_slots, cot_own, mine_in, kept_in)
    cot_held = first_hop(cot_own)
    near_in, other_in = spread_out(mine_in, kept_in)

    whole = shape_of((n, length, cols))
    q, k, v, segments, w_qkv_cols = call(
        functools.partial(project_kernel, p=p),
        "project",
        [whole] * 3 + [shape_of((n, 8, length), f32), shape_of((width, 3 * cols))],
        fsdp,
        [
            pltpu.VMEM((fsdp, own + TAG, width), bf16),
            pltpu.SemaphoreType.DMA((2 * fsdp,)),
            pltpu.SemaphoreType.DMA((fsdp,)),
        ],
        [Late(a) for a in unit1_slots + near + other + far] + [cosine, sine, place],
        4e9,
    )
    ranges = segments[:, 0].reshape(n, fsdp, p.part)
    spans = jnp.stack([jnp.min(ranges, axis=2), jnp.max(ranges, axis=2)], axis=2)
    spans = spans.astype(jnp.int32).reshape(2 * n * fsdp)
    made = call(
        functools.partial(attend_kernel, p=p),
        "attend",
        [tile] * fsdp + [whole, shape_of((n, 8, length), f32)],
        n * fsdp,
        [pltpu.VMEM((p.part, width), bf16)],
        [q, k, v, segments, w_attn_out],
        1.2e10,
    )
    made, cot_held, near_in, other_in = meet(made, cot_held, near_in, other_in)
    far_in = [away(part, 1) for part in near_in[2:]]
    cot_slots = later_hops(cot_held)
    attended_parts, attended, norms = made[:fsdp], made[fsdp], made[fsdp + 1]

    attended_parts = list(attended_parts)
    attended_parts[0], unit1_late = meet(attended_parts[0], unit1_slots)
    (flipped,) = call(
        functools.partial(flip_kernel, p=p),
        "flip",
        [shape_of((n, width, length))],
        fsdp,
        [],
        list(unit1_late),
        1e6,
    )
    addends = reduce(attended_parts)
    addends, flipped = meet(addends, flipped)
    residual, unit2 = call(
        functools.partial(middle_kernel, p=p),
        "middle",
        [shape_of((own, width), f32), tile],
        1,
        [],
        hidden_parts + list(addends),
        1e6,
    )
    unit2, far_in, cot_slots = meet(unit2, far_in, cot_slots)
    unit2_slots = later_hops(first_hop(unit2))

    wide = shape_of((fsdp * own, p.padded))
    made = call(
        functools.partial(mlp_kernel, p=p),
        "mlp",
        [Late(tile)] * (2 * fsdp)
        + [(wide, pl.BlockSpec((own, p.padded), lambda s: (s, 0)))] * 3,
        fsdp,
        [pltpu.VMEM((width, p.padded), bf16)] * 2
        + [pltpu.VMEM((p.padded, width), bf16)]
        + [pltpu.VMEM((fsdp, own, width), bf16)] * 4
        + [
            pltpu.SemaphoreType.DMA((4 * fsdp,)),
            pltpu.SemaphoreType.DMA((2 * fsdp,)),
            pltpu.SemaphoreType.DMA((2 * fsdp,)),
        ],
        [Late(a) for a in unit2_slots + cot_slots + near_in + other_in + far_in]
        + [w_mlp_out, place],
        1.2e10,
    )
    out_parts, u2_parts, (active, da, dg) = made[:fsdp], made[fsdp : 2 * fsdp], made[2 * fsdp :]

    u2 = reduce(u2_parts)
    act_sums, gate_sums, down_sums = call(
        functools.partial(mlp_sums_kernel, p=p),
        "mlp_sums",
        [shape_of((ctx, fsdp, small, units))] * 3,
        fsdp,
        [pltpu.VMEM((width, p.padded), f32)] * 3 + [pltpu.VMEM((own, width), bf16)] * 2,
        unit2_slots + cot_slots + [active, da, dg, here],
        6e9,
    )
    u2, act_sums, gate_sums, down_sums = meet(u2, act_sums, gate_sums, down_sums)
    grad_residual, grad_low = call(
        functools.partial(turn_kernel, p=p),
        "turn",
        [shape_of((own, width), f32), tile],
        1,
        [],
        list(u2) + [residual, cot_own],
        1e6,
    )
    order = p.order
    gate_order = p.last_order
    piece = [shape_of((n, span, width))] * pieces
    grad_low, out_parts, act_sums, gate_sums = meet(
        grad_low, list(out_parts), act_sums, gate_sums
    )
    low_held = first_hop(grad_low)
    act_pair, gate_pair = send(act_sums, order[0]), send(gate_sums, gate_order[0])
    held = dict(enumerate(out_parts))
    for bit in reversed(bits[1:]):
        for o in sorted(held, reverse=True):
            if o & bit:
                held[o ^ bit] = add((held[o ^ bit], partner(held.pop(o), bit)))
    low_held, out_near, out_far, act_pair, gate_pair = meet(
        low_held, held[0], held[bits[0]], act_pair, gate_pair
    )
    act_sums, gate_sums = add(act_pair), add(gate_pair)
    low_slots = later_hops(low_held)
    low_slots, out_far, act_sums, gate_sums, down_sums = meet(
        low_slots, out_far, act_sums, gate_sums, down_sums
    )
    act_pair, gate_pair = send(act_sums, order[1]), send(gate_sums, gate_order[1])
    down_pair = send(down_sums, order[0])
    out_got = partner(out_far, bits[0])
    mixed, attention_sums = [], []
    for group in range(p.groups):
        some = pl.BlockSpec(
            (n, length, p.lanes),
            lambda s, group=group: (0, 0, group),
            pipeline_mode=pl.Buffered(1),
        )
        wo_rows = pl.BlockSpec(
            (p.lanes, width), lambda s, group=group: (group, 0), pipeline_mode=pl.Buffered(1)
        )
        grad_mixed, sums = call(
            functools.partial(backward_kernel, p=p, group=group),
            "attention_back",
            [
                shape_of((n, length, 3 * p.lanes)),
                shape_of((ctx, 4 * fsdp * small, p.lanes)),
            ],
            n * fsdp + 1,
            [
                pltpu.VMEM((p.lanes, length), bf16),
                pltpu.VMEM((p.lanes, p.part), f32),
                pltpu.VMEM((length, p.lanes), f32),
                pltpu.VMEM((length, p.lanes), f32),
                pltpu.VMEM((n, length, width), bf16),
                pltpu.VMEM((length, 1), f32),
                pltpu.VMEM((width, 3 * p.lanes), f32),
                pltpu.VMEM((p.lanes, width), f32),
                pltpu.VMEM((n, width, length), bf16),
                pltpu.SemaphoreType.DMA((n * fsdp,)),
                pltpu.SemaphoreType.DMA((1,)),
            ],
            [Late(a) for a in low_slots]
            + [Late(flipped), (w_attn_out, wo_rows), (q, some), (k, some), (v, some), (attended, some)]
            + [segments, norms, cosine, sine, here, spans],
            1.5e10,
        )
        mixed.append(grad_mixed)
        if group == 0:
            sums, low_slots, act_pair, gate_pair, down_pair, out_got = meet(
                sums, low_slots, act_pair, gate_pair, down_pair, out_got
            )
            pairs = [send(sums, order[0])]
            act_sums, gate_sums, down_sums = add(act_pair), add(gate_pair), add(down_pair)
            for bit, gate_bit in zip(order[2:-1], gate_order[2:-1]):
                act_sums, gate_sums = add(send(act_sums, bit)), add(send(gate_sums, gate_bit))
            act_pair, gate_pair = send(act_sums, order[-1]), send(gate_sums, gate_order[-1])
            down_pair = send(down_sums, order[1])
            result_parts = call(
                functools.partial(result_kernel, p=p),
                "result",
                piece,
                1,
                [],
                [out_near, out_got, residual],
                1e6,
            )
            low_slots, result_parts = meet(low_slots, result_parts)
        else:
            sums, pairs, act_pair, gate_pair, down_pair = meet(
                sums, pairs, act_pair, gate_pair, down_pair
            )
            pairs = pairs + [send(sums, order[0])]

    back_order = order[::-1]

    def step_of(sums):
        return order[ctx.bit_length() - sums.shape[0].bit_length()]

    in_small = jnp.stack([add(act_pair)[0], add(gate_pair)[0]], axis=1)
    down_sums = add(down_pair)
    for bit in order[2:-1]:
        down_sums = add(send(down_sums, bit))
    down_pair = send(down_sums, order[-1])
    early, late = pairs[:-1], pairs[-1]
    if early:
        sums = add(early[0])
        early = [send(sums, step_of(sums))]
    u1_parts = call(
        functools.partial(spread_kernel, p=p),
        "spread",
        [tile] * fsdp,
        fsdp,
        [pltpu.VMEM((own, width), bf16)],
        mixed + [w_qkv_cols],
        2e9,
    )
    in_small = lax.all_to_all(in_small, "fsdp", 0, 0, tiled=True)
    in_small = in_small.transpose(2, 1, 0, 3).reshape(1, small, 2 * fsdp * units)
    u1_parts, early, late, in_small = meet(list(u1_parts), early, late, in_small)
    u1 = reduce(u1_parts)
    if early:
        sums = add(early[0])
        early = [send(sums, step_of(sums))]
    sums = add(late)
    late = send(sums, step_of(sums))
    u1, early, late, down_pair = meet(u1, early, late, down_pair)
    back_parts = call(
        functools.partial(last_kernel, p=p),
        "last",
        piece,
        1,
        [],
        hidden_parts + list(u1) + [grad_residual],
        1e6,
    )
    sums = add(late)
    late = send(sums, step_of(sums))
    down = grow(add(down_pair), back_order[0])
    late, down, in_small, result_parts = meet(late, down, in_small, result_parts)
    out_back = undeal(result_parts)

    def finished(pair):
        sums = add(pair)
        while sums.shape[0] > 1:
            sums = add(send(sums, step_of(sums)))
        return sums

    sums = jnp.concatenate([finished(pair) for pair in early + [late]], axis=0)
    in_pair = grow(in_small, back_order[0])
    back = undeal(back_parts)
    down = grow(join(down), back_order[1])
    mine = sums[:, : 3 * fsdp * small].reshape(p.groups, fsdp, 3 * small, p.lanes)
    mine = lax.all_to_all(mine, "fsdp", 1, 1, tiled=True)
    mine = mine.reshape(p.groups, 3 * fsdp * small, p.lanes)
    stack = jnp.concatenate([mine, sums[:, 3 * fsdp * small :]], axis=1)[None]
    last_back = p.last_order[::-1]
    stack = grow(stack, last_back[0])
    stack, in_pair, down, back = meet(stack, in_pair, down, back)
    stack = grow(join(stack), last_back[1])
    in_pair = grow(join(in_pair), back_order[1])
    down = grow(join(down), back_order[2])
    for bit in back_order[3:]:
        down = grow(join(down), bit)
    stack, in_pair, down = meet(stack, in_pair, down)
    mlp_stack = join(down)
    for bit in back_order[2:]:
        in_pair = grow(join(in_pair), bit)
    for bit in last_back[2:]:
        stack = grow(join(stack), bit)
    out, back = assemble(out_back), assemble(back).astype(f32)

    grad_qkv, grad_out, grad_gain_a = call(
        functools.partial(qkv_grad_kernel, p=p),
        "qkv_grad",
        [
            shape_of((rows, 3 * width), f32),
            shape_of((cols, width), f32),
            shape_of((1, rows), f32),
        ],
        1,
        [
            pltpu.VMEM((ctx, p.groups, 4 * fsdp * small, p.lanes), bf16),
            pltpu.SemaphoreType.DMA((2,)),
        ],
        [Late(stack[0]), Late(stack[1]), w_qkv, gain_a, here],
        1e6,
    )

    wide_in = 2 * fsdp * units

    def in_grads(table, sums, block, before):
        some = pl.BlockSpec((block, wide_in), lambda s, t: (t[s], 0))
        any_spec = pl.BlockSpec(memory_space=pl.ANY)
        small_out = pl.BlockSpec((1, 1, block), lambda s, t: (t[s], 0, 0))
        return pl.pallas_call(
            in_grad_kernel,
            grid_spec=pltpu.PrefetchScalarGridSpec(
                num_scalar_prefetch=1,
                grid=(sums.shape[0],),
                in_specs=[
                    pl.BlockSpec((1, block, wide_in), lambda s, t: (s, 0, 0)),
                    some,
                    pl.BlockSpec((block, 1), lambda s, t: (t[s], 0)),
                ]
                + [any_spec] * len(before),
                out_specs=[some, small_out],
            ),
            out_shape=[
                shape_of(w_in.shape, f32),
                shape_of((rows // block, 1, block), f32),
            ],
            input_output_aliases={4 + k: k for k in range(len(before))},
            compiler_params=pltpu.CompilerParams(vmem_limit_bytes=40 << 20),
            cost_estimate=pl.CostEstimate(
                flops=1000000, bytes_accessed=8 * w_in.size, transcendentals=0
            ),
            name="in_grad",
        )(table, sums, w_in, gain_m, *before)

    if small % 8:
        parts = join(in_pair)
        parts = [
            lax.dynamic_slice_in_dim(parts, storage(c ^ cc, order), 1, 0) for cc in range(ctx)
        ]
        parts = jnp.concatenate(parts, axis=1)
        grad_in, grad_gain_m = in_grads(jnp.zeros((1,), jnp.int32), parts, rows, [])
    else:
        place_of = {storage(x, order): x for x in range(ctx)}
        table = jnp.stack([c ^ place_of[at] for at in range(ctx)])
        top = ctx // 2
        before = in_grads(table[:top], in_pair[0], small, [])
        grad_in, grad_gain_m = in_grads(table[top:], in_pair[1], small, list(before))
    (grad_mlp_out,) = call(
        functools.partial(out_grad_kernel, p=p),
        "out_grad",
        [shape_of((units, width), f32)],
        1,
        [],
        [mlp_stack, here],
        1e6,
    )
    return (
        out,
        back,
        grad_qkv,
        grad_out,
        grad_in,
        grad_mlp_out,
        grad_gain_a.reshape(rows),
        grad_gain_m.reshape(rows),
    )


def solution(mesh):
    in_specs = (
        P("fsdp", "ctx", None),
        P("fsdp", "ctx"),
        P("fsdp", "ctx", None),
        P("fsdp", None),
        P("fsdp", None),
        P("fsdp", None),
        P("fsdp", None),
        P("fsdp"),
        P("fsdp"),
    )
    out_specs = (
        P("fsdp", "ctx", None),
        P("fsdp", "ctx", None),
        P("fsdp", None),
        P("fsdp", None),
        P("fsdp", None),
        P("fsdp", None),
        P("fsdp"),
        P("fsdp"),
    )
    return jax.shard_map(
        on_device, mesh=mesh, in_specs=in_specs, out_specs=out_specs, check_vma=False
    )
```

```python
import functools

import jax
import jax.numpy as jnp
from jax import lax
from jax.experimental import pallas as pl
from jax.experimental.pallas import tpu as pltpu
from jax.sharding import PartitionSpec as P

HEADS = 16
rope_base = 160000.0
norm_eps = 1e-05
masked_score = -1e30
bf16 = jnp.bfloat16
f32 = jnp.float32
NT = (((1,), (1,)), ((), ()))
NN = (((1,), (0,)), ((), ()))
TN = (((0,), (0,)), ((), ()))
TAG = 16


def mm(a, b, dims=NN):
    return lax.dot_general(a, b, dims, preferred_element_type=f32)


class Late:
    def __init__(self, value):
        self.value = self.shape_is = value


def copies(pairs, sems):
    return [pltpu.make_async_copy(a, b, sems.at[k]) for k, (a, b) in enumerate(pairs)]


def call(kernel, name, out_shape, grid, scratch, args, flops, limit=56):
    def spec(a):
        if isinstance(a, tuple):
            return a[1]
        if isinstance(a, Late):
            return pl.BlockSpec(memory_space=pl.ANY)
        if a.dtype == jnp.int32:
            return pl.BlockSpec(memory_space=pltpu.SMEM)
        return pl.BlockSpec(
            a.shape, lambda s, nd=len(a.shape): (0,) * nd, pipeline_mode=pl.Buffered(1)
        )

    specs = [spec(a) for a in args]
    args = [a[0] if isinstance(a, tuple) else getattr(a, "value", a) for a in args]
    outs = [spec(a) for a in out_shape]
    out_shape = [a[0] if isinstance(a, tuple) else getattr(a, "shape_is", a) for a in out_shape]
    moved = sum(a.size * a.dtype.itemsize for a in args)
    moved += sum(a.size * a.dtype.itemsize for a in out_shape)
    return pl.pallas_call(
        kernel,
        grid=(grid,),
        in_specs=specs,
        out_specs=outs,
        out_shape=out_shape,
        scratch_shapes=scratch,
        compiler_params=pltpu.CompilerParams(vmem_limit_bytes=limit << 20),
        cost_estimate=pl.CostEstimate(
            flops=int(flops), bytes_accessed=int(moved), transcendentals=0
        ),
        name=name,
    )(*args)


def shape_of(shape, dtype=bf16):
    return jax.ShapeDtypeStruct(shape, dtype)


def head_mask(shape, head, size):
    return lax.broadcasted_iota(jnp.int32, shape, 1) // size == head


def swap(values, size):
    width, half = values.shape[1], size // 2
    if width == size:
        return jnp.concatenate([values[:, half:], values[:, :half]], axis=1)
    lane = lax.broadcasted_iota(jnp.int32, values.shape, 1) % size
    return jnp.where(
        lane < half, pltpu.roll(values, width - half, 1), pltpu.roll(values, half, 1)
    )


def norm_stats(values):
    center = values - jnp.mean(values, axis=-1, keepdims=True)
    rate = lax.rsqrt(jnp.mean(center * center, axis=-1, keepdims=True) + norm_eps)
    return center * rate, rate


def norm_back(grad, unit, rate):
    return rate * (
        grad
        - jnp.mean(grad, axis=-1, keepdims=True)
        - unit * jnp.mean(grad * unit, axis=-1, keepdims=True)
    )


class Plan:
    def __init__(self, fsdp, ctx, batch, span, width, units, rows):
        self.fsdp, self.ctx, self.span, self.width = fsdp, ctx, span, width
        self.pieces = ctx // fsdp
        self.n = batch // self.pieces
        self.part = self.pieces * span
        self.own = self.n * self.part
        self.length = span * ctx
        self.heads = HEADS // fsdp
        self.size = width // HEADS
        self.cols = self.heads * self.size
        self.units, self.rows = units, rows
        self.padded = -(-units // 256) * 256
        self.small = rows // ctx
        self.groups = 2 if self.heads % 2 == 0 else 1
        self.lanes = self.cols // self.groups
        self.slab = self.lanes // ctx
        self.table = min(128, self.cols)
        bits = [1 << b for b in range(ctx.bit_length() - 1)]
        self.order = bits
        self.last_order = bits[1:] + bits[:1]

    def locations(self):
        return [
            (i, j, (i * self.pieces + j) * self.span)
            for i in range(self.n)
            for j in range(self.pieces)
        ]


def storage(x, order):
    at = 0
    for bit in order:
        at = at * 2 + x // bit % 2
    return at


def cut_kernel(w, gain, at_ref, mine, other, *, p, feed):
    half, here = p.rows // 2, at_ref[0]
    side = at_ref[1] % 2
    near = pl.ds(pl.multiple_of(side * half, half), half)
    far = pl.ds(pl.multiple_of((1 - side) * half, half), half)
    size = p.units if feed else p.cols
    if feed and p.padded != size:
        mine[:, :, size:] = jnp.zeros((p.fsdp, 2 * half, p.padded - size), bf16)
        other[:, :, size:] = jnp.zeros((2, 2 * half, p.padded - size), bf16)
    for t in range(p.fsdp):
        o = t ^ here
        for m in range(2 if feed else 3):
            at = (m * p.fsdp + t) * size
            if feed:
                there = slice(m * half, (m + 1) * half), slice(0, size)
            else:
                there = slice(None), slice(m * size, (m + 1) * size)
            value = w[near, at : at + size].astype(f32) * gain[near, :]
            mine[(o,) + there] = value.astype(bf16)

            @pl.when(o < 2)
            def _(at=at, there=there, o=o):
                value = w[far, at : at + size].astype(f32) * gain[far, :]
                other[(o,) + there] = value.astype(bf16)


def unit_kernel(*refs, p):
    pieces, unit = refs[:-1], refs[-1]
    unit[p.own :, :] = jnp.zeros((TAG, p.width), bf16)
    for i, j, at in p.locations():
        ref = pieces[j]
        value, _ = norm_stats(ref[i, : p.span].astype(f32))
        unit[at : at + p.span] = value.astype(bf16)
        unit[p.own :, at : at + p.span] = ref[i, p.span :, : p.span]


def project_kernel(*refs, p):
    fs, gs = p.fsdp, p.part
    xs, rest = refs[:fs], refs[fs:]
    near, other, rest = rest[:fs], rest[fs : 2 * fs], rest[2 * fs :]
    cos, sin, at_ref, q_ref, k_ref, v_ref, seg_ref, w, x, w_sems, x_sems = rest
    step = pl.program_id(0)
    scale = p.size**-0.5
    half, side = p.rows // 2, at_ref[1] % 2
    pairs = []
    for o in range(fs):
        base = (at_ref[0] ^ o) * 2
        for part, at in ((near[o], base + side), (other[o], base + 1 - side)):
            pairs.append((part, w.at[pl.ds(pl.multiple_of(at * half, half), half), :]))
    w_copies = copies(pairs, w_sems)
    x_copies = copies([(xs[o], x.at[o]) for o in range(fs)], x_sems)

    @pl.when(step == 0)
    def _():
        for copy in x_copies[:1] + w_copies + x_copies[1:]:
            copy.start()
        for copy in w_copies:
            copy.wait()

    for o in range(fs):

        @pl.when(step == o)
        def _(o=o):
            x_copies[o].wait()
            for i in range(p.n):
                tag = x[o, p.own : p.own + TAG, i * gs : (i + 1) * gs].astype(f32)
                seg_ref[i, :, o * gs : (o + 1) * gs] = tag[:8]

    mixed = mm(x[step, : p.own], w[...])
    rows = pl.ds(pl.multiple_of(step * gs, gs), gs)
    reps = p.cols // p.table
    cosine = jnp.concatenate([cos[rows, :]] * reps, axis=1)
    sine = jnp.concatenate([sin[rows, :]] * reps, axis=1)
    for i in range(p.n):
        own = mixed[i * gs : (i + 1) * gs]
        query, key = own[:, : p.cols], own[:, p.cols : 2 * p.cols]
        query = (query * cosine + swap(query, p.size) * sine) * scale
        q_ref[i, rows, :] = query.astype(bf16)
        k_ref[i, rows, :] = (key * cosine + swap(key, p.size) * sine).astype(bf16)
        v_ref[i, rows, :] = own[:, 2 * p.cols :].astype(bf16)


def attend_kernel(q_ref, k_ref, v_ref, seg_ref, wo, *rest, p):
    fs, gs = p.fsdp, p.part
    parts, (att_ref, norm_ref, made) = rest[:fs], rest[fs:]
    step = pl.program_id(0)
    i, o = step // fs, step % fs
    rows = pl.ds(pl.multiple_of(o * gs, gs), gs)
    q, k, v = q_ref[i, rows, :], k_ref[i], v_ref[i]
    allowed = seg_ref[i, :, rows].T[:, :1] == seg_ref[i, :1, :]
    attended = jnp.zeros(q.shape, f32)
    norms = jnp.zeros((gs, 128), f32)
    lane = lax.broadcasted_iota(jnp.int32, norms.shape, 1)
    for head in range(p.heads):
        here = head_mask(q.shape, head, p.size)
        scores = mm(jnp.where(here, q, jnp.zeros_like(q)), k, NT)
        scores = jnp.where(allowed, scores, masked_score)
        peak = jnp.max(scores, axis=1, keepdims=True)
        weights = jnp.exp(scores - peak)
        total = jnp.sum(weights, axis=1, keepdims=True)
        attended = jnp.where(here, mm(weights.astype(bf16), v) / total, attended)
        norms = jnp.where(lane == head, peak + jnp.log(total), norms)
    norm_ref[i, :, rows] = norms.T[:8]
    attended = attended.astype(bf16)
    att_ref[i, rows, :] = attended
    made[...] = mm(attended, wo[...]).astype(bf16)
    for oo in range(fs):

        @pl.when(o == oo)
        def _(oo=oo):
            parts[oo][pl.ds(pl.multiple_of(i * gs, gs), gs), :] = made[...]


def flip_kernel(*refs, p):
    xs, out = refs[:-1], refs[-1]
    gs = p.part
    for o in range(p.fsdp):

        @pl.when(pl.program_id(0) == o)
        def _(o=o):
            for i in range(p.n):
                out[i, :, o * gs : (o + 1) * gs] = xs[o][i * gs : (i + 1) * gs, :].T


def shares(span_ref, i, a, b, fs):
    one, two = (i * fs + a) * 2, (i * fs + b) * 2
    return jnp.logical_and(
        span_ref[one] <= span_ref[two + 1], span_ref[two] <= span_ref[one + 1]
    )


def backward_kernel(*refs, p, group):
    fs, gs, cols = p.fsdp, p.part, p.lanes
    gls, rest = refs[:fs], refs[fs:]
    xt, wo, rest = rest[0], rest[1], rest[2:]
    q_ref, k_ref, v_ref, att_ref, seg_ref, norm_ref, cos, sin, c_ref, span_ref = rest[:10]
    gm, sums, kt, dqt, dk, dv, gl, seg_col, sum_qkv, sum_out, flat, sems, flat_sem = rest[10:]
    step = pl.program_id(0)
    scale = p.size**-0.5
    reps = cols // p.table

    def turned(grad, rows):
        cosine = jnp.concatenate([cos[rows, :]] * reps, axis=1)
        sine = jnp.concatenate([sin[rows, :]] * reps, axis=1)
        return grad * cosine - swap(grad, p.size) * sine

    pairs = [
        (gls[o].at[i * gs : (i + 1) * gs], gl.at[i, o * gs : (o + 1) * gs])
        for i in range(p.n)
        for o in range(fs)
    ]
    low_copies = copies(pairs, sems)
    flat_copy = pltpu.make_async_copy(xt, flat, flat_sem.at[0])

    @pl.when(step == 0)
    def _():
        for copy in low_copies:
            copy.start()
        flat_copy.start()

    @pl.when(step < p.n * fs)
    def _():
        i, o = step // fs, step % fs
        rows = pl.ds(pl.multiple_of(o * gs, gs), gs)
        for k in range(p.n * fs):

            @pl.when(step == k)
            def _(k=k):
                low_copies[k].wait()

        q = q_ref[i, rows, :]

        @pl.when(o == 0)
        def _():
            kt[...] = k_ref[i].T
            dk[...] = jnp.zeros_like(dk)
            dv[...] = jnp.zeros_like(dv)
            seg_col[...] = seg_ref[i].T[:, :1]

        attended = att_ref[i, rows, :]
        g = mm(gl[i, rows, :], wo[...], NT).astype(bf16)
        count = p.heads // p.groups
        picks = lax.broadcasted_iota(jnp.int32, (8, cols), 0)
        picks = (lax.broadcasted_iota(jnp.int32, (8, cols), 1) // p.size == picks).astype(f32)
        deltas = lax.dot_general(
            picks,
            g.astype(f32) * attended.astype(f32),
            NT,
            precision=lax.Precision.HIGHEST,
            preferred_element_type=f32,
        )
        zero = jnp.zeros_like(q)
        masks = [head_mask(q.shape, h, p.size) for h in range(count)]
        own_q = [jnp.where(mask, q, zero) for mask in masks]
        own_g = [jnp.where(mask, g, zero) for mask in masks]
        mine = seg_ref[i, :1, rows]
        dqt[...] = jnp.zeros_like(dqt)
        for kk in range(fs):
            keys = slice(kk * gs, (kk + 1) * gs)

            @pl.when(shares(span_ref, i, o, kk, fs))
            def _(keys=keys):
                k, v = k_ref[i, keys, :], v_ref[i, keys, :]
                allowed = seg_col[keys, :] == mine
                for h in range(count):
                    first = group * count + h
                    scores = jnp.where(allowed, mm(k, own_q[h], NT), masked_score)
                    probs = jnp.exp(scores - norm_ref[i, first : first + 1, rows])
                    grad = mm(v, own_g[h], NT)
                    grad = (probs * (grad - deltas[h : h + 1, :])).astype(bf16)
                    dv[keys, :] += mm(probs.astype(bf16), own_g[h])
                    dk[keys, :] += mm(grad, own_q[h])
                    at = slice(h * p.size, (h + 1) * p.size)
                    dqt[at, :] += mm(kt[at, keys], grad)

        gm[i, rows, :cols] = (turned(dqt[...].T, rows) * scale).astype(bf16)

        @pl.when(o == fs - 1)
        def _():
            gm[i, :, cols : 2 * cols] = turned(dk[...], slice(None)).astype(bf16)
            gm[i, :, 2 * cols :] = dv[...].astype(bf16)

    @pl.when(step == p.n * fs)
    def _():
        flat_copy.wait()
        total = [mm(flat[i], gm[i]) for i in range(p.n)]
        sum_qkv[...] = sum(total[1:], total[0])
        total = [mm(att_ref[i].T, gl[i]) for i in range(p.n)]
        sum_out[...] = sum(total[1:], total[0])
        small, slab = p.small, p.slab
        for cc in range(p.ctx):
            away = storage(c_ref[0] ^ cc, p.order)
            for ff in range(fs):
                for m in range(3):
                    part = sum_qkv[
                        ff * p.rows + cc * small : ff * p.rows + (cc + 1) * small,
                        m * cols : (m + 1) * cols,
                    ]
                    at = (ff * 3 + m) * small
                    sums[away, at : at + small, :] = part.astype(bf16)
            for d in range(p.width // cols):
                part = sum_out[cc * slab : (cc + 1) * slab, d * cols : (d + 1) * cols]
                at = 3 * fs * small + d * slab
                sums[away, at : at + slab, :] = part.astype(bf16)


def spread_kernel(*refs, p):
    gms, w, parts, made = refs[: p.groups], refs[p.groups], refs[p.groups + 1 : -1], refs[-1]
    o, lanes = pl.program_id(0), p.lanes
    rows = pl.ds(pl.multiple_of(o * p.part, p.part), p.part)
    for i in range(p.n):
        grad = jnp.concatenate(
            [gm[i, rows, m * lanes : (m + 1) * lanes] for m in range(3) for gm in gms], axis=1
        )
        made[i * p.part : (i + 1) * p.part] = mm(grad, w[...], NT).astype(bf16)
    for oo in range(p.fsdp):

        @pl.when(o == oo)
        def _(oo=oo):
            parts[oo][...] = made[...]


def mlp_kernel(*refs, p):
    fs, units, pad = p.fsdp, p.units, p.padded
    xs, cs, rest = refs[:fs], refs[fs : 2 * fs], refs[2 * fs :]
    near, other, rest = rest[:fs], rest[fs : 2 * fs], rest[2 * fs :]
    w_out, at_ref, rest = rest[0], rest[1], rest[2:]
    outs, us, rest = rest[:fs], rest[fs : 2 * fs], rest[2 * fs :]
    act_ref, da_ref, dg_ref, wa, wg, wm, x, ct, made, made_u, w_sems, sems, out_sems = rest
    step = pl.program_id(0)
    half, side = p.rows // 2, at_ref[1] % 2
    pairs = []
    for o in range(fs):
        base = (at_ref[0] ^ o) * 2
        for part, at in ((near[o], base + side), (other[o], base + 1 - side)):
            at = pl.ds(pl.multiple_of(at * half, half), half)
            pairs.append((part.at[:half], wa.at[at, :]))
            pairs.append((part.at[half:], wg.at[at, :]))
    w_copies = copies(pairs, w_sems)
    pairs = []
    for o in range(fs):
        pairs += [(xs[o], x.at[o]), (cs[o], ct.at[o])]
    x_copies = copies(pairs, sems)
    pairs = []
    for o in range(fs):
        pairs += [(made.at[o], outs[o]), (made_u.at[o], us[o])]
    out_copies = copies(pairs, out_sems)

    @pl.when(step == 0)
    def _():
        for copy in x_copies[:1] + w_copies + x_copies[1:]:
            copy.start()
        if pad != units:
            wm[units:, :] = jnp.zeros((pad - units, p.width), bf16)
        wm[:units, :] = w_out[...]
        for copy in w_copies:
            copy.wait()

    for o in range(fs):

        @pl.when(step == o)
        def _(o=o):
            x_copies[2 * o].wait()
            x_copies[2 * o + 1].wait()

    act, gate = mm(x[step], wa[...]), mm(x[step], wg[...])
    phi = 0.5 * (1.0 + lax.erf(act * (2.0**-0.5)))
    gelu = act * phi
    active = (gelu * gate).astype(bf16)
    made[step] = mm(active, wm[...]).astype(bf16)
    grad = mm(ct[step], wm[...], NT)
    slope = phi + act * (jnp.exp(-0.5 * act * act) * 0.3989422804014327)
    da, dg = (grad * gate * slope).astype(bf16), (grad * gelu).astype(bf16)
    made_u[step] = (mm(da, wa[...], NT) + mm(dg, wg[...], NT)).astype(bf16)
    act_ref[...], da_ref[...], dg_ref[...] = active, da, dg
    for o in range(fs):

        @pl.when(step == o)
        def _(o=o):
            out_copies[2 * o].start()
            out_copies[2 * o + 1].start()

    @pl.when(step == fs - 1)
    def _():
        for copy in out_copies:
            copy.wait()


def mlp_sums_kernel(*refs, p):
    fs, units = p.fsdp, p.units
    xs, cs, rest = refs[:fs], refs[fs : 2 * fs], refs[2 * fs :]
    act_ref, da_ref, dg_ref, c_ref, one, two, three, sa, sg, sm, x, ct = rest
    step = pl.program_id(0)

    @pl.when(step == 0)
    def _():
        sa[...] = jnp.zeros_like(sa)
        sg[...] = jnp.zeros_like(sg)
        sm[...] = jnp.zeros_like(sm)

    for o in range(fs):

        @pl.when(step == o)
        def _(o=o):
            x[...] = xs[o][...]
            ct[...] = cs[o][...]

    rows = pl.ds(pl.multiple_of(step * p.own, p.own), p.own)
    sa[...] += mm(x[...], da_ref[rows, :], TN)
    sg[...] += mm(x[...], dg_ref[rows, :], TN)
    sm[...] += mm(ct[...], act_ref[rows, :], TN)

    @pl.when(step == fs - 1)
    def _():
        for cc in range(p.ctx):
            away = storage(c_ref[0] ^ cc, p.order)
            late = storage(c_ref[0] ^ cc, p.last_order)
            for ff in range(fs):
                at = slice(ff * p.rows + cc * p.small, ff * p.rows + (cc + 1) * p.small)
                one[away, ff] = sa[at, :units].astype(bf16)
                two[late, ff] = sg[at, :units].astype(bf16)
                three[away, ff] = sm[at, :units].astype(bf16)


def middle_kernel(*refs, p):
    g = p.pieces
    hidden, (a, b, c), (residual, unit) = refs[:g], refs[g : g + 3], refs[g + 3 :]
    for i, j, at in p.locations():
        rows = slice(at, at + p.span)
        total = a[rows].astype(f32) + b[rows].astype(f32) + c[rows].astype(f32)
        total = total + hidden[j][i, : p.span].astype(f32)
        residual[rows] = total
        unit[rows] = norm_stats(total)[0].astype(bf16)


def turn_kernel(a, b, c, residual, cot, grad, low, *, p):
    for _, _, at in p.locations():
        rows = slice(at, at + p.span)
        u = a[rows].astype(f32) + b[rows].astype(f32) + c[rows].astype(f32)
        unit, rate = norm_stats(residual[rows])
        total = cot[rows].astype(f32) + norm_back(u, unit, rate)
        grad[rows] = total
        low[rows] = total.astype(bf16)


def result_kernel(*refs, p):
    (a, b, residual), outs = refs[:3], refs[3:]
    for i, j, at in p.locations():
        rows = slice(at, at + p.span)
        total = a[rows].astype(f32) + b[rows].astype(f32)
        outs[j][i] = (total + residual[rows]).astype(bf16)


def last_kernel(*refs, p):
    g = p.pieces
    hidden, (a, b, c, grad), outs = refs[:g], refs[g : g + 4], refs[g + 4 :]
    for i, j, at in p.locations():
        rows = slice(at, at + p.span)
        u = a[rows].astype(f32) + b[rows].astype(f32) + c[rows].astype(f32)
        unit, rate = norm_stats(hidden[j][i, : p.span].astype(f32))
        outs[j][i] = (grad[rows] + norm_back(u, unit, rate)).astype(bf16)


def row_sums(values):
    ones = jnp.ones((8, values.shape[1]), f32)
    total = lax.dot_general(
        ones, values, NT, precision=lax.Precision.HIGHEST, preferred_element_type=f32
    )
    return total[:1]


def qkv_grad_kernel(low, high, w, gain, c_ref, qkv, out, gain_grad, stack, sems, *, p):
    fs, small, slab, lanes = p.fsdp, p.small, p.slab, p.lanes
    top = low.shape[0]
    loads = copies([(low, stack.at[:top]), (high, stack.at[top:])], sems)
    for load in loads:
        load.start()
    for load in loads:
        load.wait()
    for cc in range(p.ctx):
        away = storage(c_ref[0] ^ cc, p.last_order)
        rows = slice(cc * small, (cc + 1) * small)
        scale = gain[rows, :]
        total = jnp.zeros((small, lanes), f32)
        for g in range(p.groups):
            for ff in range(fs):
                for m in range(3):
                    at = (ff * 3 + m) * small
                    value = stack[away, g, at : at + small, :].astype(f32)
                    there = m * p.width + ff * p.cols + g * lanes
                    qkv[rows, there : there + lanes] = value * scale
                    total = total + value * w[rows, there : there + lanes].astype(f32)
            for d in range(p.width // lanes):
                at = 3 * fs * small + d * slab
                value = stack[away, g, at : at + slab, :].astype(f32)
                row = g * lanes + cc * slab
                out[row : row + slab, d * lanes : (d + 1) * lanes] = value
        gain_grad[:, rows] = row_sums(total)


def in_grad_kernel(table, sums, w, gain, *rest):
    grad, gain_grad = rest[-2:]
    value = sums[0].astype(f32)
    grad[...] = value * gain[...]
    total = jnp.zeros((value.shape[0], 128), f32)
    for at in range(0, value.shape[1], 128):
        total = total + value[:, at : at + 128] * w[:, at : at + 128].astype(f32)
    gain_grad[0] = row_sums(total)


def out_grad_kernel(stack, c_ref, grad, *, p):
    for cc in range(p.ctx):
        away = storage(c_ref[0] ^ cc, p.order)
        for ff in range(p.fsdp):
            at = ff * p.rows + cc * p.small
            grad[:, at : at + p.small] = stack[away, ff].astype(f32).T


def on_device(
    hidden, segment_ids, cotangent, w_qkv, w_attn_out, w_in, w_mlp_out, gain_attn, gain_mlp
):
    fsdp, ctx = lax.axis_size("fsdp"), lax.axis_size("ctx")
    f, c = lax.axis_index("fsdp"), lax.axis_index("ctx")
    batch, span, width = hidden.shape
    p = Plan(fsdp, ctx, batch, span, width, w_mlp_out.shape[0], w_in.shape[0])
    n, own, cols, units, rows, small = p.n, p.own, p.cols, p.units, p.rows, p.small
    length, pieces = p.length, p.pieces
    both = ("ctx", "fsdp")
    slots = range(fsdp)
    tile = shape_of((own, width))
    bits = [fsdp >> 1 + b for b in range(fsdp.bit_length() - 1)]

    def mixed_bits(index):
        out = 0
        for bit in bits:
            out = out + index // (fsdp // 2 // bit) % 2 * bit
        return out

    def route(j):
        pairs = []
        for cc in range(ctx):
            for ff in range(fsdp):
                to_c = (cc + j) % pieces * fsdp + mixed_bits(ff)
                to_f = cc // pieces ^ ff % 2 * (fsdp // 2)
                pairs.append((cc * fsdp + ff, to_c * fsdp + to_f))
        return pairs

    def dealt(values):
        return [
            lax.dynamic_slice_in_dim(values, (c + j) % pieces * n, n, 0) for j in range(pieces)
        ]

    def deal(parts):
        return [lax.ppermute(part, both, route(j)) for j, part in enumerate(parts)]

    def undeal(parts):
        back = [
            lax.ppermute(part, both, [(b, a) for a, b in route(j)])
            for j, part in enumerate(parts)
        ]
        return back

    def assemble(back):
        if pieces == 1:
            return back[0]
        blocks = []
        for b in range(pieces):
            block = back[0]
            for j in range(1, pieces):
                block = jnp.where((c + j) % pieces == b, back[j], block)
            blocks.append(block)
        return jnp.concatenate(blocks, axis=0)

    def partner(values, bit):
        return lax.ppermute(values, "fsdp", [(i, i ^ bit) for i in range(fsdp)])

    def meet(*values):
        return lax.optimization_barrier(values)

    def first_hop(value):
        return [value, partner(value, bits[0])]

    def later_hops(held):
        held = {0: held[0], bits[0]: held[1]}
        for bit in bits[1:]:
            for o in list(held):
                held[o ^ bit] = partner(held[o], bit)
        return [held[o] for o in slots]

    def reduce(parts):
        held, side, last = dict(enumerate(parts)), None, None
        for bit in reversed(bits):
            for o in sorted(held, reverse=True):
                if not o & bit:
                    continue
                got, mine = partner(held.pop(o), bit), held[o ^ bit]
                if o == bits[0]:
                    last = got
                elif o == bits[1]:
                    side = got
                else:
                    held[o ^ bit] = (mine.astype(f32) + got.astype(f32)).astype(bf16)
        return held[0], side, last

    def away(values, bit):
        return lax.ppermute(values, "ctx", [(i, i ^ bit) for i in range(ctx)])

    def send(stack, bit):
        half = stack.shape[0] // 2
        return stack[:half], away(stack[half:], bit)

    def add(pair):
        return (pair[0].astype(f32) + pair[1].astype(f32)).astype(bf16)

    def grow(stack, bit):
        return stack, away(stack, bit)

    def join(pair):
        return jnp.concatenate(pair, axis=0)

    flip = c % fsdp // (fsdp // 2) * (fsdp // 2)
    blocks = [
        (f ^ o ^ flip) * pieces + (c // fsdp - j) % pieces for o in slots for j in range(pieces)
    ]
    positions = (jnp.stack(blocks)[:, None] * span + jnp.arange(span)[None, :]).reshape(length)
    turns = p.size // 2
    inverse = rope_base ** (-(jnp.arange(turns, dtype=f32) * 2.0 / p.size))
    angles = positions.astype(f32)[:, None] * inverse[None, :]
    cosine, sine = jnp.cos(angles), jnp.sin(angles)
    reps = p.table // p.size
    cosine = jnp.concatenate([cosine, cosine] * reps, axis=1)
    sine = jnp.concatenate([-sine, sine] * reps, axis=1)

    tags = jnp.pad(
        segment_ids.astype(bf16)[:, None, :], ((0, 0), (0, TAG - 1), (0, width - span))
    )
    hidden_cut, w_qkv, w_in = lax.optimization_barrier(
        (dealt(jnp.concatenate([hidden, tags], axis=1)), w_qkv, w_in)
    )
    hidden_parts = deal(hidden_cut)

    gain_a, gain_m = gain_attn.astype(f32)[:, None], gain_mlp.astype(f32)[:, None]
    here, place = jnp.reshape(c, (1,)), jnp.stack([f, c])
    half = rows // 2
    mine, other = call(
        functools.partial(cut_kernel, p=p, feed=False),
        "cut",
        [shape_of((fsdp, half, 3 * cols)), shape_of((2, half, 3 * cols))],
        1,
        [],
        [w_qkv, gain_a, place],
        1e6,
    )

    def spread_out(mine, other):
        near = [mine[0]] + [
            lax.ppermute(mine[o], "fsdp", [(i, i ^ o) for i in range(fsdp)]) for o in slots[1:]
        ]
        return near, [other[0], partner(other[1], 1)]

    near, other = spread_out(mine, other)
    hidden_parts, near, other, cosine, sine, cotangent, w_in = meet(
        hidden_parts, near, other, cosine, sine, cotangent, w_in
    )
    far = [away(part, 1) for part in near[2:]]
    cot_parts = deal(dealt(cotangent))
    unit1 = call(
        functools.partial(unit_kernel, p=p),
        "unit1",
        [shape_of((own + TAG, width))],
        1,
        [],
        hidden_parts,
        1e6,
    )[0]
    unit1, w_in_late = meet(unit1, w_in)
    mine_in, kept_in = call(
        functools.partial(cut_kernel, p=p, feed=True),
        "cut_in",
        [shape_of((fsdp, rows, p.padded)), shape_of((2, rows, p.padded))],
        1,
        [],
        [w_in_late, gain_m, place],
        1e6,
    )
    held, far, cot_parts, mine_in, kept_in = meet(
        first_hop(unit1), far, cot_parts, mine_in, kept_in
    )
    unit1_slots = later_hops(held)
    cot_own = jnp.stack(cot_parts, axis=1).reshape(own, width)
    unit1_slots, cot_own, mine_in, kept_in = meet(unit1_slots, cot_own, mine_in, kept_in)
    cot_held = first_hop(cot_own)
    near_in, other_in = spread_out(mine_in, kept_in)

    whole = shape_of((n, length, cols))
    q, k, v, segments, w_qkv_cols = call(
        functools.partial(project_kernel, p=p),
        "project",
        [whole] * 3 + [shape_of((n, 8, length), f32), shape_of((width, 3 * cols))],
        fsdp,
        [
            pltpu.VMEM((fsdp, own + TAG, width), bf16),
            pltpu.SemaphoreType.DMA((2 * fsdp,)),
            pltpu.SemaphoreType.DMA((fsdp,)),
        ],
        [Late(a) for a in unit1_slots + near + other + far] + [cosine, sine, place],
        4e9,
    )
    ranges = segments[:, 0].reshape(n, fsdp, p.part)
    spans = jnp.stack([jnp.min(ranges, axis=2), jnp.max(ranges, axis=2)], axis=2)
    spans = spans.astype(jnp.int32).reshape(2 * n * fsdp)
    made = call(
        functools.partial(attend_kernel, p=p),
        "attend",
        [tile] * fsdp + [whole, shape_of((n, 8, length), f32)],
        n * fsdp,
        [pltpu.VMEM((p.part, width), bf16)],
        [q, k, v, segments, w_attn_out],
        1.2e10,
    )
    made, cot_held, near_in, other_in = meet(made, cot_held, near_in, other_in)
    far_in = [away(part, 1) for part in near_in[2:]]
    cot_slots = later_hops(cot_held)
    attended_parts, attended, norms = made[:fsdp], made[fsdp], made[fsdp + 1]

    attended_parts = list(attended_parts)
    attended_parts[0], unit1_late = meet(attended_parts[0], unit1_slots)
    (flipped,) = call(
        functools.partial(flip_kernel, p=p),
        "flip",
        [shape_of((n, width, length))],
        fsdp,
        [],
        list(unit1_late),
        1e6,
    )
    addends = reduce(attended_parts)
    addends, flipped = meet(addends, flipped)
    residual, unit2 = call(
        functools.partial(middle_kernel, p=p),
        "middle",
        [shape_of((own, width), f32), tile],
        1,
        [],
        hidden_parts + list(addends),
        1e6,
    )
    unit2, far_in, cot_slots = meet(unit2, far_in, cot_slots)
    unit2_slots = later_hops(first_hop(unit2))

    wide = shape_of((fsdp * own, p.padded))
    made = call(
        functools.partial(mlp_kernel, p=p),
        "mlp",
        [Late(tile)] * (2 * fsdp)
        + [(wide, pl.BlockSpec((own, p.padded), lambda s: (s, 0)))] * 3,
        fsdp,
        [pltpu.VMEM((width, p.padded), bf16)] * 2
        + [pltpu.VMEM((p.padded, width), bf16)]
        + [pltpu.VMEM((fsdp, own, width), bf16)] * 4
        + [
            pltpu.SemaphoreType.DMA((4 * fsdp,)),
            pltpu.SemaphoreType.DMA((2 * fsdp,)),
            pltpu.SemaphoreType.DMA((2 * fsdp,)),
        ],
        [Late(a) for a in unit2_slots + cot_slots + near_in + other_in + far_in]
        + [w_mlp_out, place],
        1.2e10,
    )
    out_parts, u2_parts, (active, da, dg) = made[:fsdp], made[fsdp : 2 * fsdp], made[2 * fsdp :]

    u2 = reduce(u2_parts)
    act_sums, gate_sums, down_sums = call(
        functools.partial(mlp_sums_kernel, p=p),
        "mlp_sums",
        [shape_of((ctx, fsdp, small, units))] * 3,
        fsdp,
        [pltpu.VMEM((width, p.padded), f32)] * 3 + [pltpu.VMEM((own, width), bf16)] * 2,
        unit2_slots + cot_slots + [active, da, dg, here],
        6e9,
    )
    u2, act_sums, gate_sums, down_sums = meet(u2, act_sums, gate_sums, down_sums)
    grad_residual, grad_low = call(
        functools.partial(turn_kernel, p=p),
        "turn",
        [shape_of((own, width), f32), tile],
        1,
        [],
        list(u2) + [residual, cot_own],
        1e6,
    )
    order = p.order
    gate_order = p.last_order
    piece = [shape_of((n, span, width))] * pieces
    grad_low, out_parts, act_sums, gate_sums = meet(
        grad_low, list(out_parts), act_sums, gate_sums
    )
    low_held = first_hop(grad_low)
    act_pair, gate_pair = send(act_sums, order[0]), send(gate_sums, gate_order[0])
    held = dict(enumerate(out_parts))
    for bit in reversed(bits[1:]):
        for o in sorted(held, reverse=True):
            if o & bit:
                held[o ^ bit] = add((held[o ^ bit], partner(held.pop(o), bit)))
    low_held, out_near, out_far, act_pair, gate_pair = meet(
        low_held, held[0], held[bits[0]], act_pair, gate_pair
    )
    act_sums, gate_sums = add(act_pair), add(gate_pair)
    low_slots = later_hops(low_held)
    low_slots, out_far, act_sums, gate_sums, down_sums = meet(
        low_slots, out_far, act_sums, gate_sums, down_sums
    )
    act_pair, gate_pair = send(act_sums, order[1]), send(gate_sums, gate_order[1])
    down_pair = send(down_sums, order[0])
    out_got = partner(out_far, bits[0])
    mixed, attention_sums = [], []
    for group in range(p.groups):
        some = pl.BlockSpec(
            (n, length, p.lanes),
            lambda s, group=group: (0, 0, group),
            pipeline_mode=pl.Buffered(1),
        )
        wo_rows = pl.BlockSpec(
            (p.lanes, width), lambda s, group=group: (group, 0), pipeline_mode=pl.Buffered(1)
        )
        grad_mixed, sums = call(
            functools.partial(backward_kernel, p=p, group=group),
            "attention_back",
            [
                shape_of((n, length, 3 * p.lanes)),
                shape_of((ctx, 4 * fsdp * small, p.lanes)),
            ],
            n * fsdp + 1,
            [
                pltpu.VMEM((p.lanes, length), bf16),
                pltpu.VMEM((p.lanes, p.part), f32),
                pltpu.VMEM((length, p.lanes), f32),
                pltpu.VMEM((length, p.lanes), f32),
                pltpu.VMEM((n, length, width), bf16),
                pltpu.VMEM((length, 1), f32),
                pltpu.VMEM((width, 3 * p.lanes), f32),
                pltpu.VMEM((p.lanes, width), f32),
                pltpu.VMEM((n, width, length), bf16),
                pltpu.SemaphoreType.DMA((n * fsdp,)),
                pltpu.SemaphoreType.DMA((1,)),
            ],
            [Late(a) for a in low_slots]
            + [Late(flipped), (w_attn_out, wo_rows), (q, some), (k, some), (v, some), (attended, some)]
            + [segments, norms, cosine, sine, here, spans],
            1.5e10,
        )
        mixed.append(grad_mixed)
        if group == 0:
            sums, low_slots, act_pair, gate_pair, down_pair, out_got = meet(
                sums, low_slots, act_pair, gate_pair, down_pair, out_got
            )
            pairs = [send(sums, order[0])]
            act_sums, gate_sums, down_sums = add(act_pair), add(gate_pair), add(down_pair)
            for bit, gate_bit in zip(order[2:-1], gate_order[2:-1]):
                act_sums, gate_sums = add(send(act_sums, bit)), add(send(gate_sums, gate_bit))
            act_pair, gate_pair = send(act_sums, order[-1]), send(gate_sums, gate_order[-1])
            down_pair = send(down_sums, order[1])
        else:
            sums, pairs, act_pair, gate_pair, down_pair = meet(
                sums, pairs, act_pair, gate_pair, down_pair
            )
            pairs = pairs + [send(sums, order[0])]

    back_order = order[::-1]

    def step_of(sums):
        return order[ctx.bit_length() - sums.shape[0].bit_length()]

    in_small = jnp.stack([add(act_pair)[0], add(gate_pair)[0]], axis=1)
    down_sums = add(down_pair)
    for bit in order[2:-1]:
        down_sums = add(send(down_sums, bit))
    down_pair = send(down_sums, order[-1])
    early, late = pairs[:-1], pairs[-1]
    if early:
        sums = add(early[0])
        early = [send(sums, step_of(sums))]
    u1_parts = call(
        functools.partial(spread_kernel, p=p),
        "spread",
        [tile] * fsdp,
        fsdp,
        [pltpu.VMEM((own, width), bf16)],
        mixed + [w_qkv_cols],
        2e9,
    )
    in_small = lax.all_to_all(in_small, "fsdp", 0, 0, tiled=True)
    in_small = in_small.transpose(2, 1, 0, 3).reshape(1, small, 2 * fsdp * units)
    u1_parts, early, late, in_small = meet(list(u1_parts), early, late, in_small)
    u1 = reduce(u1_parts)
    if early:
        sums = add(early[0])
        early = [send(sums, step_of(sums))]
    sums = add(late)
    late = send(sums, step_of(sums))
    u1, early, late, down_pair, out_got = meet(u1, early, late, down_pair, out_got)
    result_parts = call(
        functools.partial(result_kernel, p=p),
        "result",
        piece,
        1,
        [],
        [out_near, out_got, residual],
        1e6,
    )
    back_parts = call(
        functools.partial(last_kernel, p=p),
        "last",
        piece,
        1,
        [],
        hidden_parts + list(u1) + [grad_residual],
        1e6,
    )
    sums = add(late)
    late = send(sums, step_of(sums))
    down = grow(add(down_pair), back_order[0])
    late, down, in_small, result_parts = meet(late, down, in_small, result_parts)
    out_back = undeal(result_parts)

    def finished(pair):
        sums = add(pair)
        while sums.shape[0] > 1:
            sums = add(send(sums, step_of(sums)))
        return sums

    sums = jnp.concatenate([finished(pair) for pair in early + [late]], axis=0)
    in_pair = grow(in_small, back_order[0])
    back = undeal(back_parts)
    down = grow(join(down), back_order[1])
    mine = sums[:, : 3 * fsdp * small].reshape(p.groups, fsdp, 3 * small, p.lanes)
    mine = lax.all_to_all(mine, "fsdp", 1, 1, tiled=True)
    mine = mine.reshape(p.groups, 3 * fsdp * small, p.lanes)
    stack = jnp.concatenate([mine, sums[:, 3 * fsdp * small :]], axis=1)[None]
    last_back = p.last_order[::-1]
    stack = grow(stack, last_back[0])
    stack, in_pair, down, back = meet(stack, in_pair, down, back)
    stack = grow(join(stack), last_back[1])
    in_pair = grow(join(in_pair), back_order[1])
    down = grow(join(down), back_order[2])
    for bit in back_order[3:]:
        down = grow(join(down), bit)
    stack, in_pair, down = meet(stack, in_pair, down)
    mlp_stack = join(down)
    for bit in back_order[2:]:
        in_pair = grow(join(in_pair), bit)
    for bit in last_back[2:]:
        stack = grow(join(stack), bit)
    out, back = assemble(out_back), assemble(back).astype(f32)

    grad_qkv, grad_out, grad_gain_a = call(
        functools.partial(qkv_grad_kernel, p=p),
        "qkv_grad",
        [
            shape_of((rows, 3 * width), f32),
            shape_of((cols, width), f32),
            shape_of((1, rows), f32),
        ],
        1,
        [
            pltpu.VMEM((ctx, p.groups, 4 * fsdp * small, p.lanes), bf16),
            pltpu.SemaphoreType.DMA((2,)),
        ],
        [Late(stack[0]), Late(stack[1]), w_qkv, gain_a, here],
        1e6,
    )

    wide_in = 2 * fsdp * units

    def in_grads(table, sums, block, before):
        some = pl.BlockSpec((block, wide_in), lambda s, t: (t[s], 0))
        any_spec = pl.BlockSpec(memory_space=pl.ANY)
        small_out = pl.BlockSpec((1, 1, block), lambda s, t: (t[s], 0, 0))
        return pl.pallas_call(
            in_grad_kernel,
            grid_spec=pltpu.PrefetchScalarGridSpec(
                num_scalar_prefetch=1,
                grid=(sums.shape[0],),
                in_specs=[
                    pl.BlockSpec((1, block, wide_in), lambda s, t: (s, 0, 0)),
                    some,
                    pl.BlockSpec((block, 1), lambda s, t: (t[s], 0)),
                ]
                + [any_spec] * len(before),
                out_specs=[some, small_out],
            ),
            out_shape=[
                shape_of(w_in.shape, f32),
                shape_of((rows // block, 1, block), f32),
            ],
            input_output_aliases={4 + k: k for k in range(len(before))},
            compiler_params=pltpu.CompilerParams(vmem_limit_bytes=40 << 20),
            cost_estimate=pl.CostEstimate(
                flops=1000000, bytes_accessed=8 * w_in.size, transcendentals=0
            ),
            name="in_grad",
        )(table, sums, w_in, gain_m, *before)

    if small % 8:
        parts = join(in_pair)
        parts = [
            lax.dynamic_slice_in_dim(parts, storage(c ^ cc, order), 1, 0) for cc in range(ctx)
        ]
        parts = jnp.concatenate(parts, axis=1)
        grad_in, grad_gain_m = in_grads(jnp.zeros((1,), jnp.int32), parts, rows, [])
    else:
        place_of = {storage(x, order): x for x in range(ctx)}
        table = jnp.stack([c ^ place_of[at] for at in range(ctx)])
        top = ctx // 2
        before = in_grads(table[:top], in_pair[0], small, [])
        grad_in, grad_gain_m = in_grads(table[top:], in_pair[1], small, list(before))
    (grad_mlp_out,) = call(
        functools.partial(out_grad_kernel, p=p),
        "out_grad",
        [shape_of((units, width), f32)],
        1,
        [],
        [mlp_stack, here],
        1e6,
    )
    return (
        out,
        back,
        grad_qkv,
        grad_out,
        grad_in,
        grad_mlp_out,
        grad_gain_a.reshape(rows),
        grad_gain_m.reshape(rows),
    )


def solution(mesh):
    in_specs = (
        P("fsdp", "ctx", None),
        P("fsdp", "ctx"),
        P("fsdp", "ctx", None),
        P("fsdp", None),
        P("fsdp", None),
        P("fsdp", None),
        P("fsdp", None),
        P("fsdp"),
        P("fsdp"),
    )
    out_specs = (
        P("fsdp", "ctx", None),
        P("fsdp", "ctx", None),
        P("fsdp", None),
        P("fsdp", None),
        P("fsdp", None),
        P("fsdp", None),
        P("fsdp"),
        P("fsdp"),
    )
    return jax.shard_map(
        on_device, mesh=mesh, in_specs=in_specs, out_specs=out_specs, check_vma=False
    )
```
